256 devices in a mesh: segment: 8 (over z), tile: 32 (over x, y, core).
Axes of the slice: x: 4, y: 4, z: 8, core: 2. Of those that a mesh axis runs over, the one named last changes fastest.
Arguments:
- latent: bfloat16 [4, 8, 128, 384], P(None, None, 'tile'), may hold values from -6 to 6
- frame_order: int32 [4], replicated, may hold values from 0 to 3, each once
- section_weight: bfloat16 [8, 27, 384, 384], P('segment'), may hold values from -0.0625 to 0.0625
- section_gain: bfloat16 [8, 384], P('segment'), may hold values from 0.5 to 1.5
- up_weight: bfloat16 [27, 384, 192], P(None, 'tile'), may hold values from -0.0625 to 0.0625
- reward_weight: bfloat16 [49152, 1280], P(None, 'tile'), may hold values from -0.02734375 to 0.02734375
- reward_coef: float32 [1280], P('tile'), may hold values from -6 to 6
Outputs:
- input_grads: float32 [8, 4, 8, 128, 384], P('segment', None, None, 'tile')
The draws below stay inside these ranges and needn't reach their ends.
All inputs are finite; a program needn't handle non-finite values.
Results may differ from the reference program's by a relative error of at most 0.03.
Values may be sent and summed in bfloat16 or wider, within the bound.
No kernel may reach another device: no remote copies, remote signals or barrier semaphores. Data moves between devices by JAX's collectives and lax.ppermute only.
A program may use at most 128 MiB of HBM per device.

```python
import jax
import jax.numpy as jnp
from jax import lax

C = 384
CU = 192
RO = 1280
P_SIZE = 16
F = 4
H = 8
W = 128
N_SEGMENT = 8
N_TILE = 32


def block_scale(key, shape, shards, smallest, high):
    loudness, own = 1.0, jax.random.fold_in(key, 6)
    for axis_at, blocks in shards:
        heights = jnp.exp(jax.random.uniform(jax.random.fold_in(own, axis_at), (blocks,), jnp.float32, smallest / len(shards), high / len(shards)))
        loudness = loudness * jnp.repeat(heights, shape[axis_at] // blocks).reshape([-1 if axis == axis_at else 1 for axis in range(len(shape))])
    return loudness


def bell_draw(rng, extent, spread, limit, cuts=(), dtype=jnp.bfloat16):
    level = block_scale(rng, extent, cuts, -0.22, 0.18) if cuts else 1.0
    entries = jax.random.normal(rng, extent, jnp.float32) * spread * level
    return jnp.minimum(jnp.maximum(entries, -limit), limit).astype(dtype)


def setup_inputs(seed: int = 0) -> dict:
    seeds = jax.random.split(jax.random.key(seed), 8)
    return {
        "latent": bell_draw(seeds[0], (F, H, W, C), 1.0, 6.0, ((2, 32),)),
        "frame_order": jax.random.permutation(seeds[1], F).astype(jnp.int32),
        "section_weight": bell_draw(seeds[2], (N_SEGMENT, 27, C, C), (27 * C) ** -0.5, 0.0625, ((0, 8),)),
        "section_gain": jnp.clip(1.0 + 0.1 * jax.random.normal(seeds[3], (N_SEGMENT, C), jnp.float32), 0.5, 1.5).astype(jnp.bfloat16),
        "up_weight": bell_draw(seeds[4], (27, C, CU), (27 * C) ** -0.5, 0.0625, ((1, 32),)),
        "reward_weight": bell_draw(seeds[5], (P_SIZE * P_SIZE * CU, RO), (P_SIZE * P_SIZE * CU) ** -0.5, 0.02734375, ((1, 32),)),
        "reward_coef": bell_draw(seeds[6], (RO,), 1.0, 6.0, ((0, 32),), jnp.float32),
    }


EPS = 1e-06

def section_act(inputs, gain_row):
    as_float = inputs.astype(jnp.float32)
    inv_norm = lax.rsqrt(lax.optimization_barrier(jnp.mean(as_float * as_float, axis=-1, keepdims=True)) + EPS)
    return jax.nn.silu(as_float * inv_norm * gain_row.astype(jnp.float32))

def causal_taps(stacked, height, width):
    pieces = []
    for time_off in range(3):
        for row_off in range(3):
            for col_off in range(3):
                pieces.append(stacked[time_off, row_off:row_off + height, col_off:col_off + width])
    return jnp.stack(pieces, axis=2).reshape(height * width, -1)

def reverse_taps(stacked, height, width):
    pieces = []
    for time_off in range(3):
        for row_off in range(3):
            for col_off in range(3):
                pieces.append(stacked[time_off, 2 - row_off:2 - row_off + height, 2 - col_off:2 - col_off + width])
    return jnp.stack(pieces, axis=2).reshape(height * width, -1)

def plane_taps(plane, height, width):
    pieces = []
    for row_off in range(3):
        for col_off in range(3):
            pieces.append(plane[2 - row_off:2 - row_off + height, 2 - col_off:2 - col_off + width])
    return jnp.stack(pieces, axis=2).reshape(height * width, -1)

def reference(latent, frame_order, section_weight, section_gain, up_weight, reward_weight, reward_coef):
    sections = section_weight.shape[0]
    current = latent[frame_order]
    zero_pair = jnp.zeros((2, H, W, C), jnp.bfloat16)
    kept_inputs = []
    for section in range(sections):
        kept_inputs.append(current)
        activated = section_act(current, section_gain[section]).astype(jnp.bfloat16)
        padded = jnp.pad(jnp.concatenate([zero_pair, activated], 0), ((0, 0), (1, 1), (1, 1), (0, 0)))
        weight_flat = section_weight[section].reshape(27 * C, C)
        produced = []
        for frame_at in range(F):
            conv_out = jnp.dot(causal_taps(padded[frame_at:frame_at + 3], H, W), weight_flat, preferred_element_type=jnp.float32)
            produced.append((current[frame_at].astype(jnp.float32) + conv_out.reshape(H, W, C)).astype(jnp.bfloat16))
        current = jnp.stack(produced)
    upsampled = jnp.repeat(jnp.repeat(current, 2, axis=1), 2, axis=2)
    up_padded = jnp.pad(jnp.concatenate([jnp.zeros((2, 2 * H, 2 * W, C), jnp.bfloat16), upsampled], 0), ((0, 0), (1, 1), (1, 1), (0, 0)))
    up_flat = up_weight.reshape(27 * C, CU)
    back_up = up_weight.reshape(3, 9, C, CU).transpose(1, 3, 0, 2).reshape(9 * CU, 3 * C)
    group_width = RO // N_TILE
    grouped_weight = reward_weight.astype(jnp.float32).reshape(P_SIZE * P_SIZE * CU, N_TILE, group_width)
    deep_grad = jnp.zeros((F + 2, H, W, C), jnp.float32)
    for frame_at in range(F):
        preact = jnp.dot(causal_taps(up_padded[frame_at:frame_at + 3], 2 * H, 2 * W), up_flat, preferred_element_type=jnp.float32).reshape(2 * H, 2 * W, CU)
        features = jax.nn.silu(preact).astype(jnp.bfloat16)
        patches = features.reshape(2 * H // P_SIZE, P_SIZE, 2 * W // P_SIZE, P_SIZE, CU).transpose(0, 2, 1, 3, 4).reshape(-1, P_SIZE * P_SIZE * CU)
        logits = jnp.dot(patches, reward_weight, preferred_element_type=jnp.float32)
        squashed = jnp.tanh(logits)
        logit_grad = (reward_coef * (1.0 - squashed * squashed)).astype(jnp.bfloat16)
        grouped_grad = logit_grad.astype(jnp.float32).reshape(-1, N_TILE, group_width)
        tile_terms = jnp.einsum('ntr,ktr->tnk', grouped_grad, grouped_weight)
        rounded_terms = lax.optimization_barrier(tile_terms.astype(jnp.bfloat16))
        patch_grad = lax.optimization_barrier(jnp.sum(rounded_terms.astype(jnp.float32), axis=0))
        feat_grad = patch_grad.reshape(2 * H // P_SIZE, 2 * W // P_SIZE, P_SIZE, P_SIZE, CU).transpose(0, 2, 1, 3, 4).reshape(2 * H, 2 * W, CU)
        sigmoid_p = jax.nn.sigmoid(preact)
        preact_grad = (feat_grad * sigmoid_p * (1.0 + preact * (1.0 - sigmoid_p))).astype(jnp.bfloat16)
        grad_pad = jnp.pad(preact_grad, ((1, 1), (1, 1), (0, 0)))
        contribution = jnp.dot(plane_taps(grad_pad, 2 * H, 2 * W), back_up, preferred_element_type=jnp.float32)
        contribution = contribution.reshape(H, 2, W, 2, 3, C).sum(axis=(1, 3))
        for time_off in range(3):
            deep_grad = deep_grad.at[frame_at + time_off].add(contribution[:, :, time_off])
    grad_now = deep_grad[2:]
    results = [None] * sections
    for section in reversed(range(sections)):
        weight_back = section_weight[section].transpose(0, 2, 1).reshape(27 * C, C)
        grad_pad = jnp.pad(jnp.concatenate([grad_now.astype(jnp.bfloat16), zero_pair], 0), ((0, 0), (1, 1), (1, 1), (0, 0)))
        produced = []
        for frame_at in range(F):
            window = grad_pad[frame_at:frame_at + 3][::-1]
            conv_back = jnp.dot(reverse_taps(window, H, W), weight_back, preferred_element_type=jnp.float32).reshape(H, W, C)
            gain_row = section_gain[section]
            _, pullback = jax.vjp(lambda values: section_act(values, gain_row), kept_inputs[section][frame_at].astype(jnp.float32))
            produced.append(grad_now[frame_at] + pullback(conv_back)[0])
        grad_now = jnp.stack(produced)
        results[section] = grad_now
    return jnp.stack(results)
```

```python
import functools

import jax
import jax.numpy as jnp
from jax import lax
from jax.experimental import pallas as pl
from jax.experimental.pallas import tpu as pltpu
from jax.sharding import PartitionSpec as P

EPS = 1e-06
F32 = jnp.float32
BF16 = jnp.bfloat16
AXES = ("segment", "chip", "core")
TILE = ("chip", "core")
PAD = 16
VM = pl.BlockSpec(memory_space=pltpu.VMEM)
HB = pl.BlockSpec(memory_space=pl.ANY)
SM = pl.BlockSpec(memory_space=pltpu.SMEM)


def row_shifts(v):
    count = v.shape[0]
    row = lax.broadcasted_iota(jnp.int32, v.shape, 0) & 7
    before = jnp.where(row == 0, 0.0, pltpu.roll(v, 1, 0))
    after = jnp.where(row == 7, 0.0, pltpu.roll(v, count - 1, 0))
    return before, after


def start_weights(w_hbm, w_buf, sem):
    rows = w_hbm.shape[0] // 3
    copies = []
    for a in range(3):
        part = pl.ds(a * rows, rows)
        copies.append(pltpu.make_async_copy(w_hbm.at[part], w_buf.at[part], sem.at[a]))
    return copies


def fwd_kernel(edge, tile_ref, xc, xl, xr, gain_ref, w_hbm, *rest):
    wide = edge == 2
    if wide:
        y_ref, taps, w_buf, sem = rest
    else:
        y_ref, yl_ref, yr_ref, taps, w_buf, sem = rest
    copies = start_weights(w_hbm, w_buf, sem)
    for copy in copies:
        copy.start()
    frames, cols, rows, ch = xc.shape
    outer = cols + 2 * edge
    inner = outer - 2
    block = inner * rows
    gain = gain_ref[...].astype(F32)
    taps[0 : 2 * block, :] = jnp.zeros((2 * block, 9 * ch), BF16)
    kept = []
    for t in range(frames):
        x = jnp.concatenate([xl[t], xc[t], xr[t]], axis=0).astype(F32).reshape(outer * rows, ch)
        inv = lax.rsqrt(jnp.mean(x * x, axis=-1, keepdims=True) + EPS)
        act = jax.nn.silu(x * inv * gain)
        before, after = row_shifts(act)
        for b, v in enumerate((before, act, after)):
            for c in range(3):
                at = (3 * b + c) * ch
                taps[(2 + t) * block : (3 + t) * block, at : at + ch] = v[
                    c * rows : c * rows + block
                ].astype(BF16)
    acc = jnp.zeros((frames * block, ch), F32)
    for a in range(3):
        copies[a].wait()
        k = 9 * ch
        acc = acc + jnp.dot(
            taps[a * block : (a + frames) * block, :],
            w_buf[a * k : (a + 1) * k, :],
            preferred_element_type=F32,
        )
    for t in range(frames):
        if wide:
            x = jnp.concatenate([xl[t, 1:], xc[t], xr[t, :1]], axis=0)
        else:
            x = xc[t]
        out = x.astype(F32) + acc[t * block : (t + 1) * block].reshape(inner, rows, ch)
        if wide:
            tile = tile_ref[0]
            col = lax.broadcasted_iota(jnp.int32, out.shape, 0)
            low = jnp.where(tile == 0, 1, 0)
            high = jnp.where(tile == tile_ref[1] - 1, inner - 1, inner)
            out = jnp.where((col >= low) & (col < high), out, 0.0)
            y_ref[t] = out.astype(BF16)
        else:
            out = out.astype(BF16)
            y_ref[t] = out
            e = yl_ref.shape[1]
            yl_ref[t] = out[:e]
            yr_ref[t] = out[cols - e :]


def run_fwd(edge, out_edge, tile_info, xc, xl, xr, gain, weight):
    frames, cols, rows, ch = xc.shape
    block = (cols + 2 * edge - 2) * rows
    if edge == 2:
        outs = [jax.ShapeDtypeStruct((frames, cols + 2, rows, ch), BF16)]
    else:
        outs = [jax.ShapeDtypeStruct((frames, n, rows, ch), BF16) for n in (cols, out_edge, out_edge)]
    return pl.pallas_call(
        functools.partial(fwd_kernel, edge),
        out_shape=outs,
        in_specs=[SM, VM, VM, VM, VM, HB],
        out_specs=[VM] * len(outs),
        scratch_shapes=[
            pltpu.VMEM((6 * block, 9 * ch), BF16),
            pltpu.VMEM(weight.shape, BF16),
            pltpu.SemaphoreType.DMA((3,)),
        ],
        name=f"fwd{edge}{out_edge}",
    )(tile_info, xc, xl, xr, gain, weight)


def bwd_kernel(gc, gl, gr, x_ref, gain_ref, w_hbm, *rest):
    if len(rest) == 7:
        gf_ref, gb_ref, ol_ref, or_ref, taps, w_buf, sem = rest
    else:
        gf_ref, taps, w_buf, sem = rest
        gb_ref = None
    copies = start_weights(w_hbm, w_buf, sem)
    for copy in reversed(copies):
        copy.start()
    frames, cols, rows, ch = gc.shape
    block = cols * rows
    outer = cols + 2
    gain = gain_ref[...].astype(F32)
    taps[4 * block : 6 * block, :] = jnp.zeros((2 * block, 9 * ch), BF16)
    for t in range(frames):
        g = jnp.concatenate(
            [gl[t].astype(F32), gc[t].astype(F32), gr[t].astype(F32)], axis=0
        ).reshape(outer * rows, ch)
        before, after = row_shifts(g)
        for b, v in enumerate((after, g, before)):
            for c in range(3):
                at = (3 * b + c) * ch
                taps[t * block : (t + 1) * block, at : at + ch] = v[
                    (2 - c) * rows : (2 - c) * rows + block
                ].astype(BF16)
    acc = jnp.zeros((frames * block, ch), F32)
    for a in reversed(range(3)):
        copies[a].wait()
        k = 9 * ch
        acc = acc + jnp.dot(
            taps[(2 - a) * block : (2 - a + frames) * block, :],
            w_buf[a * k : (a + 1) * k, :],
            preferred_element_type=F32,
        )
    for t in range(frames):
        x = x_ref[t].astype(F32).reshape(block, ch)
        inv = lax.rsqrt(jnp.mean(x * x, axis=-1, keepdims=True) + EPS)
        u = x * inv * gain
        sig = jax.nn.sigmoid(u)
        y = acc[t * block : (t + 1) * block] * (sig * (1.0 + u * (1.0 - sig))) * gain
        mean = jnp.mean(y * x, axis=-1, keepdims=True)
        dx = inv * (y - x * (inv * inv * mean))
        out = gc[t].astype(F32) + dx.reshape(cols, rows, ch)
        gf_ref[t] = out
        if gb_ref is not None:
            out = out.astype(BF16)
            gb_ref[t] = out
            ol_ref[t] = out[:1]
            or_ref[t] = out[cols - 1 :]


def run_bwd(last, gc, gl, gr, x, gain, weight_back):
    frames, cols, rows, ch = gc.shape
    outs = [jax.ShapeDtypeStruct((frames, cols, rows, ch), F32)]
    if not last:
        outs += [jax.ShapeDtypeStruct((frames, n, rows, ch), BF16) for n in (cols, 1, 1)]
    return pl.pallas_call(
        bwd_kernel,
        out_shape=outs,
        in_specs=[VM, VM, VM, VM, VM, HB],
        out_specs=[VM] * len(outs),
        scratch_shapes=[
            pltpu.VMEM((6 * cols * rows, 9 * ch), BF16),
            pltpu.VMEM(weight_back.shape, BF16),
            pltpu.SemaphoreType.DMA((3,)),
        ],
        name="bwd",
    )(gc, gl, gr, x, gain, weight_back)


def up_kernel(x_ref, wa_ref, wb_ref, spread_ref, pre_ref, feat_ref, held):
    frames, outer, rows, ch = x_ref.shape
    cols = outer - 2
    cu = wa_ref.shape[3]
    half = wa_ref.shape[0] * wa_ref.shape[2]
    block = outer * rows
    held[0 : 2 * block, :] = jnp.zeros((2 * block, 2 * half), BF16)
    for t in range(frames):
        held[(2 + t) * block : (3 + t) * block, :] = jnp.dot(
            x_ref[t].reshape(block, ch), spread_ref[...], preferred_element_type=F32
        ).astype(BF16)
    by_phase = [[], []]
    for c in range(3):
        cells = []
        for b in range(3):
            total = jnp.zeros((frames * block, cu), F32)
            for a in range(3):
                for part, w_ref in enumerate((wa_ref, wb_ref)):
                    total = total + jnp.dot(
                        held[a * block : (a + frames) * block, part * half : (part + 1) * half],
                        w_ref[:, 9 * a + 3 * b + c].reshape(half, cu),
                        preferred_element_type=F32,
                    )
            cells.append(total)
        before, _ = row_shifts(cells[0])
        _, after = row_shifts(cells[2])
        shape = (frames, outer, rows, cu)
        by_phase[0].append((before + cells[1] + cells[2]).reshape(shape))
        by_phase[1].append((cells[0] + cells[1] + after).reshape(shape))
    for p in range(2):
        left, mid, right = by_phase[p]
        for q in range(2):
            if q == 0:
                pre = left[:, 0:cols] + mid[:, 1 : cols + 1] + right[:, 1 : cols + 1]
            else:
                pre = left[:, 1 : cols + 1] + mid[:, 1 : cols + 1] + right[:, 2 : cols + 2]
            pre_ref[p, q] = pre
            feat_ref[p, q] = jax.nn.silu(pre).astype(BF16)


def run_up(x, wa, wb, spread):
    frames, outer, rows, ch = x.shape
    shape = (2, 2, frames, outer - 2, rows, wa.shape[3])
    return pl.pallas_call(
        up_kernel,
        out_shape=[jax.ShapeDtypeStruct(shape, F32), jax.ShapeDtypeStruct(shape, BF16)],
        in_specs=[VM] * 4,
        out_specs=[VM, VM],
        scratch_shapes=[pltpu.VMEM((6 * outer * rows, spread.shape[1]), BF16)],
        name="up",
    )(x, wa, wb, spread)


def adj_kernel(pg_ref, el_ref, er_ref, wa_ref, wb_ref, spread_ref, gf_ref, gl_ref, gr_ref, held):
    _, _, frames, cols, rows, cu = pg_ref.shape
    block = cols * rows
    ch = spread_ref.shape[0]
    half = wa_ref.shape[0] * wa_ref.shape[2]
    held[:, frames * block :, :] = jnp.zeros((9, 2 * block, cu), BF16)
    for t in range(frames):
        fine = []
        for p in range(2):
            odd = jnp.concatenate([el_ref[p, t][None], pg_ref[p, 1, t]], axis=0).astype(F32)
            even = jnp.concatenate([pg_ref[p, 0, t], er_ref[p, t][None]], axis=0).astype(F32)
            own = even[:cols] + odd[1:]
            later = odd[1:] + even[1:]
            sooner = odd[:cols] + even[:cols]
            fine.append([v.reshape(block, cu) for v in (later, own, sooner)])
        for c in range(3):
            top, low = fine[0][c], fine[1][c]
            _, top_after = row_shifts(top)
            low_before, _ = row_shifts(low)
            for b, v in enumerate((low + top_after, top + low, low_before + top)):
                held[3 * b + c, t * block : (t + 1) * block, :] = v.astype(BF16)
    out = jnp.zeros((frames * block, ch), F32)
    for part, w_ref in enumerate((wa_ref, wb_ref)):
        acc = jnp.zeros((frames * block, half), F32)
        for a in range(3):
            for bc in range(9):
                acc = acc + lax.dot_general(
                    held[bc, (2 - a) * block : (2 - a + frames) * block, :],
                    w_ref[:, 9 * a + bc].reshape(half, cu),
                    (((1,), (1,)), ((), ())),
                    preferred_element_type=F32,
                )
        for _ in range(3):
            piece = acc.astype(BF16)
            acc = acc - piece.astype(F32)
            out = out + lax.dot_general(
                piece,
                spread_ref[:, part * half : (part + 1) * half],
                (((1,), (1,)), ((), ())),
                preferred_element_type=F32,
            )
    out = out.reshape(frames, cols, rows, ch)
    gf_ref[...] = out
    gl_ref[...] = out[:, :1].astype(BF16)
    gr_ref[...] = out[:, cols - 1 :].astype(BF16)


def run_adj(pg, left, right, wa, wb, spread):
    _, _, frames, cols, rows, cu = pg.shape
    ch = spread.shape[0]
    return pl.pallas_call(
        adj_kernel,
        out_shape=[
            jax.ShapeDtypeStruct((frames, cols, rows, ch), F32),
            jax.ShapeDtypeStruct((frames, 1, rows, ch), BF16),
            jax.ShapeDtypeStruct((frames, 1, rows, ch), BF16),
        ],
        in_specs=[VM] * 6,
        out_specs=[VM] * 3,
        scratch_shapes=[pltpu.VMEM((9, 6 * cols * rows, cu), BF16)],
        name="adj",
    )(pg, left, right, wa, wb, spread)


def on_device(latent, frame_order, section_weight, section_gain, up_weight, reward_weight, reward_coef):
    segs = lax.axis_size("segment")
    chips = lax.axis_size("chip")
    tiles = 2 * chips
    seg = lax.axis_index("segment")
    core = lax.axis_index("core")
    tile = 2 * lax.axis_index("chip") + core
    frames, rows, cols, ch = latent.shape
    cu = up_weight.shape[2]
    outs_dev = reward_coef.shape[0]
    last = segs - 1
    barrier = lax.optimization_barrier
    tile_info = jnp.stack([tile, jnp.full_like(tile, tiles)])

    def route(pairs_of_segments, shift):
        return [
            (source * tiles + t, target * tiles + t + shift)
            for source, target in pairs_of_segments
            for t in range(tiles)
            if 0 <= t + shift < tiles
        ]

    def send(value, source, target, shift):
        return lax.ppermute(value, AXES, route([(source, target)], shift))

    def beside(value, shift):
        return lax.ppermute(value, AXES, route([(s, s) for s in range(segs)], shift))

    def hop(center, left, right, source, target):
        step = target - source
        pairs = [(s, s + step) for s in range(source % 2, segs, 2) if 0 <= s + step < segs]
        return tuple(
            lax.ppermute(value, AXES, route(pairs, shift))
            for value, shift in ((center, 0), (right, 1), (left, -1))
        )

    weight_fwd = section_weight[0].reshape(27 * ch, ch)

    halves = segs // frames
    half = seg % halves
    rows_half = 2 * rows // halves
    span = 2 * cols * cu
    keep = rows_half * 2 * span
    patches = tiles // 2
    own = up_weight.shape[1]
    channel = lax.broadcasted_iota(jnp.int32, (ch, tiles * PAD), 0)
    place = lax.broadcasted_iota(jnp.int32, (ch, tiles * PAD), 1)
    other, chip_of, within = place // (chips * PAD), place // PAD % chips, place % PAD
    source = 2 * chip_of + jnp.where(other == 0, core, 1 - core)
    spread = ((within < own) & (channel == source * own + within)).astype(BF16)

    first = jnp.stack([lax.dynamic_index_in_dim(latent, frame_order[t], 0, False) for t in range(frames)])
    first = jnp.where(seg == 0, first.transpose(0, 2, 1, 3), jnp.zeros((), BF16))
    xc = first
    xr, xl = beside(first[:, :1], -1), beside(first[:, cols - 1 :], 1)
    kept = []
    for k in range(segs):
        kept.append(xc)
        edge = 2 if k == last else 1
        out_edge = 2 if k == last - 1 else 1

        def live(xc=xc, xl=xl, xr=xr, edge=edge, out_edge=out_edge):
            return tuple(run_fwd(edge, out_edge, tile_info, xc, xl, xr, section_gain, weight_fwd))

        shapes = [(frames, cols + 2, rows, ch)] if k == last else [
            (frames, n, rows, ch) for n in (cols, out_edge, out_edge)
        ]
        made = lax.cond(seg == k, live, lambda: tuple(jnp.zeros(s, BF16) for s in shapes))
        if k == last:
            (deep,) = made
        else:
            y, yl, yr = made
            xc, xl, xr = hop(y, yl, yr, k, k + 1)
        if k == 0:
            up_src, xc = barrier((up_weight, xc))
            up_src = jnp.pad(up_src, ((0, 0), (0, PAD - up_src.shape[1]), (0, 0)))
            up_a = lax.all_to_all(
                jnp.broadcast_to(up_src[None], (chips, *up_src.shape)), "chip", 0, 0, tiled=True
            )
        if k == 2:
            w_src, r_src, xc = barrier((section_weight, reward_weight, xc))
            weight_back = w_src[0].transpose(0, 2, 1).reshape(27 * ch, ch)
            w_half = lax.dynamic_slice_in_dim(r_src, half * keep, keep, 0).T
            w_half = w_half.reshape(outs_dev, rows_half * 2, span).transpose(1, 0, 2)
            w_half = w_half.reshape(rows_half * 2 * outs_dev, span)
        if k == 4:
            weight_back, w_half, xc = barrier((weight_back, w_half, xc))
        if k == last - 1:
            up_b = lax.ppermute(up_a, "core", [(0, 1), (1, 0)])
            up_a, up_b, xc = barrier((up_a, up_b, xc))
    x_kept = functools.reduce(jnp.add, kept)

    pre, feat = lax.cond(
        seg == last,
        lambda: tuple(run_up(deep, up_a, up_b, spread)),
        lambda: (
            jnp.zeros((2, 2, frames, cols, rows, cu), F32),
            jnp.zeros((2, 2, frames, cols, rows, cu), BF16),
        ),
    )
    feat = feat.transpose(2, 4, 0, 3, 1, 5).reshape(segs, rows_half, span)
    mine = jnp.where(seg == last, feat[last], jnp.zeros((), BF16))
    for k in range(last):
        mine = mine + send(feat[k], last, k, 0)
    everyone = lax.all_to_all(
        jnp.broadcast_to(mine[None], (tiles, rows_half, span)), TILE, 0, 0, tiled=True
    )
    everyone = everyone.reshape(tiles * rows_half, span)
    pairs = lax.dot_general(everyone, w_half, (((1,), (1,)), ((), ())), preferred_element_type=F32)
    row_group = lax.broadcasted_iota(jnp.int32, pairs.shape, 0) % (2 * rows_half)
    row_group = (row_group % rows_half) * 2 + row_group // rows_half
    col_group = lax.broadcasted_iota(jnp.int32, pairs.shape, 1) // outs_dev
    fits = row_group == col_group
    partial = jnp.where(fits, pairs, 0.0).reshape(patches, 2 * rows_half, -1).sum(1)
    partial = partial.reshape(patches, 2 * rows_half, outs_dev).sum(1)
    group = [(s, s // halves * halves + (s + 1) % halves) for s in range(segs)]
    logits = partial + lax.ppermute(partial, "segment", group)
    squashed = jnp.tanh(logits)
    logit_grad = (reward_coef * (1.0 - squashed * squashed)).astype(BF16)
    wide_grad = jnp.where(
        fits.reshape(patches, 2 * rows_half, -1),
        jnp.tile(logit_grad, (1, 2 * rows_half))[:, None, :],
        jnp.zeros((), BF16),
    ).reshape(tiles * rows_half, -1)
    back = jnp.dot(wide_grad, w_half, preferred_element_type=F32).astype(BF16)
    shares = lax.all_to_all(back.reshape(tiles, rows_half, span), TILE, 0, 0, tiled=True)
    share = shares.astype(F32).sum(0).astype(BF16)
    parts = [send(share, k, last, 0) for k in range(last)] + [share]
    feat_grad = jnp.stack(parts).reshape(frames, rows, 2, cols, 2, cu).transpose(2, 4, 0, 3, 1, 5)
    sig = jax.nn.sigmoid(pre)
    pg = (feat_grad.astype(F32) * sig * (1.0 + pre * (1.0 - sig))).astype(BF16)
    edge_l = beside(pg[:, 1, :, cols - 1], 1)
    edge_r = beside(pg[:, 0, :, 0], -1)
    gc, gl, gr = lax.cond(
        seg == last,
        lambda: tuple(run_adj(pg, edge_l, edge_r, up_a, up_b, spread)),
        lambda: (
            jnp.zeros((frames, cols, rows, ch), F32),
            jnp.zeros((frames, 1, rows, ch), BF16),
            jnp.zeros((frames, 1, rows, ch), BF16),
        ),
    )
    gl, gr = beside(gr, 1), beside(gl, -1)

    result = []
    for k in reversed(range(segs)):

        def live_back(gc=gc, gl=gl, gr=gr, k=k):
            return tuple(run_bwd(k == 0, gc, gl, gr, x_kept, section_gain, weight_back))

        widths = () if k == 0 else (cols, 1, 1)
        made = lax.cond(
            seg == k,
            live_back,
            lambda widths=widths: (
                jnp.zeros((frames, cols, rows, ch), F32),
                *(jnp.zeros((frames, n, rows, ch), BF16) for n in widths),
            ),
        )
        result.append(made[0])
        if k:
            gc, gl, gr = hop(made[1], made[2], made[3], k, k - 1)
    total = functools.reduce(jnp.add, result)
    return total.transpose(0, 2, 1, 3)[None]


def solution(mesh):
    shape = mesh.devices.shape
    fine = jax.sharding.Mesh(mesh.devices.reshape(shape[0], shape[1] // 2, 2), AXES)
    in_specs = (
        P(None, None, TILE, None),
        P(),
        P("segment", None, None, None),
        P("segment", None),
        P(None, TILE, None),
        P(None, TILE),
        P(TILE),
    )
    out_specs = P("segment", None, None, TILE, None)
    return jax.shard_map(
        on_device, mesh=fine, in_specs=in_specs, out_specs=out_specs, check_vma=False
    )
```

```python
import functools

import jax
import jax.numpy as jnp
from jax import lax
from jax.experimental import pallas as pl
from jax.experimental.pallas import tpu as pltpu
from jax.sharding import PartitionSpec as P

EPS = 1e-06
F32 = jnp.float32
BF16 = jnp.bfloat16
AXES = ("segment", "chip", "core")
TILE = ("chip", "core")
PAD = 16
VM = pl.BlockSpec(memory_space=pltpu.VMEM)
HB = pl.BlockSpec(memory_space=pl.ANY)
SM = pl.BlockSpec(memory_space=pltpu.SMEM)


def row_shifts(v):
    count = v.shape[0]
    row = lax.broadcasted_iota(jnp.int32, v.shape, 0) & 7
    before = jnp.where(row == 0, 0.0, pltpu.roll(v, 1, 0))
    after = jnp.where(row == 7, 0.0, pltpu.roll(v, count - 1, 0))
    return before, after


def start_weights(w_hbm, w_buf, sem):
    rows = w_hbm.shape[0] // 3
    copies = []
    for a in range(3):
        part = pl.ds(a * rows, rows)
        copies.append(pltpu.make_async_copy(w_hbm.at[part], w_buf.at[part], sem.at[a]))
    return copies


def fwd_kernel(edge, tile_ref, xc, xl, xr, gain_ref, w_hbm, *rest):
    wide = edge == 2
    if wide:
        y_ref, taps, w_buf, sem = rest
    else:
        y_ref, yl_ref, yr_ref, taps, w_buf, sem = rest
    copies = start_weights(w_hbm, w_buf, sem)
    for copy in copies:
        copy.start()
    frames, cols, rows, ch = xc.shape
    outer = cols + 2 * edge
    inner = outer - 2
    block = inner * rows
    gain = gain_ref[...].astype(F32)
    taps[0 : 2 * block, :] = jnp.zeros((2 * block, 9 * ch), BF16)
    kept = []
    for t in range(frames):
        x = jnp.concatenate([xl[t], xc[t], xr[t]], axis=0).astype(F32).reshape(outer * rows, ch)
        inv = lax.rsqrt(jnp.mean(x * x, axis=-1, keepdims=True) + EPS)
        act = jax.nn.silu(x * inv * gain)
        before, after = row_shifts(act)
        for b, v in enumerate((before, act, after)):
            for c in range(3):
                at = (3 * b + c) * ch
                taps[(2 + t) * block : (3 + t) * block, at : at + ch] = v[
                    c * rows : c * rows + block
                ].astype(BF16)
    acc = jnp.zeros((frames * block, ch), F32)
    for a in range(3):
        copies[a].wait()
        k = 9 * ch
        acc = acc + jnp.dot(
            taps[a * block : (a + frames) * block, :],
            w_buf[a * k : (a + 1) * k, :],
            preferred_element_type=F32,
        )
    for t in range(frames):
        if wide:
            x = jnp.concatenate([xl[t, 1:], xc[t], xr[t, :1]], axis=0)
        else:
            x = xc[t]
        out = x.astype(F32) + acc[t * block : (t + 1) * block].reshape(inner, rows, ch)
        if wide:
            tile = tile_ref[0]
            col = lax.broadcasted_iota(jnp.int32, out.shape, 0)
            low = jnp.where(tile == 0, 1, 0)
            high = jnp.where(tile == tile_ref[1] - 1, inner - 1, inner)
            out = jnp.where((col >= low) & (col < high), out, 0.0)
            y_ref[t] = out.astype(BF16)
        else:
            out = out.astype(BF16)
            y_ref[t] = out
            e = yl_ref.shape[1]
            yl_ref[t] = out[:e]
            yr_ref[t] = out[cols - e :]


def run_fwd(edge, out_edge, tile_info, xc, xl, xr, gain, weight):
    frames, cols, rows, ch = xc.shape
    block = (cols + 2 * edge - 2) * rows
    if edge == 2:
        outs = [jax.ShapeDtypeStruct((frames, cols + 2, rows, ch), BF16)]
    else:
        outs = [jax.ShapeDtypeStruct((frames, n, rows, ch), BF16) for n in (cols, out_edge, out_edge)]
    return pl.pallas_call(
        functools.partial(fwd_kernel, edge),
        out_shape=outs,
        in_specs=[SM, VM, VM, VM, VM, HB],
        out_specs=[VM] * len(outs),
        scratch_shapes=[
            pltpu.VMEM((6 * block, 9 * ch), BF16),
            pltpu.VMEM(weight.shape, BF16),
            pltpu.SemaphoreType.DMA((3,)),
        ],
        name=f"fwd{edge}{out_edge}",
    )(tile_info, xc, xl, xr, gain, weight)


def bwd_kernel(first, *refs):
    if first:
        tile_ref, gc, lp, rp, from_l, from_r, x_ref, gain_ref, w_hbm, *rest = refs
    else:
        gc, gl, gr, x_ref, gain_ref, w_hbm, *rest = refs
    *outs, taps, w_buf, sem = rest
    copies = start_weights(w_hbm, w_buf, sem)
    for copy in reversed(copies):
        copy.start()
    frames, cols, rows, ch = gc.shape
    block = cols * rows
    outer = cols + 2
    gain = gain_ref[...].astype(F32)
    taps[4 * block : 6 * block, :] = jnp.zeros((2 * block, 9 * ch), BF16)

    def center(t):
        mid = gc[t].astype(F32)
        if not first:
            return mid
        return jnp.concatenate(
            [mid[:1] + from_l[t, 1:].astype(F32), mid[1:-1], mid[-1:] + from_r[t, :1].astype(F32)], axis=0
        )

    for t in range(frames):
        if first:
            left = from_l[t, :1].astype(F32) + lp[t, :1].astype(F32)
            right = from_r[t, 1:].astype(F32) + rp[t, 1:].astype(F32)
            left = jnp.where(tile_ref[0] == 0, 0.0, left)
            right = jnp.where(tile_ref[0] == tile_ref[1] - 1, 0.0, right)
        else:
            left, right = gl[t].astype(F32), gr[t].astype(F32)
        g = jnp.concatenate([left, center(t), right], axis=0).reshape(outer * rows, ch)
        before, after = row_shifts(g)
        for b, v in enumerate((after, g, before)):
            for c in range(3):
                at = (3 * b + c) * ch
                taps[t * block : (t + 1) * block, at : at + ch] = v[
                    (2 - c) * rows : (2 - c) * rows + block
                ].astype(BF16)
    acc = jnp.zeros((frames * block, ch), F32)
    for a in reversed(range(3)):
        copies[a].wait()
        k = 9 * ch
        acc = acc + jnp.dot(
            taps[(2 - a) * block : (2 - a + frames) * block, :],
            w_buf[a * k : (a + 1) * k, :],
            preferred_element_type=F32,
        )
    for t in range(frames):
        x = x_ref[t].astype(F32).reshape(block, ch)
        inv = lax.rsqrt(jnp.mean(x * x, axis=-1, keepdims=True) + EPS)
        u = x * inv * gain
        sig = jax.nn.sigmoid(u)
        y = acc[t * block : (t + 1) * block] * (sig * (1.0 + u * (1.0 - sig))) * gain
        mean = jnp.mean(y * x, axis=-1, keepdims=True)
        dx = inv * (y - x * (inv * inv * mean))
        out = center(t) + dx.reshape(cols, rows, ch)
        outs[0][t] = out
        if len(outs) == 4:
            out = out.astype(BF16)
            outs[1][t] = out
            outs[2][t] = out[:1]
            outs[3][t] = out[cols - 1 :]


def run_bwd(first, last, args, x, gain, weight_back):
    frames, cols, rows, ch = x.shape
    outs = [jax.ShapeDtypeStruct((frames, cols, rows, ch), F32)]
    if not last:
        outs += [jax.ShapeDtypeStruct((frames, n, rows, ch), BF16) for n in (cols, 1, 1)]
    specs = [SM] + [VM] * (len(args) - 1) if first else [VM] * len(args)
    return pl.pallas_call(
        functools.partial(bwd_kernel, first),
        out_shape=outs,
        in_specs=[*specs, VM, VM, HB],
        out_specs=[VM] * len(outs),
        scratch_shapes=[
            pltpu.VMEM((6 * cols * rows, 9 * ch), BF16),
            pltpu.VMEM(weight_back.shape, BF16),
            pltpu.SemaphoreType.DMA((3,)),
        ],
        name="bwd",
    )(*args, x, gain, weight_back)


def first_kernel(order_ref, latent_ref, x_ref, l_ref, r_ref):
    for t in range(x_ref.shape[0]):
        x = latent_ref[order_ref[t]]
        x_ref[t] = x
        l_ref[t] = x[:1]
        r_ref[t] = x[x.shape[0] - 1 :]


def run_first(order, latent):
    frames, cols, rows, ch = latent.shape
    return pl.pallas_call(
        first_kernel,
        out_shape=[jax.ShapeDtypeStruct((frames, n, rows, ch), BF16) for n in (cols, 1, 1)],
        in_specs=[SM, VM],
        out_specs=[VM] * 3,
        name="first",
    )(order, latent)


def unwritten(*shapes):
    return tuple(
        pl.pallas_call(
            lambda out_ref: None,
            out_shape=jax.ShapeDtypeStruct(shape, BF16),
            out_specs=HB,
            name="unwritten",
        )()
        for shape in shapes
    )


def up_kernel(x_ref, wa_ref, wb_ref, spread_ref, *rest):
    pre_ref, *feat_refs, held = rest
    frames, outer, rows, ch = x_ref.shape
    cols = outer - 2
    cu = wa_ref.shape[3]
    half = wa_ref.shape[0] * wa_ref.shape[2]
    block = outer * rows
    held[0 : 2 * block, :] = jnp.zeros((2 * block, 2 * half), BF16)
    for t in range(frames):
        held[(2 + t) * block : (3 + t) * block, :] = jnp.dot(
            x_ref[t].reshape(block, ch), spread_ref[...], preferred_element_type=F32
        ).astype(BF16)
    by_phase = [[], []]
    for c in range(3):
        cells = []
        for b in range(3):
            total = jnp.zeros((frames * block, cu), F32)
            for a in range(3):
                for part, w_ref in enumerate((wa_ref, wb_ref)):
                    total = total + jnp.dot(
                        held[a * block : (a + frames) * block, part * half : (part + 1) * half],
                        w_ref[:, 9 * a + 3 * b + c].reshape(half, cu),
                        preferred_element_type=F32,
                    )
            cells.append(total)
        before, _ = row_shifts(cells[0])
        _, after = row_shifts(cells[2])
        shape = (frames, outer, rows, cu)
        by_phase[0].append((before + cells[1] + cells[2]).reshape(shape))
        by_phase[1].append((cells[0] + cells[1] + after).reshape(shape))
    pres = []
    for p in range(2):
        left, mid, right = by_phase[p]
        pres.append(
            [
                left[:, 0:cols] + mid[:, 1 : cols + 1] + right[:, 1 : cols + 1],
                left[:, 1 : cols + 1] + mid[:, 1 : cols + 1] + right[:, 2 : cols + 2],
            ]
        )
    for t in range(frames):
        for w in range(cols):
            pair = [jnp.concatenate([pres[p][0][t, w], pres[p][1][t, w]], axis=1) for p in range(2)]
            lanes = slice(w * 2 * cu, (w + 1) * 2 * cu)
            for h in range(2):
                mine = slice(h * rows // 2, (h + 1) * rows // 2)
                piece = jnp.concatenate([pair[0][mine], pair[1][mine]], axis=0)
                pre_ref[2 * t + h, :, lanes] = piece
                feat_refs[2 * t + h][:, lanes] = jax.nn.silu(piece).astype(BF16)


def run_up(x, wa, wb, spread):
    frames, outer, rows, ch = x.shape
    chunk = (rows, 2 * (outer - 2) * wa.shape[3])
    return pl.pallas_call(
        up_kernel,
        out_shape=[
            jax.ShapeDtypeStruct((2 * frames, *chunk), F32),
            *(jax.ShapeDtypeStruct(chunk, BF16) for _ in range(2 * frames)),
        ],
        in_specs=[VM] * 4,
        out_specs=[VM] * (1 + 2 * frames),
        scratch_shapes=[pltpu.VMEM((6 * outer * rows, spread.shape[1]), BF16)],
        name="up",
    )(x, wa, wb, spread)


def exact_dot(value, ones, dims):
    total = None
    for _ in range(3):
        piece = value.astype(BF16)
        value = value - piece.astype(F32)
        part = lax.dot_general(piece, ones, dims, preferred_element_type=F32)
        total = part if total is None else total + part
    return total


GROUP = 48


def group_masks(rows, groups):
    row = lax.broadcasted_iota(jnp.int32, (rows, groups * GROUP), 0)
    lane = lax.broadcasted_iota(jnp.int32, (rows, groups * GROUP), 1)
    wanted = (row % 8) * 2 + (row // 8) % 2
    return lane // GROUP == wanted


def fold_matrix(groups):
    lane = lax.broadcasted_iota(jnp.int32, (groups * GROUP, GROUP), 0)
    column = lax.broadcasted_iota(jnp.int32, (groups * GROUP, GROUP), 1)
    return (lane % GROUP == column).astype(F32).astype(BF16)


def logit_kernel(half_ref, z_ref, w_hbm, out_ref, table, w_buf, sem):
    outs, keep = w_buf.shape
    span = z_ref.shape[1]
    groups = keep // span
    copy = pltpu.make_async_copy(
        w_hbm.at[:, pl.ds(pl.multiple_of(half_ref[0] * keep, 128), keep)], w_buf, sem
    )
    copy.start()
    mask = group_masks(z_ref.shape[0], groups)
    fold = fold_matrix(groups)
    copy.wait()
    for r in range(groups // 2):
        true_row = 2 * (r % 4) + r // 4
        for e in range(2):
            at = (2 * r + e) * GROUP
            start = (2 * true_row + e) * span
            table[at : at + GROUP, :] = jnp.concatenate(
                [w_buf[:, start : start + span], jnp.zeros((GROUP - outs, span), BF16)], axis=0
            )
    pairs = lax.dot_general(
        z_ref[...], table[...], (((1,), (1,)), ((), ())), preferred_element_type=F32
    )
    pairs = jnp.where(mask, pairs, 0.0)
    patches = z_ref.shape[0] // groups
    summed = jnp.sum(pairs.reshape(patches, groups, groups * GROUP), axis=1)
    out_ref[...] = exact_dot(summed, fold, (((1,), (0,)), ((), ())))


def run_logit(half, z, weight, keep):
    outs = weight.shape[0]
    span = z.shape[1]
    groups = keep // span
    return pl.pallas_call(
        logit_kernel,
        out_shape=[
            jax.ShapeDtypeStruct((z.shape[0] // groups, GROUP), F32),
            jax.ShapeDtypeStruct((groups * GROUP, span), BF16),
        ],
        in_specs=[SM, VM, HB],
        out_specs=[VM, VM],
        scratch_shapes=[pltpu.VMEM((outs, keep), BF16), pltpu.SemaphoreType.DMA],
        name="logit",
    )(half, z, weight)


def back_kernel(mine_ref, other_ref, coef_ref, table_ref, out_ref):
    groups = table_ref.shape[0] // GROUP
    patches = mine_ref.shape[0]
    squashed = jnp.tanh(mine_ref[...] + other_ref[...])
    grad = (coef_ref[...] * (1.0 - squashed * squashed)).astype(BF16)
    wide = lax.dot_general(
        grad, fold_matrix(groups), (((1,), (1,)), ((), ())), preferred_element_type=F32
    )
    wide = jnp.broadcast_to(wide[:, None, :], (patches, groups, groups * GROUP))
    wide = wide.reshape(patches * groups, groups * GROUP)
    wide = jnp.where(group_masks(patches * groups, groups), wide, 0.0).astype(BF16)
    out_ref[...] = jnp.dot(wide, table_ref[...], preferred_element_type=F32).astype(BF16)


def run_back(mine, other, coef, table):
    rows = mine.shape[0] * table.shape[0] // GROUP
    return pl.pallas_call(
        back_kernel,
        out_shape=jax.ShapeDtypeStruct((rows, table.shape[1]), BF16),
        in_specs=[VM] * 4,
        out_specs=VM,
        name="back",
    )(mine, other, coef, table)


def sum_kernel(in_ref, out_ref):
    total = in_ref[0].astype(F32)
    for i in range(1, in_ref.shape[0]):
        total = total + in_ref[i].astype(F32)
    out_ref[...] = total.astype(BF16)


def run_sum(values):
    return pl.pallas_call(
        sum_kernel,
        out_shape=jax.ShapeDtypeStruct(values.shape[1:], BF16),
        in_specs=[VM],
        out_specs=VM,
        name="sum",
    )(values)


def adj_kernel(pre_ref, wa_ref, wb_ref, spread_ref, *rest):
    *grad_refs, gf_ref, l_ref, r_ref, held = rest
    frames, cols, rows, ch = gf_ref.shape
    outer = cols + 2
    cu = wa_ref.shape[1]
    half = wa_ref.shape[2]
    block = outer * rows
    held[:, frames * block :, :] = jnp.zeros((9, 2 * block, cu), BF16)
    zero = jnp.zeros((1, rows, cu), F32)
    for t in range(frames):
        chunks = []
        for h in range(2):
            pre = pre_ref[2 * t + h]
            sig = jax.nn.sigmoid(pre)
            grad = grad_refs[2 * t + h][...].astype(F32) * sig * (1.0 + pre * (1.0 - sig))
            chunks.append(grad.astype(BF16).astype(F32))
        fine = []
        for p in range(2):
            low = slice(p * rows // 2, (p + 1) * rows // 2)
            whole = jnp.concatenate([chunks[0][low], chunks[1][low]], axis=0)
            even, odd = (
                jnp.concatenate(
                    [whole[:, (2 * w + q) * cu : (2 * w + q + 1) * cu][None] for w in range(cols)], axis=0
                )
                for q in range(2)
            )
            own = jnp.concatenate([zero, even + odd, zero], axis=0)
            later = jnp.concatenate([even[:1], odd[:-1] + even[1:], odd[-1:], zero], axis=0)
            sooner = jnp.concatenate([zero, even[:1], odd[:-1] + even[1:], odd[-1:]], axis=0)
            fine.append([v.reshape(block, cu) for v in (later, own, sooner)])
        for c in range(3):
            top, low = fine[0][c], fine[1][c]
            _, top_after = row_shifts(top)
            low_before, _ = row_shifts(low)
            for b, v in enumerate((low + top_after, top + low, low_before + top)):
                held[3 * b + c, t * block : (t + 1) * block, :] = v.astype(BF16)
    out = None
    for part, w_ref in enumerate((wa_ref, wb_ref)):
        acc = jnp.zeros((frames * block, half), F32)
        for a in range(3):
            for bc in range(9):
                acc = acc + jnp.dot(
                    held[bc, (2 - a) * block : (2 - a + frames) * block, :],
                    w_ref[9 * a + bc],
                    preferred_element_type=F32,
                )
        ordered = exact_dot(
            acc, spread_ref[:, part * half : (part + 1) * half], (((1,), (1,)), ((), ()))
        )
        out = ordered if out is None else out + ordered
    out = out.reshape(frames, outer, rows, ch)
    gf_ref[...] = out[:, 1:-1]
    l_ref[...] = out[:, :2].astype(BF16)
    r_ref[...] = out[:, -2:].astype(BF16)


def run_adj(grads, pre, wa, wb, spread, frames, cols):
    rows = pre.shape[1]
    ch = spread.shape[0]
    cu = wa.shape[1]
    return pl.pallas_call(
        adj_kernel,
        out_shape=[
            jax.ShapeDtypeStruct((frames, cols, rows, ch), F32),
            jax.ShapeDtypeStruct((frames, 2, rows, ch), BF16),
            jax.ShapeDtypeStruct((frames, 2, rows, ch), BF16),
        ],
        in_specs=[VM] * (4 + len(grads)),
        out_specs=[VM] * 3,
        scratch_shapes=[pltpu.VMEM((9, 6 * (cols + 2) * rows, cu), BF16)],
        name="adj",
    )(pre, wa, wb, spread, *grads)


def on_device(latent, frame_order, section_weight, section_gain, up_weight, reward_weight, reward_coef):
    segs = lax.axis_size("segment")
    chips = lax.axis_size("chip")
    tiles = 2 * chips
    seg = lax.axis_index("segment")
    core = lax.axis_index("core")
    tile = 2 * lax.axis_index("chip") + core
    frames, rows, cols, ch = latent.shape
    cu = up_weight.shape[2]
    outs_dev = reward_coef.shape[0]
    last = segs - 1
    halves = segs // frames
    span = 2 * cols * cu
    keep = 2 * rows // halves * 2 * span
    barrier = lax.optimization_barrier
    tile_info = jnp.stack([tile, jnp.full_like(tile, tiles)])
    block = (frames, cols, rows, ch)
    side = (frames, 1, rows, ch)
    side2 = (frames, 2, rows, ch)

    def route(pairs_of_segments, shift):
        return [
            (source * tiles + t, target * tiles + t + shift)
            for source, target in pairs_of_segments
            for t in range(tiles)
            if 0 <= t + shift < tiles
        ]

    def send(value, source, target):
        return lax.ppermute(value, AXES, route([(source, target)], 0))

    def beside(value, shift):
        return lax.ppermute(value, AXES, route([(s, s) for s in range(segs)], shift))

    def hop(center, left, right, source, target):
        step = target - source
        pairs = [(s, s + step) for s in range(source % 2, segs, 2) if 0 <= s + step < segs]
        return tuple(
            lax.ppermute(value, AXES, route(pairs, shift))
            for value, shift in ((center, 0), (right, 1), (left, -1))
        )

    def gather_up():
        own = up_weight.shape[1]
        source = jnp.pad(up_weight, ((0, 0), (0, PAD - own), (0, 0)))
        wa = lax.all_to_all(
            jnp.broadcast_to(source[None], (chips, *source.shape)), "chip", 0, 0, tiled=True
        )
        wb = lax.ppermute(wa, "core", [(0, 1), (1, 0)])
        back_a, back_b = (w.transpose(1, 3, 0, 2).reshape(27, cu, chips * PAD) for w in (wa, wb))
        channel = lax.broadcasted_iota(jnp.int32, (ch, tiles * PAD), 0)
        place = lax.broadcasted_iota(jnp.int32, (ch, tiles * PAD), 1)
        other, chip_of, within = place // (chips * PAD), place // PAD % chips, place % PAD
        origin = 2 * chip_of + jnp.where(other == 0, core, 1 - core)
        spread = ((within < own) & (channel == origin * own + within)).astype(BF16)
        return wa, wb, back_a, back_b, spread

    up_shape = (chips, 27, PAD, cu)
    back_shape = (27, cu, chips * PAD)

    def turn(weight):
        return weight[0].transpose(0, 2, 1).reshape(27 * ch, ch)

    def start():
        x, left, right = run_first(frame_order, latent.transpose(0, 2, 1, 3))
        return x, beside(right, 1), beside(left, -1)

    weight_fwd = section_weight[0].reshape(27 * ch, ch)
    gathered = lax.cond(
        seg == last,
        gather_up,
        lambda: unwritten(up_shape, up_shape, back_shape, back_shape, (ch, tiles * PAD)),
    )
    turned = lax.cond(seg > 0, lambda: turn(section_weight), lambda: unwritten((27 * ch, ch))[0])
    state = lax.cond(
        seg == 0, start, lambda: tuple(jnp.zeros(s, BF16) for s in (block, side, side))
    )
    gathered, turned, state = barrier((gathered, turned, state))

    kept = [state[0]]
    for k in range(last):
        wide = k == last - 1
        edge = side2 if wide else side

        def go(state, k=k, wide=wide, edge=edge):
            made = lax.cond(
                seg == k,
                lambda: tuple(run_fwd(1, 2 if wide else 1, tile_info, *state, section_gain, weight_fwd)),
                lambda: unwritten(block, edge, edge),
            )
            return hop(*made, k, k + 1)

        def skip(state, wide=wide):
            if wide:
                return state[0], jnp.zeros(side2, BF16), jnp.zeros(side2, BF16)
            return state

        state = lax.cond((seg == k) | (seg == k + 1), go, skip, state)
        kept.append(state[0])
    x_kept = functools.reduce(jnp.add, kept)

    chunk = (rows, span)

    def upsampled():
        (deep,) = run_fwd(2, 0, tile_info, *state, section_gain, weight_fwd)
        return tuple(run_up(deep, gathered[0], gathered[1], gathered[4]))

    pre, *feats = lax.cond(
        seg == last,
        upsampled,
        lambda: (
            jnp.zeros((segs, *chunk), F32),
            *unwritten(*([chunk] * last)),
            jnp.zeros(chunk, BF16),
        ),
    )
    turned_first = lax.cond(seg == 0, lambda: turn(section_weight), lambda: unwritten((27 * ch, ch))[0])
    turned_first, feats = barrier((turned_first, feats))
    mine = functools.reduce(jnp.add, [send(feats[k], last, k) for k in range(last)], feats[last])
    everyone = lax.all_to_all(
        jnp.broadcast_to(mine[None], (tiles, *chunk)), TILE, 0, 0, tiled=True
    )
    half = (seg % halves).reshape(1)
    partial, table = run_logit(half, everyone.reshape(tiles * rows, span), reward_weight.T, keep)
    group = [(s, s // halves * halves + (s + 1) % halves) for s in range(segs)]
    other = lax.ppermute(partial, "segment", group)
    coef = jnp.pad(reward_coef, (0, GROUP - outs_dev))[None]
    shares = run_back(partial, other, coef, table)
    shares = lax.all_to_all(shares.reshape(tiles, *chunk), TILE, 0, 0, tiled=True)
    share = run_sum(shares)
    grads = [send(share, k, last) for k in range(last)] + [share]

    result = jnp.zeros(block, F32)

    def go_last(result):
        def live():
            deep, lp, rp = run_adj(grads, pre, gathered[2], gathered[3], gathered[4], frames, cols)
            from_r, from_l = beside(lp, -1), beside(rp, 1)
            args = (tile_info, deep, lp, rp, from_l, from_r)
            made = run_bwd(True, False, args, x_kept, section_gain, turned)
            return (*made[1:], made[0])

        *made, result = lax.cond(
            seg == last, live, lambda: (*unwritten(block, side, side), result)
        )
        return (*hop(*made, last, last - 1), result)

    zeros = tuple(jnp.zeros(s, BF16) for s in (block, side, side))
    state = lax.cond(seg >= last - 1, go_last, lambda result: (*zeros, result), result)
    for k in range(last - 1, 0, -1):

        def go_back(state, k=k):
            def live():
                made = run_bwd(False, False, state[:3], x_kept, section_gain, turned)
                return (*made[1:], made[0])

            *made, result = lax.cond(
                seg == k, live, lambda: (*unwritten(block, side, side), state[3])
            )
            return (*hop(*made, k, k - 1), result)

        state = lax.cond((seg == k) | (seg == k - 1), go_back, lambda state: state, state)
    result = lax.cond(
        seg == 0,
        lambda: run_bwd(False, True, state[:3], x_kept, section_gain, turned_first)[0],
        lambda: state[3],
    )
    return result.transpose(0, 2, 1, 3)[None]


def solution(mesh):
    shape = mesh.devices.shape
    fine = jax.sharding.Mesh(mesh.devices.reshape(shape[0], shape[1] // 2, 2), AXES)
    in_specs = (
        P(None, None, TILE, None),
        P(),
        P("segment", None, None, None),
        P("segment", None),
        P(None, TILE, None),
        P(None, TILE),
        P(TILE),
    )
    out_specs = P("segment", None, None, TILE, None)
    return jax.shard_map(
        on_device, mesh=fine, in_specs=in_specs, out_specs=out_specs, check_vma=False
    )
```

```python
import functools

import jax
import jax.numpy as jnp
from jax import lax
from jax.experimental import pallas as pl
from jax.experimental.pallas import tpu as pltpu
from jax.sharding import PartitionSpec as P

EPS = 1e-06
F32 = jnp.float32
BF16 = jnp.bfloat16
AXES = ("segment", "chip", "core")
TILE = ("chip", "core")
PAD = 16
VM = pl.BlockSpec(memory_space=pltpu.VMEM)
HB = pl.BlockSpec(memory_space=pl.ANY)
SM = pl.BlockSpec(memory_space=pltpu.SMEM)
GRANT = pltpu.CompilerParams(vmem_limit_bytes=24 * 2**20)


def row_shifts(v):
    count = v.shape[0]
    row = lax.broadcasted_iota(jnp.int32, v.shape, 0) & 7
    before = jnp.where(row == 0, 0.0, pltpu.roll(v, 1, 0))
    after = jnp.where(row == 7, 0.0, pltpu.roll(v, count - 1, 0))
    return before, after


PIECES = (1024, 1024, 1024, 384)


def weight_copies(w_hbm, w_buf, sem, order):
    rows = w_hbm.shape[0] // 3
    copies = []
    for a in order:
        start = a * rows
        for size in PIECES:
            part = pl.ds(start, size)
            copy = pltpu.make_async_copy(w_hbm.at[part], w_buf.at[part], sem.at[len(copies)])
            copies.append((copy, a, start, start - a * rows, size))
            start += size
    return copies


def fwd_kernel(edge, tile_ref, xc, xl, xr, gain_ref, w_hbm, *rest):
    wide = edge == 2
    if wide:
        y_ref, taps, w_buf, sem = rest
    else:
        y_ref, yl_ref, yr_ref, taps, w_buf, sem = rest
    copies = weight_copies(w_hbm, w_buf, sem, range(3))
    for copy, *_ in copies:
        copy.start()
    frames, cols, rows, ch = xc.shape
    outer = cols + 2 * edge
    inner = outer - 2
    block = inner * rows
    gain = gain_ref[...].astype(F32)
    taps[0 : 2 * block, :] = jnp.zeros((2 * block, 9 * ch), BF16)
    kept = []
    for t in range(frames):
        x = jnp.concatenate([xl[t], xc[t], xr[t]], axis=0).astype(F32).reshape(outer * rows, ch)
        inv = lax.rsqrt(jnp.mean(x * x, axis=-1, keepdims=True) + EPS)
        act = jax.nn.silu(x * inv * gain)
        before, after = row_shifts(act)
        for b, v in enumerate((before, act, after)):
            for c in range(3):
                at = (3 * b + c) * ch
                taps[(2 + t) * block : (3 + t) * block, at : at + ch] = v[
                    c * rows : c * rows + block
                ].astype(BF16)
    acc = jnp.zeros((frames * block, ch), F32)
    for copy, a, start, at, size in copies:
        copy.wait()
        acc = acc + jnp.dot(
            taps[a * block : (a + frames) * block, at : at + size],
            w_buf[start : start + size, :],
            preferred_element_type=F32,
        )
    for t in range(frames):
        if wide:
            x = jnp.concatenate([xl[t, 1:], xc[t], xr[t, :1]], axis=0)
        else:
            x = xc[t]
        out = x.astype(F32) + acc[t * block : (t + 1) * block].reshape(inner, rows, ch)
        if wide:
            tile = tile_ref[0]
            col = lax.broadcasted_iota(jnp.int32, out.shape, 0)
            low = jnp.where(tile == 0, 1, 0)
            high = jnp.where(tile == tile_ref[1] - 1, inner - 1, inner)
            out = jnp.where((col >= low) & (col < high), out, 0.0)
            y_ref[t] = out.astype(BF16)
        else:
            out = out.astype(BF16)
            y_ref[t] = out
            e = yl_ref.shape[1]
            yl_ref[t] = out[:e]
            yr_ref[t] = out[cols - e :]


def run_fwd(edge, out_edge, tile_info, xc, xl, xr, gain, weight):
    frames, cols, rows, ch = xc.shape
    block = (cols + 2 * edge - 2) * rows
    if edge == 2:
        outs = [jax.ShapeDtypeStruct((frames, cols + 2, rows, ch), BF16)]
    else:
        outs = [jax.ShapeDtypeStruct((frames, n, rows, ch), BF16) for n in (cols, out_edge, out_edge)]
    return pl.pallas_call(
        functools.partial(fwd_kernel, edge),
        out_shape=outs,
        in_specs=[SM, VM, VM, VM, VM, HB],
        out_specs=[VM] * len(outs),
        scratch_shapes=[
            pltpu.VMEM((6 * block, 9 * ch), BF16),
            pltpu.VMEM(weight.shape, BF16),
            pltpu.SemaphoreType.DMA((3 * len(PIECES),)),
        ],
        name=f"fwd{edge}{out_edge}",
        compiler_params=GRANT,
    )(tile_info, xc, xl, xr, gain, weight)


def bwd_kernel(first, *refs):
    if first:
        tile_ref, gc, lp, rp, from_l, from_r, x_ref, gain_ref, w_hbm, *rest = refs
    else:
        gc, gl, gr, x_ref, gain_ref, w_hbm, *rest = refs
    *outs, taps, w_buf, sem = rest
    copies = weight_copies(w_hbm, w_buf, sem, reversed(range(3)))
    for copy, *_ in copies:
        copy.start()
    frames, cols, rows, ch = gc.shape
    block = cols * rows
    outer = cols + 2
    gain = gain_ref[...].astype(F32)
    taps[4 * block : 6 * block, :] = jnp.zeros((2 * block, 9 * ch), BF16)

    def center(t):
        mid = gc[t].astype(F32)
        if not first:
            return mid
        return jnp.concatenate(
            [mid[:1] + from_l[t, 1:].astype(F32), mid[1:-1], mid[-1:] + from_r[t, :1].astype(F32)], axis=0
        )

    for t in range(frames):
        if first:
            left = from_l[t, :1].astype(F32) + lp[t, :1].astype(F32)
            right = from_r[t, 1:].astype(F32) + rp[t, 1:].astype(F32)
            left = jnp.where(tile_ref[0] == 0, 0.0, left)
            right = jnp.where(tile_ref[0] == tile_ref[1] - 1, 0.0, right)
        else:
            left, right = gl[t].astype(F32), gr[t].astype(F32)
        g = jnp.concatenate([left, center(t), right], axis=0).reshape(outer * rows, ch)
        before, after = row_shifts(g)
        for b, v in enumerate((after, g, before)):
            for c in range(3):
                at = (3 * b + c) * ch
                taps[t * block : (t + 1) * block, at : at + ch] = v[
                    (2 - c) * rows : (2 - c) * rows + block
                ].astype(BF16)
    acc = jnp.zeros((frames * block, ch), F32)
    for copy, a, start, at, size in copies:
        copy.wait()
        acc = acc + jnp.dot(
            taps[(2 - a) * block : (2 - a + frames) * block, at : at + size],
            w_buf[start : start + size, :],
            preferred_element_type=F32,
        )
    for t in range(frames):
        x = x_ref[t].astype(F32).reshape(block, ch)
        inv = lax.rsqrt(jnp.mean(x * x, axis=-1, keepdims=True) + EPS)
        u = x * inv * gain
        sig = jax.nn.sigmoid(u)
        y = acc[t * block : (t + 1) * block] * (sig * (1.0 + u * (1.0 - sig))) * gain
        mean = jnp.mean(y * x, axis=-1, keepdims=True)
        dx = inv * (y - x * (inv * inv * mean))
        out = center(t) + dx.reshape(cols, rows, ch)
        outs[0][t] = out
        if len(outs) == 4:
            out = out.astype(BF16)
            outs[1][t] = out
            outs[2][t] = out[:1]
            outs[3][t] = out[cols - 1 :]


def run_bwd(first, last, args, x, gain, weight_back):
    frames, cols, rows, ch = x.shape
    outs = [jax.ShapeDtypeStruct((frames, cols, rows, ch), F32)]
    if not last:
        outs += [jax.ShapeDtypeStruct((frames, n, rows, ch), BF16) for n in (cols, 1, 1)]
    specs = [SM] + [VM] * (len(args) - 1) if first else [VM] * len(args)
    return pl.pallas_call(
        functools.partial(bwd_kernel, first),
        out_shape=outs,
        in_specs=[*specs, VM, VM, HB],
        out_specs=[VM] * len(outs),
        scratch_shapes=[
            pltpu.VMEM((6 * cols * rows, 9 * ch), BF16),
            pltpu.VMEM(weight_back.shape, BF16),
            pltpu.SemaphoreType.DMA((3 * len(PIECES),)),
        ],
        name="bwd",
        compiler_params=GRANT,
    )(*args, x, gain, weight_back)


def first_kernel(order_ref, latent_ref, x_ref, l_ref, r_ref):
    for t in range(x_ref.shape[0]):
        x = latent_ref[order_ref[t]]
        x_ref[t] = x
        l_ref[t] = x[:1]
        r_ref[t] = x[x.shape[0] - 1 :]


def run_first(order, latent):
    frames, cols, rows, ch = latent.shape
    return pl.pallas_call(
        first_kernel,
        out_shape=[jax.ShapeDtypeStruct((frames, n, rows, ch), BF16) for n in (cols, 1, 1)],
        in_specs=[SM, VM],
        out_specs=[VM] * 3,
        name="first",
        compiler_params=GRANT,
    )(order, latent)


def unwritten(*shapes):
    return tuple(
        pl.pallas_call(
            lambda out_ref: None,
            out_shape=jax.ShapeDtypeStruct(shape, BF16),
            out_specs=HB,
            name="unwritten",
        )()
        for shape in shapes
    )


def up_kernel(x_ref, wa_ref, wb_ref, spread_ref, *rest):
    pre_ref, *feat_refs, held = rest
    frames, outer, rows, ch = x_ref.shape
    cols = outer - 2
    cu = wa_ref.shape[3]
    half = wa_ref.shape[0] * wa_ref.shape[2]
    block = outer * rows
    held[0 : 2 * block, :] = jnp.zeros((2 * block, 2 * half), BF16)
    for t in range(frames):
        held[(2 + t) * block : (3 + t) * block, :] = jnp.dot(
            x_ref[t].reshape(block, ch), spread_ref[...], preferred_element_type=F32
        ).astype(BF16)
    by_phase = [[], []]
    for c in range(3):
        cells = []
        for b in range(3):
            total = jnp.zeros((frames * block, cu), F32)
            for a in range(3):
                for part, w_ref in enumerate((wa_ref, wb_ref)):
                    total = total + jnp.dot(
                        held[a * block : (a + frames) * block, part * half : (part + 1) * half],
                        w_ref[:, 9 * a + 3 * b + c].reshape(half, cu),
                        preferred_element_type=F32,
                    )
            cells.append(total)
        before, _ = row_shifts(cells[0])
        _, after = row_shifts(cells[2])
        shape = (frames, outer, rows, cu)
        by_phase[0].append((before + cells[1] + cells[2]).reshape(shape))
        by_phase[1].append((cells[0] + cells[1] + after).reshape(shape))
    pres = []
    for p in range(2):
        left, mid, right = by_phase[p]
        pres.append(
            [
                left[:, 0:cols] + mid[:, 1 : cols + 1] + right[:, 1 : cols + 1],
                left[:, 1 : cols + 1] + mid[:, 1 : cols + 1] + right[:, 2 : cols + 2],
            ]
        )
    for t in range(frames):
        for w in range(cols):
            pair = [jnp.concatenate([pres[p][0][t, w], pres[p][1][t, w]], axis=1) for p in range(2)]
            lanes = slice(w * 2 * cu, (w + 1) * 2 * cu)
            for h in range(2):
                mine = slice(h * rows // 2, (h + 1) * rows // 2)
                piece = jnp.concatenate([pair[0][mine], pair[1][mine]], axis=0)
                pre_ref[2 * t + h, :, lanes] = piece
                feat_refs[2 * t + h][:, lanes] = jax.nn.silu(piece).astype(BF16)


def run_up(x, wa, wb, spread):
    frames, outer, rows, ch = x.shape
    chunk = (rows, 2 * (outer - 2) * wa.shape[3])
    return pl.pallas_call(
        up_kernel,
        out_shape=[
            jax.ShapeDtypeStruct((2 * frames, *chunk), F32),
            *(jax.ShapeDtypeStruct(chunk, BF16) for _ in range(2 * frames)),
        ],
        in_specs=[VM] * 4,
        out_specs=[VM] * (1 + 2 * frames),
        scratch_shapes=[pltpu.VMEM((6 * outer * rows, spread.shape[1]), BF16)],
        name="up",
        compiler_params=GRANT,
    )(x, wa, wb, spread)


def exact_dot(value, ones, dims):
    total = None
    for _ in range(3):
        piece = value.astype(BF16)
        value = value - piece.astype(F32)
        part = lax.dot_general(piece, ones, dims, preferred_element_type=F32)
        total = part if total is None else total + part
    return total


GROUP = 48


def group_masks(rows, groups):
    row = lax.broadcasted_iota(jnp.int32, (rows, groups * GROUP), 0)
    lane = lax.broadcasted_iota(jnp.int32, (rows, groups * GROUP), 1)
    wanted = (row % 8) * 2 + (row // 8) % 2
    return lane // GROUP == wanted


def fold_matrix(groups):
    lane = lax.broadcasted_iota(jnp.int32, (groups * GROUP, GROUP), 0)
    column = lax.broadcasted_iota(jnp.int32, (groups * GROUP, GROUP), 1)
    return (lane % GROUP == column).astype(F32).astype(BF16)


def logit_kernel(half_ref, z_ref, w_hbm, out_ref, table, w_buf, sem):
    outs, keep = w_buf.shape
    span = z_ref.shape[1]
    groups = keep // span
    copy = pltpu.make_async_copy(
        w_hbm.at[:, pl.ds(pl.multiple_of(half_ref[0] * keep, 128), keep)], w_buf, sem
    )
    copy.start()
    mask = group_masks(z_ref.shape[0], groups)
    fold = fold_matrix(groups)
    copy.wait()
    for r in range(groups // 2):
        true_row = 2 * (r % 4) + r // 4
        for e in range(2):
            at = (2 * r + e) * GROUP
            start = (2 * true_row + e) * span
            table[at : at + GROUP, :] = jnp.concatenate(
                [w_buf[:, start : start + span], jnp.zeros((GROUP - outs, span), BF16)], axis=0
            )
    pairs = lax.dot_general(
        z_ref[...], table[...], (((1,), (1,)), ((), ())), preferred_element_type=F32
    )
    pairs = jnp.where(mask, pairs, 0.0)
    patches = z_ref.shape[0] // groups
    summed = jnp.sum(pairs.reshape(patches, groups, groups * GROUP), axis=1)
    out_ref[...] = exact_dot(summed, fold, (((1,), (0,)), ((), ())))


def run_logit(half, z, weight, keep):
    outs = weight.shape[0]
    span = z.shape[1]
    groups = keep // span
    return pl.pallas_call(
        logit_kernel,
        out_shape=[
            jax.ShapeDtypeStruct((z.shape[0] // groups, GROUP), F32),
            jax.ShapeDtypeStruct((groups * GROUP, span), BF16),
        ],
        in_specs=[SM, VM, HB],
        out_specs=[VM, VM],
        scratch_shapes=[pltpu.VMEM((outs, keep), BF16), pltpu.SemaphoreType.DMA],
        name="logit",
        compiler_params=GRANT,
    )(half, z, weight)


def back_kernel(mine_ref, other_ref, coef_ref, table_ref, out_ref):
    groups = table_ref.shape[0] // GROUP
    patches = mine_ref.shape[0]
    squashed = jnp.tanh(mine_ref[...] + other_ref[...])
    grad = (coef_ref[...] * (1.0 - squashed * squashed)).astype(BF16)
    wide = lax.dot_general(
        grad, fold_matrix(groups), (((1,), (1,)), ((), ())), preferred_element_type=F32
    )
    wide = jnp.broadcast_to(wide[:, None, :], (patches, groups, groups * GROUP))
    wide = wide.reshape(patches * groups, groups * GROUP)
    wide = jnp.where(group_masks(patches * groups, groups), wide, 0.0).astype(BF16)
    out_ref[...] = jnp.dot(wide, table_ref[...], preferred_element_type=F32).astype(BF16)


def run_back(mine, other, coef, table):
    rows = mine.shape[0] * table.shape[0] // GROUP
    return pl.pallas_call(
        back_kernel,
        out_shape=jax.ShapeDtypeStruct((rows, table.shape[1]), BF16),
        in_specs=[VM] * 4,
        out_specs=VM,
        name="back",
        compiler_params=GRANT,
    )(mine, other, coef, table)


def sum_kernel(in_ref, out_ref):
    total = in_ref[0].astype(F32)
    for i in range(1, in_ref.shape[0]):
        total = total + in_ref[i].astype(F32)
    out_ref[...] = total.astype(BF16)


def run_sum(values):
    return pl.pallas_call(
        sum_kernel,
        out_shape=jax.ShapeDtypeStruct(values.shape[1:], BF16),
        in_specs=[VM],
        out_specs=VM,
        name="sum",
        compiler_params=GRANT,
    )(values)


def adj_kernel(pre_ref, wa_ref, wb_ref, spread_ref, *rest):
    *grad_refs, gf_ref, l_ref, r_ref, held = rest
    frames, cols, rows, ch = gf_ref.shape
    outer = cols + 2
    cu = wa_ref.shape[3]
    half = wa_ref.shape[0] * wa_ref.shape[2]
    block = outer * rows
    held[:, frames * block :, :] = jnp.zeros((9, 2 * block, cu), BF16)
    zero = jnp.zeros((1, rows, cu), F32)
    for t in range(frames):
        chunks = []
        for h in range(2):
            pre = pre_ref[2 * t + h]
            sig = jax.nn.sigmoid(pre)
            grad = grad_refs[2 * t + h][...].astype(F32) * sig * (1.0 + pre * (1.0 - sig))
            chunks.append(grad.astype(BF16).astype(F32))
        fine = []
        for p in range(2):
            low = slice(p * rows // 2, (p + 1) * rows // 2)
            whole = jnp.concatenate([chunks[0][low], chunks[1][low]], axis=0)
            even, odd = (
                jnp.concatenate(
                    [whole[:, (2 * w + q) * cu : (2 * w + q + 1) * cu][None] for w in range(cols)], axis=0
                )
                for q in range(2)
            )
            own = jnp.concatenate([zero, even + odd, zero], axis=0)
            later = jnp.concatenate([even[:1], odd[:-1] + even[1:], odd[-1:], zero], axis=0)
            sooner = jnp.concatenate([zero, even[:1], odd[:-1] + even[1:], odd[-1:]], axis=0)
            fine.append([v.reshape(block, cu) for v in (later, own, sooner)])
        for c in range(3):
            top, low = fine[0][c], fine[1][c]
            _, top_after = row_shifts(top)
            low_before, _ = row_shifts(low)
            for b, v in enumerate((low + top_after, top + low, low_before + top)):
                held[3 * b + c, t * block : (t + 1) * block, :] = v.astype(BF16)
    out = None
    for part, w_ref in enumerate((wa_ref, wb_ref)):
        acc = jnp.zeros((frames * block, half), F32)
        for a in range(3):
            for bc in range(9):
                acc = acc + lax.dot_general(
                    held[bc, (2 - a) * block : (2 - a + frames) * block, :],
                    w_ref[:, 9 * a + bc].reshape(half, cu),
                    (((1,), (1,)), ((), ())),
                    preferred_element_type=F32,
                )
        ordered = exact_dot(
            acc, spread_ref[:, part * half : (part + 1) * half], (((1,), (1,)), ((), ()))
        )
        out = ordered if out is None else out + ordered
    out = out.reshape(frames, outer, rows, ch)
    gf_ref[...] = out[:, 1:-1]
    l_ref[...] = out[:, :2].astype(BF16)
    r_ref[...] = out[:, -2:].astype(BF16)


def run_adj(grads, pre, wa, wb, spread, frames, cols):
    rows = pre.shape[1]
    ch = spread.shape[0]
    cu = wa.shape[3]
    return pl.pallas_call(
        adj_kernel,
        out_shape=[
            jax.ShapeDtypeStruct((frames, cols, rows, ch), F32),
            jax.ShapeDtypeStruct((frames, 2, rows, ch), BF16),
            jax.ShapeDtypeStruct((frames, 2, rows, ch), BF16),
        ],
        in_specs=[VM] * (4 + len(grads)),
        out_specs=[VM] * 3,
        scratch_shapes=[pltpu.VMEM((9, 6 * (cols + 2) * rows, cu), BF16)],
        name="adj",
        compiler_params=GRANT,
    )(pre, wa, wb, spread, *grads)


def on_device(latent, frame_order, section_weight, section_gain, up_weight, reward_weight, reward_coef):
    segs = lax.axis_size("segment")
    chips = lax.axis_size("chip")
    tiles = 2 * chips
    seg = lax.axis_index("segment")
    core = lax.axis_index("core")
    tile = 2 * lax.axis_index("chip") + core
    frames, rows, cols, ch = latent.shape
    cu = up_weight.shape[2]
    outs_dev = reward_coef.shape[0]
    last = segs - 1
    halves = segs // frames
    span = 2 * cols * cu
    keep = 2 * rows // halves * 2 * span
    barrier = lax.optimization_barrier
    tile_info = jnp.stack([tile, jnp.full_like(tile, tiles)])
    block = (frames, cols, rows, ch)
    side = (frames, 1, rows, ch)
    side2 = (frames, 2, rows, ch)

    def route(pairs_of_segments, shift):
        return [
            (source * tiles + t, target * tiles + t + shift)
            for source, target in pairs_of_segments
            for t in range(tiles)
            if 0 <= t + shift < tiles
        ]

    def send(value, source, target):
        return lax.ppermute(value, AXES, route([(source, target)], 0))

    def beside(value, shift):
        return lax.ppermute(value, AXES, route([(s, s) for s in range(segs)], shift))

    def hop(center, left, right, source, target):
        step = target - source
        pairs = [(s, s + step) for s in range(source % 2, segs, 2) if 0 <= s + step < segs]
        return tuple(
            lax.ppermute(value, AXES, route(pairs, shift))
            for value, shift in ((center, 0), (right, 1), (left, -1))
        )

    def gather_up():
        own = up_weight.shape[1]
        source = jnp.pad(up_weight, ((0, 0), (0, PAD - own), (0, 0)))
        wa = lax.all_to_all(
            jnp.broadcast_to(source[None], (chips, *source.shape)), "chip", 0, 0, tiled=True
        )
        wb = lax.ppermute(wa, "core", [(0, 1), (1, 0)])
        channel = lax.broadcasted_iota(jnp.int32, (ch, tiles * PAD), 0)
        place = lax.broadcasted_iota(jnp.int32, (ch, tiles * PAD), 1)
        other, chip_of, within = place // (chips * PAD), place // PAD % chips, place % PAD
        origin = 2 * chip_of + jnp.where(other == 0, core, 1 - core)
        spread = ((within < own) & (channel == origin * own + within)).astype(BF16)
        return wa, wb, spread

    up_shape = (chips, 27, PAD, cu)

    def turn(weight):
        return weight[0].transpose(0, 2, 1).reshape(27 * ch, ch)

    def start():
        x, left, right = run_first(frame_order, latent.transpose(0, 2, 1, 3))
        return x, beside(right, 1), beside(left, -1)

    weight_fwd = section_weight[0].reshape(27 * ch, ch)
    gathered = lax.cond(
        seg == last,
        gather_up,
        lambda: unwritten(up_shape, up_shape, (ch, tiles * PAD)),
    )
    turned = lax.cond(seg > 0, lambda: turn(section_weight), lambda: unwritten((27 * ch, ch))[0])
    state = lax.cond(
        seg == 0, start, lambda: tuple(jnp.zeros(s, BF16) for s in (block, side, side))
    )
    gathered, turned, state = barrier((gathered, turned, state))

    kept = [state[0]]
    for k in range(last):
        wide = k == last - 1
        edge = side2 if wide else side

        def go(state, k=k, wide=wide, edge=edge):
            made = lax.cond(
                seg == k,
                lambda: tuple(run_fwd(1, 2 if wide else 1, tile_info, *state, section_gain, weight_fwd)),
                lambda: unwritten(block, edge, edge),
            )
            return hop(*made, k, k + 1)

        def skip(state, wide=wide):
            if wide:
                return state[0], jnp.zeros(side2, BF16), jnp.zeros(side2, BF16)
            return state

        state = lax.cond((seg == k) | (seg == k + 1), go, skip, state)
        kept.append(state[0])
        if k == 1:
            late, state = barrier((section_weight, state))
            turned_first = lax.cond(
                seg == 0, lambda late=late: turn(late), lambda: unwritten((27 * ch, ch))[0]
            )
            turned_first, state = barrier((turned_first, state))
    x_kept = functools.reduce(jnp.add, kept)

    chunk = (rows, span)

    def upsampled():
        (deep,) = run_fwd(2, 0, tile_info, *state, section_gain, weight_fwd)
        return tuple(run_up(deep, *gathered))

    pre, *feats = lax.cond(
        seg == last,
        upsampled,
        lambda: (
            jnp.zeros((segs, *chunk), F32),
            *unwritten(*([chunk] * last)),
            jnp.zeros(chunk, BF16),
        ),
    )
    mine = functools.reduce(jnp.add, [send(feats[k], last, k) for k in range(last)], feats[last])
    coef = jnp.pad(reward_coef, (0, GROUP - outs_dev))[None]
    mine, x_kept, coef = barrier((mine, x_kept, coef))
    everyone = lax.all_to_all(
        jnp.broadcast_to(mine[None], (tiles, *chunk)), TILE, 0, 0, tiled=True
    )
    half = (seg % halves).reshape(1)
    partial, table = run_logit(half, everyone.reshape(tiles * rows, span), reward_weight.T, keep)
    group = [(s, s // halves * halves + (s + 1) % halves) for s in range(segs)]
    other = lax.ppermute(partial, "segment", group)
    shares = run_back(partial, other, coef, table)
    shares = lax.all_to_all(shares.reshape(tiles, *chunk), TILE, 0, 0, tiled=True)
    share = run_sum(shares)
    grads = [send(share, k, last) for k in range(last)] + [share]

    result = jnp.zeros(block, F32)

    def go_last(result):
        def live():
            deep, lp, rp = run_adj(grads, pre, *gathered, frames, cols)
            from_r, from_l = beside(lp, -1), beside(rp, 1)
            args = (tile_info, deep, lp, rp, from_l, from_r)
            made = run_bwd(True, False, args, x_kept, section_gain, turned)
            return (*made[1:], made[0])

        *made, result = lax.cond(
            seg == last, live, lambda: (*unwritten(block, side, side), result)
        )
        return (*hop(*made, last, last - 1), result)

    zeros = tuple(jnp.zeros(s, BF16) for s in (block, side, side))
    state = lax.cond(seg >= last - 1, go_last, lambda result: (*zeros, result), result)
    for k in range(last - 1, 0, -1):

        def go_back(state, k=k):
            def live():
                made = run_bwd(False, False, state[:3], x_kept, section_gain, turned)
                return (*made[1:], made[0])

            *made, result = lax.cond(
                seg == k, live, lambda: (*unwritten(block, side, side), state[3])
            )
            return (*hop(*made, k, k - 1), result)

        state = lax.cond((seg == k) | (seg == k - 1), go_back, lambda state: state, state)
    result = lax.cond(
        seg == 0,
        lambda: run_bwd(False, True, state[:3], x_kept, section_gain, turned_first)[0],
        lambda: state[3],
    )
    return result.transpose(0, 2, 1, 3)[None]


def solution(mesh):
    shape = mesh.devices.shape
    fine = jax.sharding.Mesh(mesh.devices.reshape(shape[0], shape[1] // 2, 2), AXES)
    in_specs = (
        P(None, None, TILE, None),
        P(),
        P("segment", None, None, None),
        P("segment", None),
        P(None, TILE, None),
        P(None, TILE),
        P(TILE),
    )
    out_specs = P("segment", None, None, TILE, None)
    return jax.shard_map(
        on_device, mesh=fine, in_specs=in_specs, out_specs=out_specs, check_vma=False
    )
```

```python
import functools

import jax
import jax.numpy as jnp
from jax import lax
from jax.experimental import pallas as pl
from jax.experimental.pallas import tpu as pltpu
from jax.sharding import PartitionSpec as P

EPS = 1e-06
F32 = jnp.float32
BF16 = jnp.bfloat16
AXES = ("segment", "chip", "core")
TILE = ("chip", "core")
PAD = 16
VM = pl.BlockSpec(memory_space=pltpu.VMEM)
HB = pl.BlockSpec(memory_space=pl.ANY)
SM = pl.BlockSpec(memory_space=pltpu.SMEM)
GRANT = pltpu.CompilerParams(vmem_limit_bytes=24 * 2**20)


def row_shifts(v):
    count = v.shape[0]
    row = lax.broadcasted_iota(jnp.int32, v.shape, 0) & 7
    before = jnp.where(row == 0, 0.0, pltpu.roll(v, 1, 0))
    after = jnp.where(row == 7, 0.0, pltpu.roll(v, count - 1, 0))
    return before, after


PIECES = (1024, 1024, 1024, 384)


def weight_copies(w_hbm, w_buf, sem, order):
    rows = w_hbm.shape[0] // 3
    copies = []
    for a in order:
        start = a * rows
        for size in PIECES:
            part = pl.ds(start, size)
            copy = pltpu.make_async_copy(w_hbm.at[part], w_buf.at[part], sem.at[len(copies)])
            copies.append((copy, a, start, start - a * rows, size))
            start += size
    return copies


def column_block(pieces, t):
    parts = [piece[t] for piece in pieces]
    return parts[0] if len(parts) == 1 else jnp.concatenate(parts, axis=0)


def write_block(out, refs, t):
    cols = out.shape[0]
    if len(refs) == 2:
        refs[0][t] = out[:3]
        refs[1][t] = out[cols - 3 :]
    else:
        edge = refs[1].shape[1]
        refs[0][t] = out
        refs[1][t] = out[:edge]
        refs[2][t] = out[cols - edge :]


def edge_scales(form, tile_ref, dtype):
    one, none = jnp.ones((), dtype), jnp.zeros((), dtype)
    low = jnp.where(tile_ref[0] == 0, none, one) if form == "even" else one
    high = jnp.where(tile_ref[0] == tile_ref[1] - 1, none, one)
    return low, high


def put_taps(taps, t_at, v, b, columns, ch, cut, backward):
    rows = 8
    block = columns * rows
    for c in range(3):
        start = (2 - c if backward else c) * rows
        piece = v[start : start + block]
        if cut is not None and c != 1:
            bad = (2 if start == 0 else 1) * rows
            piece = jnp.concatenate([piece[:bad], piece[bad : bad + rows] * cut, piece[bad + rows :]], axis=0)
        at = (3 * b + c) * ch
        taps[t_at * block : (t_at + 1) * block, at : at + ch] = piece.astype(BF16)


def fwd_kernel(form, count, *refs):
    tile_ref, *pieces = refs[: count + 1]
    gain_ref, w_hbm = refs[count + 1 : count + 3]
    *outs, taps, w_buf, sem = refs[count + 3 :]
    copies = weight_copies(w_hbm, w_buf, sem, range(3))
    for copy, *_ in copies:
        copy.start()
    frames, _, rows, ch = pieces[0].shape
    outer = sum(piece.shape[1] for piece in pieces)
    inner = outer - 2
    block = inner * rows
    gain = gain_ref[...].astype(F32)
    low, high = edge_scales(form, tile_ref, F32)
    taps[0 : 2 * block, :] = jnp.zeros((2 * block, 9 * ch), BF16)
    for t in range(frames):
        x = column_block(pieces, t).astype(F32)
        if form == "even":
            x = jnp.concatenate([x[:1] * low, x[1:-1], x[-1:] * high], axis=0)
        x = x.reshape(outer * rows, ch)
        inv = lax.rsqrt(jnp.mean(x * x, axis=-1, keepdims=True) + EPS)
        act = jax.nn.silu(x * inv * gain)
        before, after = row_shifts(act)
        for b, v in enumerate((before, act, after)):
            put_taps(taps, 2 + t, v, b, inner, ch, high if form == "odd" else None, False)
    acc = jnp.zeros((frames * block, ch), F32)
    for copy, a, start, at, size in copies:
        copy.wait()
        acc = acc + jnp.dot(
            taps[a * block : (a + frames) * block, at : at + size],
            w_buf[start : start + size, :],
            preferred_element_type=F32,
        )
    for t in range(frames):
        x = column_block(pieces, t)[1:-1].astype(F32)
        out = x + acc[t * block : (t + 1) * block].reshape(inner, rows, ch)
        if form == "wide":
            tile = tile_ref[0]
            col = lax.broadcasted_iota(jnp.int32, out.shape, 0)
            first = jnp.where(tile == 0, 1, 0)
            stop = jnp.where(tile == tile_ref[1] - 1, inner - 1, inner)
            outs[0][t] = jnp.where((col >= first) & (col < stop), out, 0.0).astype(BF16)
        else:
            write_block(out.astype(BF16), outs, t)


def run_fwd(form, out_cols, tile_info, pieces, gain, weight):
    frames, _, rows, ch = pieces[0].shape
    inner = sum(piece.shape[1] for piece in pieces) - 2
    return pl.pallas_call(
        functools.partial(fwd_kernel, form, len(pieces)),
        out_shape=[jax.ShapeDtypeStruct((frames, n, rows, ch), BF16) for n in out_cols],
        in_specs=[SM] + [VM] * (len(pieces) + 1) + [HB],
        out_specs=[VM] * len(out_cols),
        scratch_shapes=[
            pltpu.VMEM((6 * inner * rows, 9 * ch), BF16),
            pltpu.VMEM(weight.shape, BF16),
            pltpu.SemaphoreType.DMA((3 * len(PIECES),)),
        ],
        name=f"fwd_{form}",
        compiler_params=GRANT,
    )(tile_info, *pieces, gain, weight)


def bwd_kernel(form, n_x, n_g, *refs):
    tile_ref, *refs = refs
    xs, gs, (gain_ref, w_hbm, *rest) = refs[:n_x], refs[n_x : n_x + n_g], refs[n_x + n_g :]
    gf_ref, *outs, taps, w_buf, fac_ref, sem = rest
    copies = weight_copies(w_hbm, w_buf, sem, reversed(range(3)))
    for copy, *_ in copies:
        copy.start()
    frames, cols, rows, ch = gf_ref.shape
    block = cols * rows
    outer = cols + 2
    gain = gain_ref[...].astype(F32)
    low, high = edge_scales("odd" if form == "odd" else "even", tile_ref, F32)
    taps[4 * block : 6 * block, :] = jnp.zeros((2 * block, 9 * ch), BF16)

    def gradient(t):
        if form == "first":
            gc, lp, rp, from_l, from_r = gs
            mid = gc[t].astype(F32)
            left = from_l[t, :1].astype(F32) + lp[t, :1].astype(F32)
            right = from_r[t, 1:].astype(F32) + rp[t, 1:].astype(F32)
            return jnp.concatenate(
                [
                    left,
                    mid[:1] + from_l[t, 1:].astype(F32),
                    mid[1:-1],
                    mid[-1:] + from_r[t, :1].astype(F32),
                    right,
                ],
                axis=0,
            )
        return column_block(gs, t).astype(F32)

    def inputs(t):
        x = column_block(xs, t)
        return (x if n_x == 1 else x[1:-1]).astype(F32).reshape(block, ch)

    for t in range(frames):
        g = gradient(t)
        if form != "odd":
            g = jnp.concatenate([g[:1] * low, g[1:-1], g[-1:] * high], axis=0)
        g = g.reshape(outer * rows, ch)
        before, after = row_shifts(g)
        for b, v in enumerate((after, g, before)):
            put_taps(taps, t, v, b, cols, ch, high if form == "odd" else None, True)
    for t in range(frames):
        x = inputs(t)
        inv = lax.rsqrt(jnp.mean(x * x, axis=-1, keepdims=True) + EPS)
        u = x * inv * gain
        sig = jax.nn.sigmoid(u)
        fac_ref[t] = sig * (1.0 + u * (1.0 - sig)) * gain * inv
    acc = jnp.zeros((frames * block, ch), F32)
    for copy, a, start, at, size in copies:
        copy.wait()
        acc = acc + jnp.dot(
            taps[(2 - a) * block : (2 - a + frames) * block, at : at + size],
            w_buf[start : start + size, :],
            preferred_element_type=F32,
        )
    for t in range(frames):
        x = inputs(t)
        inv2 = 1.0 / (jnp.mean(x * x, axis=-1, keepdims=True) + EPS)
        y = acc[t * block : (t + 1) * block] * fac_ref[t]
        dx = y - x * (inv2 * jnp.mean(y * x, axis=-1, keepdims=True))
        out = gradient(t)[1:-1] + dx.reshape(cols, rows, ch)
        gf_ref[t] = out
        if outs:
            write_block(out.astype(BF16), outs, t)


def run_bwd(form, out_cols, tile_info, xs, gs, gain, weight_back):
    frames, _, rows, ch = xs[0].shape
    cols = xs[0].shape[1] if len(xs) == 1 else sum(x.shape[1] for x in xs) - 2
    outs = [jax.ShapeDtypeStruct((frames, cols, rows, ch), F32)]
    outs += [jax.ShapeDtypeStruct((frames, n, rows, ch), BF16) for n in out_cols]
    return pl.pallas_call(
        functools.partial(bwd_kernel, form, len(xs), len(gs)),
        out_shape=outs,
        in_specs=[SM] + [VM] * (len(xs) + len(gs) + 1) + [HB],
        out_specs=[VM] * len(outs),
        scratch_shapes=[
            pltpu.VMEM((6 * cols * rows, 9 * ch), BF16),
            pltpu.VMEM(weight_back.shape, BF16),
            pltpu.VMEM((frames, cols * rows, ch), F32),
            pltpu.SemaphoreType.DMA((3 * len(PIECES),)),
        ],
        name=f"bwd_{form}",
        compiler_params=GRANT,
    )(tile_info, *xs, *gs, gain, weight_back)


def first_kernel(order_ref, latent_ref, x_ref, l_ref, r_ref):
    for t in range(x_ref.shape[0]):
        x = latent_ref[order_ref[t]]
        x_ref[t] = x
        l_ref[t] = x[:1]
        r_ref[t] = x[x.shape[0] - 1 :]


def run_first(order, latent):
    frames, cols, rows, ch = latent.shape
    return pl.pallas_call(
        first_kernel,
        out_shape=[jax.ShapeDtypeStruct((frames, n, rows, ch), BF16) for n in (cols, 1, 1)],
        in_specs=[SM, VM],
        out_specs=[VM] * 3,
        name="first",
        compiler_params=GRANT,
    )(order, latent)


def unwritten(*shapes):
    return tuple(
        pl.pallas_call(
            lambda out_ref: None,
            out_shape=jax.ShapeDtypeStruct(shape, BF16),
            out_specs=HB,
            name="unwritten",
        )()
        for shape in shapes
    )


def up_kernel(x_ref, wa_ref, wb_ref, spread_ref, *rest):
    pre_ref, *feat_refs, held = rest
    frames, outer, rows, ch = x_ref.shape
    cols = outer - 2
    cu = wa_ref.shape[3]
    half = wa_ref.shape[0] * wa_ref.shape[2]
    block = outer * rows
    held[0 : 2 * block, :] = jnp.zeros((2 * block, 2 * half), BF16)
    for t in range(frames):
        held[(2 + t) * block : (3 + t) * block, :] = jnp.dot(
            x_ref[t].reshape(block, ch), spread_ref[...], preferred_element_type=F32
        ).astype(BF16)
    by_phase = [[], []]
    for c in range(3):
        cells = []
        for b in range(3):
            total = jnp.zeros((frames * block, cu), F32)
            for a in range(3):
                for part, w_ref in enumerate((wa_ref, wb_ref)):
                    total = total + jnp.dot(
                        held[a * block : (a + frames) * block, part * half : (part + 1) * half],
                        w_ref[:, 9 * a + 3 * b + c].reshape(half, cu),
                        preferred_element_type=F32,
                    )
            cells.append(total)
        before, _ = row_shifts(cells[0])
        _, after = row_shifts(cells[2])
        shape = (frames, outer, rows, cu)
        by_phase[0].append((before + cells[1] + cells[2]).reshape(shape))
        by_phase[1].append((cells[0] + cells[1] + after).reshape(shape))
    pres = []
    for p in range(2):
        left, mid, right = by_phase[p]
        pres.append(
            [
                left[:, 0:cols] + mid[:, 1 : cols + 1] + right[:, 1 : cols + 1],
                left[:, 1 : cols + 1] + mid[:, 1 : cols + 1] + right[:, 2 : cols + 2],
            ]
        )
    for t in range(frames):
        for w in range(cols):
            pair = [jnp.concatenate([pres[p][0][t, w], pres[p][1][t, w]], axis=1) for p in range(2)]
            lanes = slice(w * 2 * cu, (w + 1) * 2 * cu)
            for h in range(2):
                mine = slice(h * rows // 2, (h + 1) * rows // 2)
                piece = jnp.concatenate([pair[0][mine], pair[1][mine]], axis=0)
                pre_ref[2 * t + h, :, lanes] = piece
                feat_refs[2 * t + h][:, lanes] = jax.nn.silu(piece).astype(BF16)


def run_up(x, wa, wb, spread):
    frames, outer, rows, ch = x.shape
    chunk = (rows, 2 * (outer - 2) * wa.shape[3])
    return pl.pallas_call(
        up_kernel,
        out_shape=[
            jax.ShapeDtypeStruct((2 * frames, *chunk), F32),
            *(jax.ShapeDtypeStruct(chunk, BF16) for _ in range(2 * frames)),
        ],
        in_specs=[VM] * 4,
        out_specs=[VM] * (1 + 2 * frames),
        scratch_shapes=[pltpu.VMEM((6 * outer * rows, spread.shape[1]), BF16)],
        name="up",
        compiler_params=GRANT,
    )(x, wa, wb, spread)


def exact_dot(value, ones, dims):
    total = None
    for _ in range(3):
        piece = value.astype(BF16)
        value = value - piece.astype(F32)
        part = lax.dot_general(piece, ones, dims, preferred_element_type=F32)
        total = part if total is None else total + part
    return total


GROUP = 48


def group_masks(rows, groups):
    row = lax.broadcasted_iota(jnp.int32, (rows, groups * GROUP), 0)
    lane = lax.broadcasted_iota(jnp.int32, (rows, groups * GROUP), 1)
    wanted = (row % 8) * 2 + (row // 8) % 2
    return lane // GROUP == wanted


def fold_matrix(groups):
    lane = lax.broadcasted_iota(jnp.int32, (groups * GROUP, GROUP), 0)
    column = lax.broadcasted_iota(jnp.int32, (groups * GROUP, GROUP), 1)
    return (lane % GROUP == column).astype(F32).astype(BF16)


def logit_kernel(half_ref, z_ref, w_hbm, out_ref, table, w_buf, sem):
    outs, keep = w_buf.shape
    span = z_ref.shape[1]
    groups = keep // span
    copy = pltpu.make_async_copy(
        w_hbm.at[:, pl.ds(pl.multiple_of(half_ref[0] * keep, 128), keep)], w_buf, sem
    )
    copy.start()
    mask = group_masks(z_ref.shape[0], groups)
    fold = fold_matrix(groups)
    copy.wait()
    for r in range(groups // 2):
        true_row = 2 * (r % 4) + r // 4
        for e in range(2):
            at = (2 * r + e) * GROUP
            start = (2 * true_row + e) * span
            table[at : at + GROUP, :] = jnp.concatenate(
                [w_buf[:, start : start + span], jnp.zeros((GROUP - outs, span), BF16)], axis=0
            )
    pairs = lax.dot_general(
        z_ref[...], table[...], (((1,), (1,)), ((), ())), preferred_element_type=F32
    )
    pairs = jnp.where(mask, pairs, 0.0)
    patches = z_ref.shape[0] // groups
    summed = jnp.sum(pairs.reshape(patches, groups, groups * GROUP), axis=1)
    out_ref[...] = exact_dot(summed, fold, (((1,), (0,)), ((), ())))


def run_logit(half, z, weight, keep):
    outs = weight.shape[0]
    span = z.shape[1]
    groups = keep // span
    return pl.pallas_call(
        logit_kernel,
        out_shape=[
            jax.ShapeDtypeStruct((z.shape[0] // groups, GROUP), F32),
            jax.ShapeDtypeStruct((groups * GROUP, span), BF16),
        ],
        in_specs=[SM, VM, HB],
        out_specs=[VM, VM],
        scratch_shapes=[pltpu.VMEM((outs, keep), BF16), pltpu.SemaphoreType.DMA],
        name="logit",
        compiler_params=GRANT,
    )(half, z, weight)


def back_kernel(mine_ref, other_ref, coef_ref, table_ref, out_ref):
    groups = table_ref.shape[0] // GROUP
    patches = mine_ref.shape[0]
    squashed = jnp.tanh(mine_ref[...] + other_ref[...])
    grad = (coef_ref[...] * (1.0 - squashed * squashed)).astype(BF16)
    wide = lax.dot_general(
        grad, fold_matrix(groups), (((1,), (1,)), ((), ())), preferred_element_type=F32
    )
    wide = jnp.broadcast_to(wide[:, None, :], (patches, groups, groups * GROUP))
    wide = wide.reshape(patches * groups, groups * GROUP)
    wide = jnp.where(group_masks(patches * groups, groups), wide, 0.0).astype(BF16)
    out_ref[...] = jnp.dot(wide, table_ref[...], preferred_element_type=F32).astype(BF16)


def run_back(mine, other, coef, table):
    rows = mine.shape[0] * table.shape[0] // GROUP
    return pl.pallas_call(
        back_kernel,
        out_shape=jax.ShapeDtypeStruct((rows, table.shape[1]), BF16),
        in_specs=[VM] * 4,
        out_specs=VM,
        name="back",
        compiler_params=GRANT,
    )(mine, other, coef, table)


def sum_kernel(in_ref, out_ref):
    total = in_ref[0].astype(F32)
    for i in range(1, in_ref.shape[0]):
        total = total + in_ref[i].astype(F32)
    out_ref[...] = total.astype(BF16)


def run_sum(values):
    return pl.pallas_call(
        sum_kernel,
        out_shape=jax.ShapeDtypeStruct(values.shape[1:], BF16),
        in_specs=[VM],
        out_specs=VM,
        name="sum",
        compiler_params=GRANT,
    )(values)


def order_kernel(wa_ref, wb_ref, spread_ref, out_ref):
    half = wa_ref.shape[0] * wa_ref.shape[2]
    cu = wa_ref.shape[3]
    for tap in range(wa_ref.shape[1]):
        total = None
        for part, w_ref in enumerate((wa_ref, wb_ref)):
            turned = lax.dot_general(
                w_ref[:, tap].reshape(half, cu),
                spread_ref[:, part * half : (part + 1) * half],
                (((0,), (1,)), ((), ())),
                preferred_element_type=F32,
            )
            total = turned if total is None else total + turned
        out_ref[tap] = total.astype(BF16)


def run_order(wa, wb, spread):
    return pl.pallas_call(
        order_kernel,
        out_shape=jax.ShapeDtypeStruct((wa.shape[1], wa.shape[3], spread.shape[0]), BF16),
        in_specs=[VM] * 3,
        out_specs=VM,
        name="order",
        compiler_params=GRANT,
    )(wa, wb, spread)


def adj_kernel(pre_ref, w_ref, *rest):
    *grad_refs, gf_ref, l_ref, r_ref, held = rest
    frames, cols, rows, ch = gf_ref.shape
    outer = cols + 2
    cu = w_ref.shape[1]
    block = outer * rows
    held[:, frames * block :, :] = jnp.zeros((9, 2 * block, cu), BF16)
    zero = jnp.zeros((1, rows, cu), F32)
    for t in range(frames):
        chunks = []
        for h in range(2):
            pre = pre_ref[2 * t + h]
            sig = jax.nn.sigmoid(pre)
            grad = grad_refs[2 * t + h][...].astype(F32) * sig * (1.0 + pre * (1.0 - sig))
            chunks.append(grad.astype(BF16).astype(F32))
        fine = []
        for p in range(2):
            low = slice(p * rows // 2, (p + 1) * rows // 2)
            whole = jnp.concatenate([chunks[0][low], chunks[1][low]], axis=0)
            even, odd = (
                jnp.concatenate(
                    [whole[:, (2 * w + q) * cu : (2 * w + q + 1) * cu][None] for w in range(cols)], axis=0
                )
                for q in range(2)
            )
            own = jnp.concatenate([zero, even + odd, zero], axis=0)
            later = jnp.concatenate([even[:1], odd[:-1] + even[1:], odd[-1:], zero], axis=0)
            sooner = jnp.concatenate([zero, even[:1], odd[:-1] + even[1:], odd[-1:]], axis=0)
            fine.append([v.reshape(block, cu) for v in (later, own, sooner)])
        for c in range(3):
            top, low = fine[0][c], fine[1][c]
            _, top_after = row_shifts(top)
            low_before, _ = row_shifts(low)
            for b, v in enumerate((low + top_after, top + low, low_before + top)):
                held[3 * b + c, t * block : (t + 1) * block, :] = v.astype(BF16)
    out = jnp.zeros((frames * block, ch), F32)
    for a in range(3):
        for bc in range(9):
            out = out + jnp.dot(
                held[bc, (2 - a) * block : (2 - a + frames) * block, :],
                w_ref[9 * a + bc],
                preferred_element_type=F32,
            )
    out = out.reshape(frames, outer, rows, ch)
    gf_ref[...] = out[:, 1:-1]
    l_ref[...] = out[:, :2].astype(BF16)
    r_ref[...] = out[:, -2:].astype(BF16)


def run_adj(grads, pre, weight, frames, cols):
    rows = pre.shape[1]
    cu, ch = weight.shape[1:]
    return pl.pallas_call(
        adj_kernel,
        out_shape=[
            jax.ShapeDtypeStruct((frames, cols, rows, ch), F32),
            jax.ShapeDtypeStruct((frames, 2, rows, ch), BF16),
            jax.ShapeDtypeStruct((frames, 2, rows, ch), BF16),
        ],
        in_specs=[VM] * (2 + len(grads)),
        out_specs=[VM] * 3,
        scratch_shapes=[pltpu.VMEM((9, 6 * (cols + 2) * rows, cu), BF16)],
        name="adj",
        compiler_params=GRANT,
    )(pre, weight, *grads)


def on_device(latent, frame_order, section_weight, section_gain, up_weight, reward_weight, reward_coef):
    segs = lax.axis_size("segment")
    chips = lax.axis_size("chip")
    tiles = 2 * chips
    seg = lax.axis_index("segment")
    core = lax.axis_index("core")
    tile = 2 * lax.axis_index("chip") + core
    frames, rows, cols, ch = latent.shape
    cu = up_weight.shape[2]
    outs_dev = reward_coef.shape[0]
    last = segs - 1
    halves = segs // frames
    span = 2 * cols * cu
    keep = 2 * rows // halves * 2 * span
    barrier = lax.optimization_barrier
    tile_info = jnp.stack([tile, jnp.full_like(tile, tiles)])
    block = (frames, cols, rows, ch)
    side = (frames, 1, rows, ch)
    side2 = (frames, 2, rows, ch)

    def route(pairs_of_segments, shift):
        return [
            (source * tiles + t, target * tiles + t + shift)
            for source, target in pairs_of_segments
            for t in range(tiles)
            if 0 <= t + shift < tiles
        ]

    def send(value, source, target):
        return lax.ppermute(value, AXES, route([(source, target)], 0))

    def beside(value, shift):
        return lax.ppermute(value, AXES, route([(s, s) for s in range(segs)], shift))

    def hop_route(source, target, shift):
        step = target - source
        pairs = [(s, s + step) for s in range(source % 2, segs, 2) if 0 <= s + step < segs]
        return pairs, shift

    def hop(center, left, right, source, target):
        return tuple(
            lax.ppermute(value, AXES, route(*hop_route(source, target, shift)))
            for value, shift in ((center, 0), (right, 1), (left, -1))
        )

    def turn_round(pairs_of_segments, shift):
        return [
            (source * tiles + t, target * tiles + (t + shift) % tiles)
            for source, target in pairs_of_segments
            for t in range(tiles)
        ]

    def half_hop(first_three, last_three, source, target):
        to_left, to_right = (-1, 0) if source % 2 == 0 else (0, 1)
        left = lax.ppermute(last_three, AXES, turn_round(*hop_route(source, target, to_right)))
        right = lax.ppermute(first_three, AXES, turn_round(*hop_route(source, target, to_left)))
        return left, right

    def gather_up():
        own = up_weight.shape[1]
        source = jnp.pad(up_weight, ((0, 0), (0, PAD - own), (0, 0)))
        wa = lax.all_to_all(
            jnp.broadcast_to(source[None], (chips, *source.shape)), "chip", 0, 0, tiled=True
        )
        wb = lax.ppermute(wa, "core", [(0, 1), (1, 0)])
        channel = lax.broadcasted_iota(jnp.int32, (ch, tiles * PAD), 0)
        place = lax.broadcasted_iota(jnp.int32, (ch, tiles * PAD), 1)
        other, chip_of, within = place // (chips * PAD), place // PAD % chips, place % PAD
        origin = 2 * chip_of + jnp.where(other == 0, core, 1 - core)
        spread = ((within < own) & (channel == origin * own + within)).astype(BF16)
        return wa, wb, spread, run_order(wa, wb, spread)

    up_shape = (chips, 27, PAD, cu)

    def turn(weight):
        return weight[0].transpose(0, 2, 1).reshape(27 * ch, ch)

    def start():
        x, left, right = run_first(frame_order, latent.transpose(0, 2, 1, 3))
        return x, beside(right, 1), beside(left, -1)

    weight_fwd = section_weight[0].reshape(27 * ch, ch)
    gathered = lax.cond(
        seg == last,
        gather_up,
        lambda: unwritten(up_shape, up_shape, (ch, tiles * PAD), (27, cu, ch)),
    )
    turned = lax.cond(seg > 0, lambda: turn(section_weight), lambda: unwritten((27 * ch, ch))[0])
    state = lax.cond(
        seg == 0, start, lambda: tuple(jnp.zeros(s, BF16) for s in (block, side, side))
    )
    gathered, turned, state = barrier((gathered, turned, state))

    three = (frames, 3, rows, ch)
    ends, halves_kept = [state[0]], []
    for k in range(last):
        wide = k == last - 1
        made_shapes = (block, side2, side2) if wide else (three, three)

        def go(state, k=k, wide=wide, made_shapes=made_shapes):
            form = "odd" if k % 2 else "even"
            pieces = (state[1], state[0], state[2]) if k == 0 else state
            made = lax.cond(
                seg == k,
                lambda: tuple(
                    run_fwd(form, [m[1] for m in made_shapes], tile_info, pieces, section_gain, weight_fwd)
                ),
                lambda: unwritten(*made_shapes),
            )
            return hop(*made, k, k + 1) if wide else half_hop(*made, k, k + 1)

        def skip(state, k=k, wide=wide, made_shapes=made_shapes):
            if k == 0 or wide:
                return tuple(jnp.zeros(m, BF16) for m in made_shapes)
            return state

        state = lax.cond((seg == k) | (seg == k + 1), go, skip, state)
        if wide:
            ends.append(state[0])
        else:
            halves_kept.append(state)
        if k == 1:
            late, state = barrier((section_weight, state))
            turned_first = lax.cond(
                seg == 0, lambda late=late: turn(late), lambda: unwritten((27 * ch, ch))[0]
            )
            turned_first, state = barrier((turned_first, state))
    x_ends = ends[0] + ends[1]
    x_halves = tuple(functools.reduce(jnp.add, side_of) for side_of in zip(*halves_kept))

    chunk = (rows, span)

    def upsampled():
        center, left, right = state
        (deep,) = run_fwd(
            "wide", [cols + 2], tile_info, (left, center, right), section_gain, weight_fwd
        )
        return tuple(run_up(deep, *gathered[:3]))

    pre, *feats = lax.cond(
        seg == last,
        upsampled,
        lambda: (
            jnp.zeros((segs, *chunk), F32),
            *unwritten(*([chunk] * last)),
            jnp.zeros(chunk, BF16),
        ),
    )
    mine = functools.reduce(jnp.add, [send(feats[k], last, k) for k in range(last)], feats[last])
    coef = jnp.pad(reward_coef, (0, GROUP - outs_dev))[None]
    mine, x_ends, x_halves, coef = barrier((mine, x_ends, x_halves, coef))
    everyone = lax.cond(
        seg >= 0,
        lambda: lax.all_to_all(
            jnp.broadcast_to(mine[None], (tiles, *chunk)), TILE, 0, 0, tiled=True
        ),
        lambda: unwritten((tiles, *chunk))[0],
    )
    half = (seg % halves).reshape(1)
    partial, table = run_logit(half, everyone.reshape(tiles * rows, span), reward_weight.T, keep)
    group = [(s, s // halves * halves + (s + 1) % halves) for s in range(segs)]
    other = lax.ppermute(partial, "segment", group)
    shares = run_back(partial, other, coef, table)
    shares = lax.all_to_all(shares.reshape(tiles, *chunk), TILE, 0, 0, tiled=True)
    share = run_sum(shares)
    grads = [send(share, k, last) for k in range(last)] + [share]

    result = jnp.zeros(block, F32)

    def go_last(result):
        def live():
            deep, lp, rp = run_adj(grads, pre, gathered[3], frames, cols)
            from_r, from_l = beside(lp, -1), beside(rp, 1)
            gs = (deep, lp, rp, from_l, from_r)
            made = run_bwd("first", (cols, 1, 1), tile_info, (x_ends,), gs, section_gain, turned)
            return (*made[1:], made[0])

        *made, result = lax.cond(
            seg == last, live, lambda: (*unwritten(block, side, side), result)
        )
        center, left, right = hop(*made, last, last - 1)
        return left, center, right, result

    zeros = tuple(jnp.zeros(s, BF16) for s in (side, block, side))
    state = lax.cond(seg >= last - 1, go_last, lambda result: (*zeros, result), result)
    for k in range(last - 1, 0, -1):

        def go_back(state, k=k):
            *gs, result = state

            def live():
                form = "odd" if k % 2 else "even"
                made = run_bwd(form, (3, 3), tile_info, x_halves, gs, section_gain, turned)
                return (*made[1:], made[0])

            *made, result = lax.cond(seg == k, live, lambda: (*unwritten(three, three), result))
            return (*half_hop(*made, k, k - 1), result)

        def skip_back(state, k=k):
            if k == last - 1:
                return jnp.zeros(three, BF16), jnp.zeros(three, BF16), state[-1]
            return state

        state = lax.cond((seg == k) | (seg == k - 1), go_back, skip_back, state)
        if k % 2:
            def settle(result, k=k):
                left = lax.ppermute(
                    result[:, cols - 2 :], AXES, turn_round([(s, s) for s in range(segs)], 1)
                )
                return jnp.concatenate([left, result[:, : cols - 2]], axis=1)

            state = (*state[:-1], lax.cond(seg == k, settle, lambda result: result, state[-1]))
    *gs, result = state
    result = lax.cond(
        seg == 0,
        lambda: run_bwd("even", (), tile_info, (x_ends,), gs, section_gain, turned_first)[0],
        lambda: result,
    )
    return result.transpose(0, 2, 1, 3)[None]


def solution(mesh):
    shape = mesh.devices.shape
    fine = jax.sharding.Mesh(mesh.devices.reshape(shape[0], shape[1] // 2, 2), AXES)
    in_specs = (
        P(None, None, TILE, None),
        P(),
        P("segment", None, None, None),
        P("segment", None),
        P(None, TILE, None),
        P(None, TILE),
        P(TILE),
    )
    out_specs = P("segment", None, None, TILE, None)
    return jax.shard_map(
        on_device, mesh=fine, in_specs=in_specs, out_specs=out_specs, check_vma=False
    )
```

```python
import functools

import jax
import jax.numpy as jnp
from jax import lax
from jax.experimental import pallas as pl
from jax.experimental.pallas import tpu as pltpu
from jax.sharding import PartitionSpec as P

EPS = 1e-06
F32 = jnp.float32
BF16 = jnp.bfloat16
AXES = ("segment", "chip", "core")
TILE = ("chip", "core")
PAD = 16
VM = pl.BlockSpec(memory_space=pltpu.VMEM)
HB = pl.BlockSpec(memory_space=pl.ANY)
SM = pl.BlockSpec(memory_space=pltpu.SMEM)
GRANT = pltpu.CompilerParams(vmem_limit_bytes=24 * 2**20)


def row_shifts(v):
    count = v.shape[0]
    row = lax.broadcasted_iota(jnp.int32, v.shape, 0) & 7
    before = jnp.where(row == 0, 0.0, pltpu.roll(v, 1, 0))
    after = jnp.where(row == 7, 0.0, pltpu.roll(v, count - 1, 0))
    return before, after


PIECES = (1024, 1024, 1024, 384)


def weight_copy(w_hbm, w_buf, sem, a, piece):
    rows = w_hbm.shape[0] // 3
    part = pl.ds(pl.multiple_of(a * rows + sum(PIECES[:piece]), 128), PIECES[piece])
    return pltpu.make_async_copy(w_hbm.at[part], w_buf.at[part], sem.at[a, piece])


def start_weights(w_hbm, w_buf, sem, order):
    for a in order:
        for piece in range(len(PIECES)):
            weight_copy(w_hbm, w_buf, sem, a, piece).start()


def convolve(taps, w_hbm, w_buf, sem, acc_ref, backward):
    count = acc_ref.shape[0]
    block = count // 4
    rows = w_hbm.shape[0] // 3
    acc_ref[...] = jnp.zeros_like(acc_ref)

    @pl.loop(0, 3)
    def _(step):
        a = 2 - step if backward else step
        total = acc_ref[...]
        at = 0
        for piece, size in enumerate(PIECES):
            weight_copy(w_hbm, w_buf, sem, a, piece).wait()
            start = pl.multiple_of(a * rows + at, 128)
            total = total + jnp.dot(
                taps[pl.ds(pl.multiple_of(step * block, 16), count), at : at + size],
                w_buf[pl.ds(start, size), :],
                preferred_element_type=F32,
            )
            at += size
        acc_ref[...] = total


def column_block(pieces, t):
    parts = [piece[t] for piece in pieces]
    return parts[0] if len(parts) == 1 else jnp.concatenate(parts, axis=0)


def write_block(out, refs, t):
    cols = out.shape[0]
    if len(refs) == 2:
        refs[0][t] = out[:3]
        refs[1][t] = out[cols - 3 :]
    else:
        edge = refs[1].shape[1]
        refs[0][t] = out
        refs[1][t] = out[:edge]
        refs[2][t] = out[cols - edge :]


def edge_scales(form, tile_ref, dtype):
    one, none = jnp.ones((), dtype), jnp.zeros((), dtype)
    low = jnp.where(tile_ref[0] == 0, none, one) if form == "even" else one
    high = jnp.where(tile_ref[0] == tile_ref[1] - 1, none, one)
    return low, high


def put_taps(taps, t_at, v, b, columns, ch, cut, backward):
    rows = 8
    block = columns * rows
    for c in range(3):
        start = (2 - c if backward else c) * rows
        piece = v[start : start + block]
        if cut is not None and c != 1:
            bad = (2 if start == 0 else 1) * rows
            piece = jnp.concatenate([piece[:bad], piece[bad : bad + rows] * cut, piece[bad + rows :]], axis=0)
        at = (3 * b + c) * ch
        taps[t_at * block : (t_at + 1) * block, at : at + ch] = piece.astype(BF16)


def fwd_kernel(form, count, *refs):
    tile_ref, *pieces = refs[: count + 1]
    gain_ref, w_hbm = refs[count + 1 : count + 3]
    *outs, taps, w_buf, acc, sem = refs[count + 3 :]
    start_weights(w_hbm, w_buf, sem, range(3))
    frames, _, rows, ch = pieces[0].shape
    outer = sum(piece.shape[1] for piece in pieces)
    inner = outer - 2
    block = inner * rows
    gain = gain_ref[...].astype(F32)
    low, high = edge_scales(form, tile_ref, F32)
    taps[0 : 2 * block, :] = jnp.zeros((2 * block, 9 * ch), BF16)
    for t in range(frames):
        x = column_block(pieces, t).astype(F32)
        if form == "even":
            x = jnp.concatenate([x[:1] * low, x[1:-1], x[-1:] * high], axis=0)
        x = x.reshape(outer * rows, ch)
        inv = lax.rsqrt(jnp.mean(x * x, axis=-1, keepdims=True) + EPS)
        act = jax.nn.silu(x * inv * gain)
        before, after = row_shifts(act)
        for b, v in enumerate((before, act, after)):
            put_taps(taps, 2 + t, v, b, inner, ch, high if form == "odd" else None, False)
    convolve(taps, w_hbm, w_buf, sem, acc, False)
    for t in range(frames):
        x = column_block(pieces, t)[1:-1].astype(F32)
        out = x + acc[t * block : (t + 1) * block].reshape(inner, rows, ch)
        if form == "wide":
            tile = tile_ref[0]
            col = lax.broadcasted_iota(jnp.int32, out.shape, 0)
            first = jnp.where(tile == 0, 1, 0)
            stop = jnp.where(tile == tile_ref[1] - 1, inner - 1, inner)
            outs[0][t] = jnp.where((col >= first) & (col < stop), out, 0.0).astype(BF16)
        else:
            write_block(out.astype(BF16), outs, t)


def run_fwd(form, out_cols, tile_info, pieces, gain, weight):
    frames, _, rows, ch = pieces[0].shape
    inner = sum(piece.shape[1] for piece in pieces) - 2
    return pl.pallas_call(
        functools.partial(fwd_kernel, form, len(pieces)),
        out_shape=[jax.ShapeDtypeStruct((frames, n, rows, ch), BF16) for n in out_cols],
        in_specs=[SM] + [VM] * (len(pieces) + 1) + [HB],
        out_specs=[VM] * len(out_cols),
        scratch_shapes=[
            pltpu.VMEM((6 * inner * rows, 9 * ch), BF16),
            pltpu.VMEM(weight.shape, BF16),
            pltpu.VMEM((frames * inner * rows, ch), F32),
            pltpu.SemaphoreType.DMA((3, len(PIECES))),
        ],
        name=f"fwd_{form}",
        compiler_params=GRANT,
    )(tile_info, *pieces, gain, weight)


def bwd_kernel(form, n_x, n_g, *refs):
    tile_ref, *refs = refs
    xs, gs, (gain_ref, w_hbm, *rest) = refs[:n_x], refs[n_x : n_x + n_g], refs[n_x + n_g :]
    gf_ref, *outs, taps, w_buf, fac_ref, acc, sem = rest
    start_weights(w_hbm, w_buf, sem, reversed(range(3)))
    frames, cols, rows, ch = gf_ref.shape
    block = cols * rows
    outer = cols + 2
    gain = gain_ref[...].astype(F32)
    low, high = edge_scales("odd" if form == "odd" else "even", tile_ref, F32)
    taps[4 * block : 6 * block, :] = jnp.zeros((2 * block, 9 * ch), BF16)

    def gradient(t):
        if form == "first":
            gc, lp, rp, from_l, from_r = gs
            mid = gc[t].astype(F32)
            left = from_l[t, :1].astype(F32) + lp[t, :1].astype(F32)
            right = from_r[t, 1:].astype(F32) + rp[t, 1:].astype(F32)
            return jnp.concatenate(
                [
                    left,
                    mid[:1] + from_l[t, 1:].astype(F32),
                    mid[1:-1],
                    mid[-1:] + from_r[t, :1].astype(F32),
                    right,
                ],
                axis=0,
            )
        return column_block(gs, t).astype(F32)

    def inputs(t):
        x = column_block(xs, t)
        return (x if n_x == 1 else x[1:-1]).astype(F32).reshape(block, ch)

    for t in range(frames):
        g = gradient(t)
        if form != "odd":
            g = jnp.concatenate([g[:1] * low, g[1:-1], g[-1:] * high], axis=0)
        g = g.reshape(outer * rows, ch)
        before, after = row_shifts(g)
        for b, v in enumerate((after, g, before)):
            put_taps(taps, t, v, b, cols, ch, high if form == "odd" else None, True)
    for t in range(frames):
        x = inputs(t)
        inv = lax.rsqrt(jnp.mean(x * x, axis=-1, keepdims=True) + EPS)
        u = x * inv * gain
        sig = jax.nn.sigmoid(u)
        fac_ref[t] = sig * (1.0 + u * (1.0 - sig)) * gain * inv
    convolve(taps, w_hbm, w_buf, sem, acc, True)
    for t in range(frames):
        x = inputs(t)
        inv2 = 1.0 / (jnp.mean(x * x, axis=-1, keepdims=True) + EPS)
        y = acc[t * block : (t + 1) * block] * fac_ref[t]
        dx = y - x * (inv2 * jnp.mean(y * x, axis=-1, keepdims=True))
        out = gradient(t)[1:-1] + dx.reshape(cols, rows, ch)
        gf_ref[t] = out
        if outs:
            write_block(out.astype(BF16), outs, t)


def run_bwd(form, out_cols, tile_info, xs, gs, gain, weight_back):
    frames, _, rows, ch = xs[0].shape
    cols = xs[0].shape[1] if len(xs) == 1 else sum(x.shape[1] for x in xs) - 2
    outs = [jax.ShapeDtypeStruct((frames, cols, rows, ch), F32)]
    outs += [jax.ShapeDtypeStruct((frames, n, rows, ch), BF16) for n in out_cols]
    return pl.pallas_call(
        functools.partial(bwd_kernel, form, len(xs), len(gs)),
        out_shape=outs,
        in_specs=[SM] + [VM] * (len(xs) + len(gs) + 1) + [HB],
        out_specs=[VM] * len(outs),
        scratch_shapes=[
            pltpu.VMEM((6 * cols * rows, 9 * ch), BF16),
            pltpu.VMEM(weight_back.shape, BF16),
            pltpu.VMEM((frames, cols * rows, ch), F32),
            pltpu.VMEM((frames * cols * rows, ch), F32),
            pltpu.SemaphoreType.DMA((3, len(PIECES))),
        ],
        name=f"bwd_{form}",
        compiler_params=GRANT,
    )(tile_info, *xs, *gs, gain, weight_back)


def first_kernel(order_ref, latent_ref, x_ref, l_ref, r_ref):
    for t in range(x_ref.shape[0]):
        x = latent_ref[order_ref[t]]
        x_ref[t] = x
        l_ref[t] = x[:1]
        r_ref[t] = x[x.shape[0] - 1 :]


def run_first(order, latent):
    frames, cols, rows, ch = latent.shape
    return pl.pallas_call(
        first_kernel,
        out_shape=[jax.ShapeDtypeStruct((frames, n, rows, ch), BF16) for n in (cols, 1, 1)],
        in_specs=[SM, VM],
        out_specs=[VM] * 3,
        name="first",
        compiler_params=GRANT,
    )(order, latent)


def unwritten(*shapes, dtype=BF16):
    return tuple(
        pl.pallas_call(
            lambda out_ref: None,
            out_shape=jax.ShapeDtypeStruct(shape, dtype),
            out_specs=HB,
            name="unwritten",
        )()
        for shape in shapes
    )


def up_kernel(x_ref, wa_ref, wb_ref, spread_ref, *rest):
    pre_ref, *feat_refs, held = rest
    frames, outer, rows, ch = x_ref.shape
    cols = outer - 2
    cu = wa_ref.shape[3]
    half = wa_ref.shape[0] * wa_ref.shape[2]
    block = outer * rows
    held[0 : 2 * block, :] = jnp.zeros((2 * block, 2 * half), BF16)
    for t in range(frames):
        held[(2 + t) * block : (3 + t) * block, :] = jnp.dot(
            x_ref[t].reshape(block, ch), spread_ref[...], preferred_element_type=F32
        ).astype(BF16)
    by_phase = [[], []]
    for c in range(3):
        cells = []
        for b in range(3):
            total = jnp.zeros((frames * block, cu), F32)
            for a in range(3):
                for part, w_ref in enumerate((wa_ref, wb_ref)):
                    total = total + jnp.dot(
                        held[a * block : (a + frames) * block, part * half : (part + 1) * half],
                        w_ref[:, 9 * a + 3 * b + c].reshape(half, cu),
                        preferred_element_type=F32,
                    )
            cells.append(total)
        before, _ = row_shifts(cells[0])
        _, after = row_shifts(cells[2])
        shape = (frames, outer, rows, cu)
        by_phase[0].append((before + cells[1] + cells[2]).reshape(shape))
        by_phase[1].append((cells[0] + cells[1] + after).reshape(shape))
    pres = []
    for p in range(2):
        left, mid, right = by_phase[p]
        pres.append(
            [
                left[:, 0:cols] + mid[:, 1 : cols + 1] + right[:, 1 : cols + 1],
                left[:, 1 : cols + 1] + mid[:, 1 : cols + 1] + right[:, 2 : cols + 2],
            ]
        )
    for t in range(frames):
        for w in range(cols):
            pair = [jnp.concatenate([pres[p][0][t, w], pres[p][1][t, w]], axis=1) for p in range(2)]
            lanes = slice(w * 2 * cu, (w + 1) * 2 * cu)
            for h in range(2):
                mine = slice(h * rows // 2, (h + 1) * rows // 2)
                piece = jnp.concatenate([pair[0][mine], pair[1][mine]], axis=0)
                pre_ref[2 * t + h, :, lanes] = piece
                feat_refs[2 * t + h][:, lanes] = jax.nn.silu(piece).astype(BF16)


def run_up(x, wa, wb, spread):
    frames, outer, rows, ch = x.shape
    chunk = (rows, 2 * (outer - 2) * wa.shape[3])
    return pl.pallas_call(
        up_kernel,
        out_shape=[
            jax.ShapeDtypeStruct((2 * frames, *chunk), F32),
            *(jax.ShapeDtypeStruct(chunk, BF16) for _ in range(2 * frames)),
        ],
        in_specs=[VM] * 4,
        out_specs=[VM] * (1 + 2 * frames),
        scratch_shapes=[pltpu.VMEM((6 * outer * rows, spread.shape[1]), BF16)],
        name="up",
        compiler_params=GRANT,
    )(x, wa, wb, spread)


def exact_dot(value, ones, dims):
    total = None
    for _ in range(3):
        piece = value.astype(BF16)
        value = value - piece.astype(F32)
        part = lax.dot_general(piece, ones, dims, preferred_element_type=F32)
        total = part if total is None else total + part
    return total


GROUP = 48


def group_masks(rows, groups):
    row = lax.broadcasted_iota(jnp.int32, (rows, groups * GROUP), 0)
    lane = lax.broadcasted_iota(jnp.int32, (rows, groups * GROUP), 1)
    wanted = (row % 8) * 2 + (row // 8) % 2
    return lane // GROUP == wanted


def fold_matrix(groups):
    lane = lax.broadcasted_iota(jnp.int32, (groups * GROUP, GROUP), 0)
    column = lax.broadcasted_iota(jnp.int32, (groups * GROUP, GROUP), 1)
    return (lane % GROUP == column).astype(F32).astype(BF16)


def logit_kernel(half_ref, z_ref, w_hbm, out_ref, table, w_buf, sem):
    outs, keep = w_buf.shape
    span = z_ref.shape[1]
    groups = keep // span
    copy = pltpu.make_async_copy(
        w_hbm.at[:, pl.ds(pl.multiple_of(half_ref[0] * keep, 128), keep)], w_buf, sem
    )
    copy.start()
    mask = group_masks(z_ref.shape[0], groups)
    fold = fold_matrix(groups)
    copy.wait()
    for r in range(groups // 2):
        true_row = 2 * (r % 4) + r // 4
        for e in range(2):
            at = (2 * r + e) * GROUP
            start = (2 * true_row + e) * span
            table[at : at + GROUP, :] = jnp.concatenate(
                [w_buf[:, start : start + span], jnp.zeros((GROUP - outs, span), BF16)], axis=0
            )
    pairs = lax.dot_general(
        z_ref[...], table[...], (((1,), (1,)), ((), ())), preferred_element_type=F32
    )
    pairs = jnp.where(mask, pairs, 0.0)
    patches = z_ref.shape[0] // groups
    summed = jnp.sum(pairs.reshape(patches, groups, groups * GROUP), axis=1)
    out_ref[...] = exact_dot(summed, fold, (((1,), (0,)), ((), ())))


def run_logit(half, z, weight, keep):
    outs = weight.shape[0]
    span = z.shape[1]
    groups = keep // span
    return pl.pallas_call(
        logit_kernel,
        out_shape=[
            jax.ShapeDtypeStruct((z.shape[0] // groups, GROUP), F32),
            jax.ShapeDtypeStruct((groups * GROUP, span), BF16),
        ],
        in_specs=[SM, VM, HB],
        out_specs=[VM, VM],
        scratch_shapes=[pltpu.VMEM((outs, keep), BF16), pltpu.SemaphoreType.DMA],
        name="logit",
        compiler_params=GRANT,
    )(half, z, weight)


def back_kernel(mine_ref, other_ref, coef_ref, table_ref, out_ref):
    groups = table_ref.shape[0] // GROUP
    patches = mine_ref.shape[0]
    squashed = jnp.tanh(mine_ref[...] + other_ref[...])
    grad = (coef_ref[...] * (1.0 - squashed * squashed)).astype(BF16)
    wide = lax.dot_general(
        grad, fold_matrix(groups), (((1,), (1,)), ((), ())), preferred_element_type=F32
    )
    wide = jnp.broadcast_to(wide[:, None, :], (patches, groups, groups * GROUP))
    wide = wide.reshape(patches * groups, groups * GROUP)
    wide = jnp.where(group_masks(patches * groups, groups), wide, 0.0).astype(BF16)
    out_ref[...] = jnp.dot(wide, table_ref[...], preferred_element_type=F32).astype(BF16)


def run_back(mine, other, coef, table):
    rows = mine.shape[0] * table.shape[0] // GROUP
    return pl.pallas_call(
        back_kernel,
        out_shape=jax.ShapeDtypeStruct((rows, table.shape[1]), BF16),
        in_specs=[VM] * 4,
        out_specs=VM,
        name="back",
        compiler_params=GRANT,
    )(mine, other, coef, table)


def sum_kernel(in_ref, out_ref):
    total = in_ref[0].astype(F32)
    for i in range(1, in_ref.shape[0]):
        total = total + in_ref[i].astype(F32)
    out_ref[...] = total.astype(BF16)


def run_sum(values):
    return pl.pallas_call(
        sum_kernel,
        out_shape=jax.ShapeDtypeStruct(values.shape[1:], BF16),
        in_specs=[VM],
        out_specs=VM,
        name="sum",
        compiler_params=GRANT,
    )(values)


def order_kernel(wa_ref, wb_ref, spread_ref, out_ref):
    half = wa_ref.shape[0] * wa_ref.shape[2]
    cu = wa_ref.shape[3]
    for tap in range(wa_ref.shape[1]):
        total = None
        for part, w_ref in enumerate((wa_ref, wb_ref)):
            turned = lax.dot_general(
                w_ref[:, tap].reshape(half, cu),
                spread_ref[:, part * half : (part + 1) * half],
                (((0,), (1,)), ((), ())),
                preferred_element_type=F32,
            )
            total = turned if total is None else total + turned
        out_ref[tap] = total.astype(BF16)


def run_order(wa, wb, spread):
    return pl.pallas_call(
        order_kernel,
        out_shape=jax.ShapeDtypeStruct((wa.shape[1], wa.shape[3], spread.shape[0]), BF16),
        in_specs=[VM] * 3,
        out_specs=VM,
        name="order",
        compiler_params=GRANT,
    )(wa, wb, spread)


def adj_kernel(pre_ref, w_ref, *rest):
    *grad_refs, gf_ref, l_ref, r_ref, held = rest
    frames, cols, rows, ch = gf_ref.shape
    outer = cols + 2
    cu = w_ref.shape[1]
    block = outer * rows
    held[:, frames * block :, :] = jnp.zeros((9, 2 * block, cu), BF16)
    zero = jnp.zeros((1, rows, cu), F32)
    for t in range(frames):
        chunks = []
        for h in range(2):
            pre = pre_ref[2 * t + h]
            sig = jax.nn.sigmoid(pre)
            grad = grad_refs[2 * t + h][...].astype(F32) * sig * (1.0 + pre * (1.0 - sig))
            chunks.append(grad.astype(BF16).astype(F32))
        fine = []
        for p in range(2):
            low = slice(p * rows // 2, (p + 1) * rows // 2)
            whole = jnp.concatenate([chunks[0][low], chunks[1][low]], axis=0)
            even, odd = (
                jnp.concatenate(
                    [whole[:, (2 * w + q) * cu : (2 * w + q + 1) * cu][None] for w in range(cols)], axis=0
                )
                for q in range(2)
            )
            own = jnp.concatenate([zero, even + odd, zero], axis=0)
            later = jnp.concatenate([even[:1], odd[:-1] + even[1:], odd[-1:], zero], axis=0)
            sooner = jnp.concatenate([zero, even[:1], odd[:-1] + even[1:], odd[-1:]], axis=0)
            fine.append([v.reshape(block, cu) for v in (later, own, sooner)])
        for c in range(3):
            top, low = fine[0][c], fine[1][c]
            _, top_after = row_shifts(top)
            low_before, _ = row_shifts(low)
            for b, v in enumerate((low + top_after, top + low, low_before + top)):
                held[3 * b + c, t * block : (t + 1) * block, :] = v.astype(BF16)
    out = jnp.zeros((frames * block, ch), F32)
    for a in range(3):
        for bc in range(9):
            out = out + jnp.dot(
                held[bc, (2 - a) * block : (2 - a + frames) * block, :],
                w_ref[9 * a + bc],
                preferred_element_type=F32,
            )
    out = out.reshape(frames, outer, rows, ch)
    gf_ref[...] = out[:, 1:-1]
    l_ref[...] = out[:, :2].astype(BF16)
    r_ref[...] = out[:, -2:].astype(BF16)


def run_adj(grads, pre, weight, frames, cols):
    rows = pre.shape[1]
    cu, ch = weight.shape[1:]
    return pl.pallas_call(
        adj_kernel,
        out_shape=[
            jax.ShapeDtypeStruct((frames, cols, rows, ch), F32),
            jax.ShapeDtypeStruct((frames, 2, rows, ch), BF16),
            jax.ShapeDtypeStruct((frames, 2, rows, ch), BF16),
        ],
        in_specs=[VM] * (2 + len(grads)),
        out_specs=[VM] * 3,
        scratch_shapes=[pltpu.VMEM((9, 6 * (cols + 2) * rows, cu), BF16)],
        name="adj",
        compiler_params=GRANT,
    )(pre, weight, *grads)


def on_device(latent, frame_order, section_weight, section_gain, up_weight, reward_weight, reward_coef):
    segs = lax.axis_size("segment")
    chips = lax.axis_size("chip")
    tiles = 2 * chips
    seg = lax.axis_index("segment")
    core = lax.axis_index("core")
    tile = 2 * lax.axis_index("chip") + core
    frames, rows, cols, ch = latent.shape
    cu = up_weight.shape[2]
    outs_dev = reward_coef.shape[0]
    last = segs - 1
    halves = segs // frames
    span = 2 * cols * cu
    keep = 2 * rows // halves * 2 * span
    barrier = lax.optimization_barrier
    tile_info = jnp.stack([tile, jnp.full_like(tile, tiles)])
    block = (frames, cols, rows, ch)
    side = (frames, 1, rows, ch)
    side2 = (frames, 2, rows, ch)

    def route(pairs_of_segments, shift):
        return [
            (source * tiles + t, target * tiles + t + shift)
            for source, target in pairs_of_segments
            for t in range(tiles)
            if 0 <= t + shift < tiles
        ]

    def send(value, source, target):
        return lax.ppermute(value, AXES, route([(source, target)], 0))

    def beside(value, shift):
        return lax.ppermute(value, AXES, route([(s, s) for s in range(segs)], shift))

    def hop_route(source, target, shift):
        step = target - source
        pairs = [(s, s + step) for s in range(source % 2, segs, 2) if 0 <= s + step < segs]
        return pairs, shift

    def hop(center, left, right, source, target):
        center, left, right = (
            lax.ppermute(value, AXES, route(*hop_route(source, target, shift)))
            for value, shift in ((center, 0), (right, 1), (left, -1))
        )
        return left, center, right

    def turn_round(pairs_of_segments, shift):
        return [
            (source * tiles + t, target * tiles + (t + shift) % tiles)
            for source, target in pairs_of_segments
            for t in range(tiles)
        ]

    def half_hop(first_three, last_three, source, target):
        to_left, to_right = (-1, 0) if source % 2 == 0 else (0, 1)
        left = lax.ppermute(last_three, AXES, turn_round(*hop_route(source, target, to_right)))
        right = lax.ppermute(first_three, AXES, turn_round(*hop_route(source, target, to_left)))
        return left, right

    def gather_up():
        own = up_weight.shape[1]
        source = jnp.pad(up_weight, ((0, 0), (0, PAD - own), (0, 0)))
        wa = lax.all_to_all(
            jnp.broadcast_to(source[None], (chips, *source.shape)), "chip", 0, 0, tiled=True
        )
        wb = lax.ppermute(wa, "core", [(0, 1), (1, 0)])
        channel = lax.broadcasted_iota(jnp.int32, (ch, tiles * PAD), 0)
        place = lax.broadcasted_iota(jnp.int32, (ch, tiles * PAD), 1)
        other, chip_of, within = place // (chips * PAD), place // PAD % chips, place % PAD
        origin = 2 * chip_of + jnp.where(other == 0, core, 1 - core)
        spread = ((within < own) & (channel == origin * own + within)).astype(BF16)
        return wa, wb, spread, run_order(wa, wb, spread)

    up_shape = (chips, 27, PAD, cu)

    def turn(weight):
        return weight[0].transpose(0, 2, 1).reshape(27 * ch, ch)

    def start():
        x, left, right = run_first(frame_order, latent.transpose(0, 2, 1, 3))
        return beside(right, 1), x, beside(left, -1)

    weight_fwd = section_weight[0].reshape(27 * ch, ch)
    gathered = lax.cond(
        seg == last,
        gather_up,
        lambda: unwritten(up_shape, up_shape, (ch, tiles * PAD), (27, cu, ch)),
    )
    turned = lax.cond(seg > 1, lambda: turn(section_weight), lambda: unwritten((27 * ch, ch))[0])
    state = lax.cond(seg == 0, start, lambda: unwritten(side, block, side))
    gathered, turned, state = barrier((gathered, turned, state))

    three = (frames, 3, rows, ch)
    taken = [state]
    for k in range(last):
        wide = k == last - 1
        made_shapes = (block, side2, side2) if wide else (three, three)

        def go(state=state, k=k, wide=wide, made_shapes=made_shapes):
            form = "odd" if k % 2 else "even"
            made = lax.cond(
                seg == k,
                lambda: tuple(
                    run_fwd(form, [m[1] for m in made_shapes], tile_info, state, section_gain, weight_fwd)
                ),
                lambda: unwritten(*made_shapes),
            )
            return hop(*made, k, k + 1) if wide else half_hop(*made, k, k + 1)

        given = (side2, block, side2) if wide else (three, three)
        state = lax.cond(
            (seg == k) | (seg == k + 1), go, lambda given=given: unwritten(*given)
        )
        taken.append(state)
        if k == 1:
            late, state = barrier((section_weight, state))
            turned_late = lax.cond(
                seg <= 1, lambda late=late: turn(late), lambda: unwritten((27 * ch, ch))[0]
            )
            turned_late, state = barrier((turned_late, state))
            taken[-1] = state

    chunk = (rows, span)

    def upsampled():
        (deep,) = run_fwd("wide", [cols + 2], tile_info, state, section_gain, weight_fwd)
        return tuple(run_up(deep, *gathered[:3]))

    pre, *feats = lax.cond(
        seg == last,
        upsampled,
        lambda: (
            unwritten((segs, *chunk), dtype=F32)[0],
            *unwritten(*([chunk] * last)),
            jnp.zeros(chunk, BF16),
        ),
    )
    mine = functools.reduce(jnp.add, [send(feats[k], last, k) for k in range(last)], feats[last])
    coef = jnp.pad(reward_coef, (0, GROUP - outs_dev))[None]
    mine, coef = barrier((mine, coef))
    everyone = lax.cond(
        seg >= 0,
        lambda: lax.all_to_all(
            jnp.broadcast_to(mine[None], (tiles, *chunk)), TILE, 0, 0, tiled=True
        ),
        lambda: unwritten((tiles, *chunk))[0],
    )
    half = (seg % halves).reshape(1)
    partial, table = run_logit(half, everyone.reshape(tiles * rows, span), reward_weight.T, keep)
    group = [(s, s // halves * halves + (s + 1) % halves) for s in range(segs)]
    other = lax.ppermute(partial, "segment", group)
    shares = run_back(partial, other, coef, table)
    shares = lax.all_to_all(shares.reshape(tiles, *chunk), TILE, 0, 0, tiled=True)
    share = run_sum(shares)
    grads = [send(share, k, last) for k in range(last)] + [share]

    results = {}
    for k in range(last, 0, -1):

        def go_back(state=state, k=k):
            def live():
                if k == last:
                    deep, lp, rp = run_adj(grads, pre, gathered[3], frames, cols)
                    from_r, from_l = beside(lp, -1), beside(rp, 1)
                    gs = (deep, lp, rp, from_l, from_r)
                    made = run_bwd(
                        "first", (cols, 1, 1), tile_info, taken[k][1:2], gs, section_gain, turned
                    )
                else:
                    form = "odd" if k % 2 else "even"
                    weight = turned if k > 1 else turned_late
                    made = run_bwd(form, (3, 3), tile_info, taken[k], state, section_gain, weight)
                return (*made[1:], made[0])

            shapes = (block, side, side) if k == last else (three, three)
            *made, result = lax.cond(
                seg == k,
                live,
                lambda: (*unwritten(*shapes), *unwritten(block, dtype=F32)),
            )
            passed = hop(*made, k, k - 1) if k == last else half_hop(*made, k, k - 1)
            return passed, result

        given = (side, block, side) if k == last else (three, three)
        state, results[k] = lax.cond(
            (seg == k) | (seg == k - 1),
            go_back,
            lambda given=given: (unwritten(*given), unwritten(block, dtype=F32)[0]),
        )

    def finish(k):
        if k == 0:
            result = run_bwd(
                "even", (), tile_info, taken[0][1:2], state, section_gain, turned_late
            )[0]
        else:
            result = results[k]
            if k != last and k % 2:
                moved = turn_round([(s, s) for s in range(segs)], 1)
                left = lax.ppermute(result[:, cols - 2 :], AXES, moved)
                result = jnp.concatenate([left, result[:, : cols - 2]], axis=1)
        return result.transpose(0, 2, 1, 3)

    return lax.switch(seg, [functools.partial(finish, k) for k in range(segs)])[None]


def solution(mesh):
    shape = mesh.devices.shape
    fine = jax.sharding.Mesh(mesh.devices.reshape(shape[0], shape[1] // 2, 2), AXES)
    in_specs = (
        P(None, None, TILE, None),
        P(),
        P("segment", None, None, None),
        P("segment", None),
        P(None, TILE, None),
        P(None, TILE),
        P(TILE),
    )
    out_specs = P("segment", None, None, TILE, None)
    return jax.shard_map(
        on_device, mesh=fine, in_specs=in_specs, out_specs=out_specs, check_vma=False
    )
```

```python
import functools

import jax
import jax.numpy as jnp
from jax import lax
from jax.experimental import pallas as pl
from jax.experimental.pallas import tpu as pltpu
from jax.sharding import PartitionSpec as P

EPS = 1e-06
F32 = jnp.float32
BF16 = jnp.bfloat16
AXES = ("segment", "chip", "core")
TILE = ("chip", "core")
PAD = 16
VM = pl.BlockSpec(memory_space=pltpu.VMEM)
HB = pl.BlockSpec(memory_space=pl.ANY)
SM = pl.BlockSpec(memory_space=pltpu.SMEM)
GRANT = pltpu.CompilerParams(vmem_limit_bytes=24 * 2**20)


def row_shifts(v):
    count = v.shape[0]
    row = lax.broadcasted_iota(jnp.int32, v.shape, 0) & 7
    before = jnp.where(row == 0, 0.0, pltpu.roll(v, 1, 0))
    after = jnp.where(row == 7, 0.0, pltpu.roll(v, count - 1, 0))
    return before, after


PIECES = 6


def weight_copy(w_hbm, w_buf, sem, piece):
    rows = w_hbm.shape[0] // PIECES
    part = pl.ds(pl.multiple_of(piece * rows, 64), rows)
    return pltpu.make_async_copy(w_hbm.at[part], w_buf.at[part], sem.at[piece])


def start_weights(w_hbm, w_buf, sem, backward):
    per = PIECES // 3
    for step in range(PIECES):
        a = 2 - step // per if backward else step // per
        weight_copy(w_hbm, w_buf, sem, a * per + step % per).start()


def convolve(taps, w_hbm, w_buf, sem, acc_ref, backward):
    count = acc_ref.shape[0]
    block = count // 4
    per = PIECES // 3
    rows = w_hbm.shape[0] // PIECES
    acc_ref[...] = jnp.zeros_like(acc_ref)

    @pl.loop(0, 3)
    def _(step):
        a = 2 - step if backward else step
        for part in range(per):
            piece = a * per + part
            weight_copy(w_hbm, w_buf, sem, piece).wait()
            acc_ref[...] += jnp.dot(
                taps[pl.ds(pl.multiple_of(step * block, 16), count), part * rows : (part + 1) * rows],
                w_buf[pl.ds(pl.multiple_of(piece * rows, 64), rows), :],
                preferred_element_type=F32,
            )


def column_block(pieces, t):
    parts = [piece[t] for piece in pieces]
    return parts[0] if len(parts) == 1 else jnp.concatenate(parts, axis=0)


def write_block(out, refs, t):
    cols = out.shape[0]
    if len(refs) == 2:
        refs[0][t] = out[:3]
        refs[1][t] = out[cols - 3 :]
    else:
        edge = refs[1].shape[1]
        refs[0][t] = out
        refs[1][t] = out[:edge]
        refs[2][t] = out[cols - edge :]


def edge_scales(form, tile_ref, dtype):
    one, none = jnp.ones((), dtype), jnp.zeros((), dtype)
    low = jnp.where(tile_ref[0] == 0, none, one) if form == "even" else one
    high = jnp.where(tile_ref[0] == tile_ref[1] - 1, none, one)
    return low, high


def put_taps(taps, t_at, v, b, columns, ch, cut, backward):
    rows = 8
    block = columns * rows
    for c in range(3):
        start = (2 - c if backward else c) * rows
        piece = v[start : start + block]
        if cut is not None and c != 1:
            bad = (2 if start == 0 else 1) * rows
            piece = jnp.concatenate([piece[:bad], piece[bad : bad + rows] * cut, piece[bad + rows :]], axis=0)
        at = (3 * b + c) * ch
        taps[pl.ds(pl.multiple_of(t_at * block, 16), block), at : at + ch] = piece.astype(BF16)


def fwd_kernel(form, count, *refs):
    tile_ref, *pieces = refs[: count + 1]
    gain_ref, w_hbm = refs[count + 1 : count + 3]
    *outs, taps, w_buf, acc, sem = refs[count + 3 :]
    start_weights(w_hbm, w_buf, sem, False)
    frames, _, rows, ch = pieces[0].shape
    outer = sum(piece.shape[1] for piece in pieces)
    inner = outer - 2
    block = inner * rows
    gain = gain_ref[...].astype(F32)
    low, high = edge_scales(form, tile_ref, F32)
    taps[0 : 2 * block, :] = jnp.zeros((2 * block, 9 * ch), BF16)
    @pl.loop(0, frames)
    def _(t):
        x = column_block(pieces, t).astype(F32)
        if form == "even":
            x = jnp.concatenate([x[:1] * low, x[1:-1], x[-1:] * high], axis=0)
        x = x.reshape(outer * rows, ch)
        inv = lax.rsqrt(jnp.mean(x * x, axis=-1, keepdims=True) + EPS)
        act = jax.nn.silu(x * inv * gain)
        before, after = row_shifts(act)
        for b, v in enumerate((before, act, after)):
            put_taps(taps, 2 + t, v, b, inner, ch, high if form == "odd" else None, False)
    convolve(taps, w_hbm, w_buf, sem, acc, False)
    @pl.loop(0, frames)
    def _(t):
        x = column_block(pieces, t)[1:-1].astype(F32)
        out = x + acc[pl.ds(pl.multiple_of(t * block, 8), block)].reshape(inner, rows, ch)
        if form == "wide":
            tile = tile_ref[0]
            col = lax.broadcasted_iota(jnp.int32, out.shape, 0)
            first = jnp.where(tile == 0, 1, 0)
            stop = jnp.where(tile == tile_ref[1] - 1, inner - 1, inner)
            outs[0][t] = jnp.where((col >= first) & (col < stop), out, 0.0).astype(BF16)
        else:
            write_block(out.astype(BF16), outs, t)


def run_fwd(form, out_cols, tile_info, pieces, gain, weight):
    frames, _, rows, ch = pieces[0].shape
    inner = sum(piece.shape[1] for piece in pieces) - 2
    return pl.pallas_call(
        functools.partial(fwd_kernel, form, len(pieces)),
        out_shape=[jax.ShapeDtypeStruct((frames, n, rows, ch), BF16) for n in out_cols],
        in_specs=[SM] + [VM] * (len(pieces) + 1) + [HB],
        out_specs=[VM] * len(out_cols),
        scratch_shapes=[
            pltpu.VMEM((6 * inner * rows, 9 * ch), BF16),
            pltpu.VMEM(weight.shape, BF16),
            pltpu.VMEM((frames * inner * rows, ch), F32),
            pltpu.SemaphoreType.DMA((PIECES,)),
        ],
        name=f"fwd_{form}",
        compiler_params=GRANT,
    )(tile_info, *pieces, gain, weight)


def bwd_kernel(form, n_x, n_g, *refs):
    tile_ref, *refs = refs
    xs, gs, (gain_ref, w_hbm, *rest) = refs[:n_x], refs[n_x : n_x + n_g], refs[n_x + n_g :]
    gf_ref, *outs, taps, w_buf, fac_ref, acc, sem = rest
    start_weights(w_hbm, w_buf, sem, True)
    frames, cols, rows, ch = gf_ref.shape
    block = cols * rows
    outer = cols + 2
    gain = gain_ref[...].astype(F32)
    low, high = edge_scales("odd" if form == "odd" else "even", tile_ref, F32)
    taps[4 * block : 6 * block, :] = jnp.zeros((2 * block, 9 * ch), BF16)

    def gradient(t):
        if form == "first":
            gc, lp, rp, from_l, from_r = gs
            mid = gc[t].astype(F32)
            left = from_l[t, :1].astype(F32) + lp[t, :1].astype(F32)
            right = from_r[t, 1:].astype(F32) + rp[t, 1:].astype(F32)
            return jnp.concatenate(
                [
                    left,
                    mid[:1] + from_l[t, 1:].astype(F32),
                    mid[1:-1],
                    mid[-1:] + from_r[t, :1].astype(F32),
                    right,
                ],
                axis=0,
            )
        return column_block(gs, t).astype(F32)

    def inputs(t):
        x = column_block(xs, t)
        return (x if n_x == 1 else x[1:-1]).astype(F32).reshape(block, ch)

    @pl.loop(0, frames)
    def _(t):
        g = gradient(t)
        if form != "odd":
            g = jnp.concatenate([g[:1] * low, g[1:-1], g[-1:] * high], axis=0)
        g = g.reshape(outer * rows, ch)
        before, after = row_shifts(g)
        for b, v in enumerate((after, g, before)):
            put_taps(taps, t, v, b, cols, ch, high if form == "odd" else None, True)
    @pl.loop(0, frames)
    def _(t):
        x = inputs(t)
        inv = lax.rsqrt(jnp.mean(x * x, axis=-1, keepdims=True) + EPS)
        u = x * inv * gain
        sig = jax.nn.sigmoid(u)
        fac_ref[t] = sig * (1.0 + u * (1.0 - sig)) * gain * inv
    convolve(taps, w_hbm, w_buf, sem, acc, True)
    for t in range(frames):
        x = inputs(t)
        inv2 = 1.0 / (jnp.mean(x * x, axis=-1, keepdims=True) + EPS)
        y = acc[t * block : (t + 1) * block] * fac_ref[t]
        dx = y - x * (inv2 * jnp.mean(y * x, axis=-1, keepdims=True))
        out = gradient(t)[1:-1] + dx.reshape(cols, rows, ch)
        gf_ref[t] = out
        if outs:
            write_block(out.astype(BF16), outs, t)


def run_bwd(form, out_cols, tile_info, xs, gs, gain, weight_back):
    frames, _, rows, ch = xs[0].shape
    cols = xs[0].shape[1] if len(xs) == 1 else sum(x.shape[1] for x in xs) - 2
    outs = [jax.ShapeDtypeStruct((frames, cols, rows, ch), F32)]
    outs += [jax.ShapeDtypeStruct((frames, n, rows, ch), BF16) for n in out_cols]
    return pl.pallas_call(
        functools.partial(bwd_kernel, form, len(xs), len(gs)),
        out_shape=outs,
        in_specs=[SM] + [VM] * (len(xs) + len(gs) + 1) + [HB],
        out_specs=[VM] * len(outs),
        scratch_shapes=[
            pltpu.VMEM((6 * cols * rows, 9 * ch), BF16),
            pltpu.VMEM(weight_back.shape, BF16),
            pltpu.VMEM((frames, cols * rows, ch), F32),
            pltpu.VMEM((frames * cols * rows, ch), F32),
            pltpu.SemaphoreType.DMA((PIECES,)),
        ],
        name=f"bwd_{form}",
        compiler_params=GRANT,
    )(tile_info, *xs, *gs, gain, weight_back)


def first_kernel(order_ref, latent_ref, x_ref, l_ref, r_ref):
    for t in range(x_ref.shape[0]):
        x = latent_ref[order_ref[t]]
        x_ref[t] = x
        l_ref[t] = x[:1]
        r_ref[t] = x[x.shape[0] - 1 :]


def run_first(order, latent):
    frames, cols, rows, ch = latent.shape
    return pl.pallas_call(
        first_kernel,
        out_shape=[jax.ShapeDtypeStruct((frames, n, rows, ch), BF16) for n in (cols, 1, 1)],
        in_specs=[SM, VM],
        out_specs=[VM] * 3,
        name="first",
        compiler_params=GRANT,
    )(order, latent)


def unwritten(*shapes, dtype=BF16):
    return tuple(
        pl.pallas_call(
            lambda out_ref: None,
            out_shape=jax.ShapeDtypeStruct(shape, dtype),
            out_specs=HB,
            name="unwritten",
        )()
        for shape in shapes
    )


def up_kernel(x_ref, wa_ref, wb_ref, spread_ref, *rest):
    pre_ref, *feat_refs, held, cells, phases, feats = rest
    frames, outer, rows, ch = x_ref.shape
    cols = outer - 2
    cu = wa_ref.shape[3]
    half = wa_ref.shape[0] * wa_ref.shape[2]
    block = outer * rows
    held[0 : 2 * block, :] = jnp.zeros((2 * block, 2 * half), BF16)
    for t in range(frames):
        held[(2 + t) * block : (3 + t) * block, :] = jnp.dot(
            x_ref[t].reshape(block, ch), spread_ref[...], preferred_element_type=F32
        ).astype(BF16)

    @pl.loop(0, 9)
    def _(tap):
        total = jnp.zeros((frames * block, cu), F32)
        for a in range(3):
            for part, w_ref in enumerate((wa_ref, wb_ref)):
                total = total + jnp.dot(
                    held[a * block : (a + frames) * block, part * half : (part + 1) * half],
                    w_ref[:, 9 * a + tap].reshape(half, cu),
                    preferred_element_type=F32,
                )
        cells[tap] = total

    shape = (frames, outer, rows, cu)
    by_phase = [[], []]
    for c in range(3):
        before, _ = row_shifts(cells[c])
        _, after = row_shifts(cells[6 + c])
        middle = cells[3 + c]
        by_phase[0].append((before + middle + cells[6 + c]).reshape(shape))
        by_phase[1].append((cells[c] + middle + after).reshape(shape))
    for p in range(2):
        left, mid, right = by_phase[p]
        phases[p, 0] = left[:, 0:cols] + mid[:, 1 : cols + 1] + right[:, 1 : cols + 1]
        phases[p, 1] = left[:, 1 : cols + 1] + mid[:, 1 : cols + 1] + right[:, 2 : cols + 2]

    @pl.loop(0, frames)
    def _(t):
        for w in range(cols):
            pair = [jnp.concatenate([phases[p, 0, t, w], phases[p, 1, t, w]], axis=1) for p in range(2)]
            lanes = slice(w * 2 * cu, (w + 1) * 2 * cu)
            for h in range(2):
                mine = slice(h * rows // 2, (h + 1) * rows // 2)
                piece = jnp.concatenate([pair[0][mine], pair[1][mine]], axis=0)
                pre_ref[2 * t + h, :, lanes] = piece
                feats[2 * t + h, :, lanes] = jax.nn.silu(piece).astype(BF16)

    for i, feat_ref in enumerate(feat_refs):
        feat_ref[...] = feats[i]


def run_up(x, wa, wb, spread):
    frames, outer, rows, ch = x.shape
    chunk = (rows, 2 * (outer - 2) * wa.shape[3])
    return pl.pallas_call(
        up_kernel,
        out_shape=[
            jax.ShapeDtypeStruct((2 * frames, *chunk), F32),
            *(jax.ShapeDtypeStruct(chunk, BF16) for _ in range(2 * frames)),
        ],
        in_specs=[VM] * 4,
        out_specs=[VM] * (1 + 2 * frames),
        scratch_shapes=[
            pltpu.VMEM((6 * outer * rows, spread.shape[1]), BF16),
            pltpu.VMEM((9, frames * outer * rows, wa.shape[3]), F32),
            pltpu.VMEM((2, 2, frames, outer - 2, rows, wa.shape[3]), F32),
            pltpu.VMEM((2 * frames, *chunk), BF16),
        ],
        name="up",
        compiler_params=GRANT,
    )(x, wa, wb, spread)


def exact_dot(value, ones, dims):
    total = None
    for _ in range(3):
        piece = value.astype(BF16)
        value = value - piece.astype(F32)
        part = lax.dot_general(piece, ones, dims, preferred_element_type=F32)
        total = part if total is None else total + part
    return total


GROUP = 48


def group_masks(rows, groups):
    row = lax.broadcasted_iota(jnp.int32, (rows, groups * GROUP), 0)
    lane = lax.broadcasted_iota(jnp.int32, (rows, groups * GROUP), 1)
    wanted = (row % 8) * 2 + (row // 8) % 2
    return lane // GROUP == wanted


def fold_matrix(groups):
    lane = lax.broadcasted_iota(jnp.int32, (groups * GROUP, GROUP), 0)
    column = lax.broadcasted_iota(jnp.int32, (groups * GROUP, GROUP), 1)
    return (lane % GROUP == column).astype(F32).astype(BF16)


def logit_kernel(half_ref, z_ref, w_hbm, out_ref, table, w_buf, sem):
    outs, keep = w_buf.shape
    span = z_ref.shape[1]
    groups = keep // span
    copy = pltpu.make_async_copy(
        w_hbm.at[:, pl.ds(pl.multiple_of(half_ref[0] * keep, 128), keep)], w_buf, sem
    )
    copy.start()
    mask = group_masks(z_ref.shape[0], groups)
    fold = fold_matrix(groups)
    copy.wait()

    @pl.loop(0, groups)
    def _(group):
        r, e = group // 2, group % 2
        true_row = 2 * (r % 4) + r // 4
        start = pl.multiple_of((2 * true_row + e) * span, 128)
        table[pl.ds(pl.multiple_of(group * GROUP, 16), GROUP), :] = jnp.concatenate(
            [w_buf[:, pl.ds(start, span)], jnp.zeros((GROUP - outs, span), BF16)], axis=0
        )

    pairs = lax.dot_general(
        z_ref[...], table[...], (((1,), (1,)), ((), ())), preferred_element_type=F32
    )
    pairs = jnp.where(mask, pairs, 0.0)
    patches = z_ref.shape[0] // groups
    summed = jnp.sum(pairs.reshape(patches, groups, groups * GROUP), axis=1)
    out_ref[...] = exact_dot(summed, fold, (((1,), (0,)), ((), ())))


def run_logit(half, z, weight, keep):
    outs = weight.shape[0]
    span = z.shape[1]
    groups = keep // span
    return pl.pallas_call(
        logit_kernel,
        out_shape=[
            jax.ShapeDtypeStruct((z.shape[0] // groups, GROUP), F32),
            jax.ShapeDtypeStruct((groups * GROUP, span), BF16),
        ],
        in_specs=[SM, VM, HB],
        out_specs=[VM, VM],
        scratch_shapes=[pltpu.VMEM((outs, keep), BF16), pltpu.SemaphoreType.DMA],
        name="logit",
        compiler_params=GRANT,
    )(half, z, weight)


def back_kernel(mine_ref, other_ref, coef_ref, table_ref, out_ref):
    groups = table_ref.shape[0] // GROUP
    patches = mine_ref.shape[0]
    squashed = jnp.tanh(mine_ref[...] + other_ref[...])
    grad = (coef_ref[...] * (1.0 - squashed * squashed)).astype(BF16)
    wide = lax.dot_general(
        grad, fold_matrix(groups), (((1,), (1,)), ((), ())), preferred_element_type=F32
    )
    wide = jnp.broadcast_to(wide[:, None, :], (patches, groups, groups * GROUP))
    wide = wide.reshape(patches * groups, groups * GROUP)
    wide = jnp.where(group_masks(patches * groups, groups), wide, 0.0).astype(BF16)
    out_ref[...] = jnp.dot(wide, table_ref[...], preferred_element_type=F32).astype(BF16)


def run_back(mine, other, coef, table):
    rows = mine.shape[0] * table.shape[0] // GROUP
    return pl.pallas_call(
        back_kernel,
        out_shape=jax.ShapeDtypeStruct((rows, table.shape[1]), BF16),
        in_specs=[VM] * 4,
        out_specs=VM,
        name="back",
        compiler_params=GRANT,
    )(mine, other, coef, table)


def sum_kernel(in_ref, out_ref):
    total = in_ref[0].astype(F32)
    for i in range(1, in_ref.shape[0]):
        total = total + in_ref[i].astype(F32)
    out_ref[...] = total.astype(BF16)


def run_sum(values):
    return pl.pallas_call(
        sum_kernel,
        out_shape=jax.ShapeDtypeStruct(values.shape[1:], BF16),
        in_specs=[VM],
        out_specs=VM,
        name="sum",
        compiler_params=GRANT,
    )(values)


def order_kernel(wa_ref, wb_ref, spread_ref, out_ref):
    half = wa_ref.shape[0] * wa_ref.shape[2]
    cu = wa_ref.shape[3]

    @pl.loop(0, wa_ref.shape[1])
    def _(tap):
        total = None
        for part, w_ref in enumerate((wa_ref, wb_ref)):
            turned = lax.dot_general(
                w_ref[:, tap].reshape(half, cu),
                spread_ref[:, part * half : (part + 1) * half],
                (((0,), (1,)), ((), ())),
                preferred_element_type=F32,
            )
            total = turned if total is None else total + turned
        out_ref[tap] = total.astype(BF16)


def run_order(wa, wb, spread):
    return pl.pallas_call(
        order_kernel,
        out_shape=jax.ShapeDtypeStruct((wa.shape[1], wa.shape[3], spread.shape[0]), BF16),
        in_specs=[VM] * 3,
        out_specs=VM,
        name="order",
        compiler_params=GRANT,
    )(wa, wb, spread)


def adj_kernel(pre_ref, w_ref, *rest):
    *grad_refs, gf_ref, l_ref, r_ref, held, acc_ref, grads = rest
    frames, cols, rows, ch = gf_ref.shape
    outer = cols + 2
    cu = w_ref.shape[1]
    block = outer * rows
    held[:, frames * block :, :] = jnp.zeros((9, 2 * block, cu), BF16)
    zero = jnp.zeros((1, rows, cu), F32)
    for i, grad_ref in enumerate(grad_refs):
        grads[i] = grad_ref[...]

    @pl.loop(0, frames)
    def _(t):
        chunks = []
        for h in range(2):
            pre = pre_ref[2 * t + h]
            sig = jax.nn.sigmoid(pre)
            grad = grads[2 * t + h].astype(F32) * sig * (1.0 + pre * (1.0 - sig))
            chunks.append(grad.astype(BF16).astype(F32))
        fine = []
        for p in range(2):
            low = slice(p * rows // 2, (p + 1) * rows // 2)
            whole = jnp.concatenate([chunks[0][low], chunks[1][low]], axis=0)
            even, odd = (
                jnp.concatenate(
                    [whole[:, (2 * w + q) * cu : (2 * w + q + 1) * cu][None] for w in range(cols)], axis=0
                )
                for q in range(2)
            )
            own = jnp.concatenate([zero, even + odd, zero], axis=0)
            later = jnp.concatenate([even[:1], odd[:-1] + even[1:], odd[-1:], zero], axis=0)
            sooner = jnp.concatenate([zero, even[:1], odd[:-1] + even[1:], odd[-1:]], axis=0)
            fine.append([v.reshape(block, cu) for v in (later, own, sooner)])
        for c in range(3):
            top, low = fine[0][c], fine[1][c]
            _, top_after = row_shifts(top)
            low_before, _ = row_shifts(low)
            for b, v in enumerate((low + top_after, top + low, low_before + top)):
                held[3 * b + c, pl.ds(pl.multiple_of(t * block, 16), block), :] = v.astype(BF16)
    acc_ref[...] = jnp.zeros_like(acc_ref)

    @pl.loop(0, 3)
    def _(a):
        total = acc_ref[...]
        for bc in range(9):
            total = total + jnp.dot(
                held[bc, pl.ds(pl.multiple_of((2 - a) * block, 16), frames * block), :],
                w_ref[9 * a + bc],
                preferred_element_type=F32,
            )
        acc_ref[...] = total

    out = acc_ref[...]
    out = out.reshape(frames, outer, rows, ch)
    gf_ref[...] = out[:, 1:-1]
    l_ref[...] = out[:, :2].astype(BF16)
    r_ref[...] = out[:, -2:].astype(BF16)


def run_adj(grads, pre, weight, frames, cols):
    rows = pre.shape[1]
    cu, ch = weight.shape[1:]
    return pl.pallas_call(
        adj_kernel,
        out_shape=[
            jax.ShapeDtypeStruct((frames, cols, rows, ch), F32),
            jax.ShapeDtypeStruct((frames, 2, rows, ch), BF16),
            jax.ShapeDtypeStruct((frames, 2, rows, ch), BF16),
        ],
        in_specs=[VM] * (2 + len(grads)),
        out_specs=[VM] * 3,
        scratch_shapes=[
            pltpu.VMEM((9, 6 * (cols + 2) * rows, cu), BF16),
            pltpu.VMEM((frames * (cols + 2) * rows, ch), F32),
            pltpu.VMEM(pre.shape, BF16),
        ],
        name="adj",
        compiler_params=GRANT,
    )(pre, weight, *grads)


def on_device(latent, frame_order, section_weight, section_gain, up_weight, reward_weight, reward_coef):
    segs = lax.axis_size("segment")
    chips = lax.axis_size("chip")
    tiles = 2 * chips
    seg = lax.axis_index("segment")
    core = lax.axis_index("core")
    tile = 2 * lax.axis_index("chip") + core
    frames, rows, cols, ch = latent.shape
    cu = up_weight.shape[2]
    outs_dev = reward_coef.shape[0]
    last = segs - 1
    halves = segs // frames
    span = 2 * cols * cu
    keep = 2 * rows // halves * 2 * span
    barrier = lax.optimization_barrier
    tile_info = jnp.stack([tile, jnp.full_like(tile, tiles)])
    block = (frames, cols, rows, ch)
    side = (frames, 1, rows, ch)
    side2 = (frames, 2, rows, ch)

    def route(pairs_of_segments, shift):
        return [
            (source * tiles + t, target * tiles + t + shift)
            for source, target in pairs_of_segments
            for t in range(tiles)
            if 0 <= t + shift < tiles
        ]

    def send(value, source, target):
        return lax.ppermute(value, AXES, route([(source, target)], 0))

    def beside(value, shift):
        return lax.ppermute(value, AXES, route([(s, s) for s in range(segs)], shift))

    def hop_route(source, target, shift):
        step = target - source
        pairs = [(s, s + step) for s in range(source % 2, segs, 2) if 0 <= s + step < segs]
        return pairs, shift

    def hop(center, left, right, source, target):
        center, left, right = (
            lax.ppermute(value, AXES, route(*hop_route(source, target, shift)))
            for value, shift in ((center, 0), (right, 1), (left, -1))
        )
        return left, center, right

    def turn_round(pairs_of_segments, shift):
        return [
            (source * tiles + t, target * tiles + (t + shift) % tiles)
            for source, target in pairs_of_segments
            for t in range(tiles)
        ]

    def half_hop(first_three, last_three, source, target):
        to_left, to_right = (-1, 0) if source % 2 == 0 else (0, 1)
        left = lax.ppermute(last_three, AXES, turn_round(*hop_route(source, target, to_right)))
        right = lax.ppermute(first_three, AXES, turn_round(*hop_route(source, target, to_left)))
        return left, right

    def gather_up():
        own = up_weight.shape[1]
        source = jnp.pad(up_weight, ((0, 0), (0, PAD - own), (0, 0)))
        wa = lax.all_to_all(
            jnp.broadcast_to(source[None], (chips, *source.shape)), "chip", 0, 0, tiled=True
        )
        wb = lax.ppermute(wa, "core", [(0, 1), (1, 0)])
        channel = lax.broadcasted_iota(jnp.int32, (ch, tiles * PAD), 0)
        place = lax.broadcasted_iota(jnp.int32, (ch, tiles * PAD), 1)
        other, chip_of, within = place // (chips * PAD), place // PAD % chips, place % PAD
        origin = 2 * chip_of + jnp.where(other == 0, core, 1 - core)
        spread = ((within < own) & (channel == origin * own + within)).astype(BF16)
        return wa, wb, spread, run_order(wa, wb, spread)

    up_shape = (chips, 27, PAD, cu)

    def turn(weight):
        return weight[0].transpose(0, 2, 1).reshape(27 * ch, ch)

    def start():
        x, left, right = run_first(frame_order, latent.transpose(0, 2, 1, 3))
        return beside(right, 1), x, beside(left, -1)

    weight_fwd = section_weight[0].reshape(27 * ch, ch)
    gathered = lax.cond(
        seg == last,
        gather_up,
        lambda: unwritten(up_shape, up_shape, (ch, tiles * PAD), (27, cu, ch)),
    )
    turned = lax.cond(seg > 1, lambda: turn(section_weight), lambda: unwritten((27 * ch, ch))[0])
    state = lax.cond(seg == 0, start, lambda: unwritten(side, block, side))
    gathered, turned, state = barrier((gathered, turned, state))

    three = (frames, 3, rows, ch)
    taken = [state]
    for k in range(last):
        wide = k == last - 1
        made_shapes = (block, side2, side2) if wide else (three, three)

        def go(state=state, k=k, wide=wide, made_shapes=made_shapes):
            form = "odd" if k % 2 else "even"
            made = lax.cond(
                seg == k,
                lambda: tuple(
                    run_fwd(form, [m[1] for m in made_shapes], tile_info, state, section_gain, weight_fwd)
                ),
                lambda: unwritten(*made_shapes),
            )
            return hop(*made, k, k + 1) if wide else half_hop(*made, k, k + 1)

        given = (side2, block, side2) if wide else (three, three)
        state = lax.cond(
            (seg == k) | (seg == k + 1), go, lambda given=given: unwritten(*given)
        )
        taken.append(state)
        if k == 1:
            late, state = barrier((section_weight, state))
            turned_late = lax.cond(
                seg <= 1, lambda late=late: turn(late), lambda: unwritten((27 * ch, ch))[0]
            )
            turned_late, state = barrier((turned_late, state))
            taken[-1] = state

    chunk = (rows, span)

    def upsampled():
        (deep,) = run_fwd("wide", [cols + 2], tile_info, state, section_gain, weight_fwd)
        return tuple(run_up(deep, *gathered[:3]))

    pre, *feats = lax.cond(
        seg == last,
        upsampled,
        lambda: (
            unwritten((segs, *chunk), dtype=F32)[0],
            *unwritten(*([chunk] * last)),
            jnp.zeros(chunk, BF16),
        ),
    )
    mine = functools.reduce(jnp.add, [send(feats[k], last, k) for k in range(last)], feats[last])
    coef = jnp.pad(reward_coef, (0, GROUP - outs_dev))[None]
    mine, coef = barrier((mine, coef))
    everyone = lax.cond(
        seg >= 0,
        lambda: lax.all_to_all(
            jnp.broadcast_to(mine[None], (tiles, *chunk)), TILE, 0, 0, tiled=True
        ),
        lambda: unwritten((tiles, *chunk))[0],
    )
    half = (seg % halves).reshape(1)
    partial, table = run_logit(half, everyone.reshape(tiles * rows, span), reward_weight.T, keep)
    group = [(s, s // halves * halves + (s + 1) % halves) for s in range(segs)]
    other = lax.ppermute(partial, "segment", group)
    shares = run_back(partial, other, coef, table)
    shares = lax.all_to_all(shares.reshape(tiles, *chunk), TILE, 0, 0, tiled=True)
    share = run_sum(shares)
    grads = [send(share, k, last) for k in range(last)] + [share]

    results = {}
    for k in range(last, 0, -1):

        def go_back(state=state, k=k):
            def live():
                if k == last:
                    deep, lp, rp = run_adj(grads, pre, gathered[3], frames, cols)
                    from_r, from_l = beside(lp, -1), beside(rp, 1)
                    gs = (deep, lp, rp, from_l, from_r)
                    made = run_bwd(
                        "first", (cols, 1, 1), tile_info, taken[k][1:2], gs, section_gain, turned
                    )
                else:
                    form = "odd" if k % 2 else "even"
                    weight = turned if k > 1 else turned_late
                    made = run_bwd(form, (3, 3), tile_info, taken[k], state, section_gain, weight)
                return (*made[1:], made[0])

            shapes = (block, side, side) if k == last else (three, three)
            *made, result = lax.cond(
                seg == k,
                live,
                lambda: (*unwritten(*shapes), *unwritten(block, dtype=F32)),
            )
            passed = hop(*made, k, k - 1) if k == last else half_hop(*made, k, k - 1)
            return passed, result

        given = (side, block, side) if k == last else (three, three)
        state, results[k] = lax.cond(
            (seg == k) | (seg == k - 1),
            go_back,
            lambda given=given: (unwritten(*given), unwritten(block, dtype=F32)[0]),
        )

    def finish(k):
        if k == 0:
            result = run_bwd(
                "even", (), tile_info, taken[0][1:2], state, section_gain, turned_late
            )[0]
        else:
            result = results[k]
            if k != last and k % 2:
                moved = turn_round([(s, s) for s in range(segs)], 1)
                left = lax.ppermute(result[:, cols - 2 :], AXES, moved)
                result = jnp.concatenate([left, result[:, : cols - 2]], axis=1)
        return result.transpose(0, 2, 1, 3)

    return lax.switch(seg, [functools.partial(finish, k) for k in range(segs)])[None]


def solution(mesh):
    shape = mesh.devices.shape
    fine = jax.sharding.Mesh(mesh.devices.reshape(shape[0], shape[1] // 2, 2), AXES)
    in_specs = (
        P(None, None, TILE, None),
        P(),
        P("segment", None, None, None),
        P("segment", None),
        P(None, TILE, None),
        P(None, TILE),
        P(TILE),
    )
    out_specs = P("segment", None, None, TILE, None)
    return jax.shard_map(
        on_device, mesh=fine, in_specs=in_specs, out_specs=out_specs, check_vma=False
    )
```

```python
import functools

import jax
import jax.numpy as jnp
from jax import lax
from jax.experimental import pallas as pl
from jax.experimental.pallas import tpu as pltpu
from jax.sharding import PartitionSpec as P

EPS = 1e-06
F32 = jnp.float32
BF16 = jnp.bfloat16
AXES = ("segment", "chip", "core")
TILE = ("chip", "core")
PAD = 16
VM = pl.BlockSpec(memory_space=pltpu.VMEM)
HB = pl.BlockSpec(memory_space=pl.ANY)
SM = pl.BlockSpec(memory_space=pltpu.SMEM)
GRANT = pltpu.CompilerParams(vmem_limit_bytes=24 * 2**20)


def row_shifts(v):
    count = v.shape[0]
    row = lax.broadcasted_iota(jnp.int32, v.shape, 0) & 7
    before = jnp.where(row == 0, 0.0, pltpu.roll(v, 1, 0))
    after = jnp.where(row == 7, 0.0, pltpu.roll(v, count - 1, 0))
    return before, after


PIECES = 6


def weight_copy(w_hbm, w_buf, sem, piece):
    rows = w_hbm.shape[0] // PIECES
    part = pl.ds(pl.multiple_of(piece * rows, 64), rows)
    return pltpu.make_async_copy(w_hbm.at[part], w_buf.at[part], sem.at[piece])


def start_weights(w_hbm, w_buf, sem, backward):
    per = PIECES // 3
    for step in range(PIECES):
        a = 2 - step // per if backward else step // per
        weight_copy(w_hbm, w_buf, sem, a * per + step % per).start()


def convolve(taps, w_hbm, w_buf, sem, acc_ref, backward):
    count = acc_ref.shape[0]
    block = count // 4
    per = PIECES // 3
    rows = w_hbm.shape[0] // PIECES
    acc_ref[...] = jnp.zeros_like(acc_ref)

    @pl.loop(0, 3)
    def _(step):
        a = 2 - step if backward else step
        for part in range(per):
            piece = a * per + part
            weight_copy(w_hbm, w_buf, sem, piece).wait()
            acc_ref[...] += jnp.dot(
                taps[pl.ds(pl.multiple_of(step * block, 16), count), part * rows : (part + 1) * rows],
                w_buf[pl.ds(pl.multiple_of(piece * rows, 64), rows), :],
                preferred_element_type=F32,
            )


def column_block(pieces, t):
    parts = [piece[t] for piece in pieces]
    return parts[0] if len(parts) == 1 else jnp.concatenate(parts, axis=0)


def write_block(out, refs, t):
    cols = out.shape[0]
    if len(refs) == 2:
        refs[0][t] = out[:3]
        refs[1][t] = out[cols - 3 :]
    else:
        edge = refs[1].shape[1]
        refs[0][t] = out
        refs[1][t] = out[:edge]
        refs[2][t] = out[cols - edge :]


def edge_scales(form, tile_ref, dtype):
    one, none = jnp.ones((), dtype), jnp.zeros((), dtype)
    low = jnp.where(tile_ref[0] == 0, none, one) if form == "even" else one
    high = jnp.where(tile_ref[0] == tile_ref[1] - 1, none, one)
    return low, high


def put_taps(taps, t_at, v, b, columns, ch, cut, backward):
    rows = 8
    block = columns * rows
    for c in range(3):
        start = (2 - c if backward else c) * rows
        piece = v[start : start + block]
        if cut is not None and c != 1:
            bad = (2 if start == 0 else 1) * rows
            piece = jnp.concatenate([piece[:bad], piece[bad : bad + rows] * cut, piece[bad + rows :]], axis=0)
        at = (3 * b + c) * ch
        taps[pl.ds(pl.multiple_of(t_at * block, 16), block), at : at + ch] = piece.astype(BF16)


def fwd_kernel(form, count, *refs):
    tile_ref, *pieces = refs[: count + 1]
    gain_ref, w_hbm = refs[count + 1 : count + 3]
    *outs, taps, w_buf, acc, sem = refs[count + 3 :]
    start_weights(w_hbm, w_buf, sem, False)
    frames, _, rows, ch = pieces[0].shape
    outer = sum(piece.shape[1] for piece in pieces)
    inner = outer - 2
    block = inner * rows
    gain = gain_ref[...].astype(F32)
    low, high = edge_scales(form, tile_ref, F32)
    taps[0 : 2 * block, :] = jnp.zeros((2 * block, 9 * ch), BF16)
    @pl.loop(0, frames)
    def _(t):
        x = column_block(pieces, t).astype(F32)
        if form == "even":
            x = jnp.concatenate([x[:1] * low, x[1:-1], x[-1:] * high], axis=0)
        x = x.reshape(outer * rows, ch)
        inv = lax.rsqrt(jnp.mean(x * x, axis=-1, keepdims=True) + EPS)
        act = jax.nn.silu(x * inv * gain)
        before, after = row_shifts(act)
        for b, v in enumerate((before, act, after)):
            put_taps(taps, 2 + t, v, b, inner, ch, high if form == "odd" else None, False)
    convolve(taps, w_hbm, w_buf, sem, acc, False)
    @pl.loop(0, frames)
    def _(t):
        x = column_block(pieces, t)[1:-1].astype(F32)
        out = x + acc[pl.ds(pl.multiple_of(t * block, 8), block)].reshape(inner, rows, ch)
        if form == "wide":
            tile = tile_ref[0]
            col = lax.broadcasted_iota(jnp.int32, out.shape, 0)
            first = jnp.where(tile == 0, 1, 0)
            stop = jnp.where(tile == tile_ref[1] - 1, inner - 1, inner)
            outs[0][t] = jnp.where((col >= first) & (col < stop), out, 0.0).astype(BF16)
        else:
            write_block(out.astype(BF16), outs, t)


def run_fwd(form, out_cols, tile_info, pieces, gain, weight):
    frames, _, rows, ch = pieces[0].shape
    inner = sum(piece.shape[1] for piece in pieces) - 2
    return pl.pallas_call(
        functools.partial(fwd_kernel, form, len(pieces)),
        out_shape=[jax.ShapeDtypeStruct((frames, n, rows, ch), BF16) for n in out_cols],
        in_specs=[SM] + [VM] * (len(pieces) + 1) + [HB],
        out_specs=[VM] * len(out_cols),
        scratch_shapes=[
            pltpu.VMEM((6 * inner * rows, 9 * ch), BF16),
            pltpu.VMEM(weight.shape, BF16),
            pltpu.VMEM((frames * inner * rows, ch), F32),
            pltpu.SemaphoreType.DMA((PIECES,)),
        ],
        name=f"fwd_{form}",
        compiler_params=GRANT,
    )(tile_info, *pieces, gain, weight)


def bwd_kernel(form, n_x, n_g, *refs):
    tile_ref, *refs = refs
    xs, gs, (gain_ref, w_hbm, *rest) = refs[:n_x], refs[n_x : n_x + n_g], refs[n_x + n_g :]
    gf_ref, *outs, taps, w_buf, fac_ref, acc, sem = rest
    start_weights(w_hbm, w_buf, sem, True)
    frames, cols, rows, ch = gf_ref.shape
    block = cols * rows
    outer = cols + 2
    gain = gain_ref[...].astype(F32)
    low, high = edge_scales("odd" if form == "odd" else "even", tile_ref, F32)
    taps[4 * block : 6 * block, :] = jnp.zeros((2 * block, 9 * ch), BF16)

    def gradient(t):
        if form == "first":
            gc, lp, rp, from_l, from_r = gs
            mid = gc[t].astype(F32)
            left = from_l[t, :1].astype(F32) + lp[t, :1].astype(F32)
            right = from_r[t, 1:].astype(F32) + rp[t, 1:].astype(F32)
            return jnp.concatenate(
                [
                    left,
                    mid[:1] + from_l[t, 1:].astype(F32),
                    mid[1:-1],
                    mid[-1:] + from_r[t, :1].astype(F32),
                    right,
                ],
                axis=0,
            )
        return column_block(gs, t).astype(F32)

    def inputs(t):
        x = column_block(xs, t)
        return (x if n_x == 1 else x[1:-1]).astype(F32).reshape(block, ch)

    @pl.loop(0, frames)
    def _(t):
        g = gradient(t)
        if form != "odd":
            g = jnp.concatenate([g[:1] * low, g[1:-1], g[-1:] * high], axis=0)
        g = g.reshape(outer * rows, ch)
        before, after = row_shifts(g)
        for b, v in enumerate((after, g, before)):
            put_taps(taps, t, v, b, cols, ch, high if form == "odd" else None, True)
    @pl.loop(0, frames)
    def _(t):
        x = inputs(t)
        inv = lax.rsqrt(jnp.mean(x * x, axis=-1, keepdims=True) + EPS)
        u = x * inv * gain
        sig = jax.nn.sigmoid(u)
        fac_ref[t] = sig * (1.0 + u * (1.0 - sig)) * gain * inv
    convolve(taps, w_hbm, w_buf, sem, acc, True)
    for t in range(frames):
        x = inputs(t)
        inv2 = 1.0 / (jnp.mean(x * x, axis=-1, keepdims=True) + EPS)
        y = acc[t * block : (t + 1) * block] * fac_ref[t]
        dx = y - x * (inv2 * jnp.mean(y * x, axis=-1, keepdims=True))
        out = gradient(t)[1:-1] + dx.reshape(cols, rows, ch)
        gf_ref[t] = out
        if outs:
            write_block(out.astype(BF16), outs, t)


def run_bwd(form, out_cols, tile_info, xs, gs, gain, weight_back):
    frames, _, rows, ch = xs[0].shape
    cols = xs[0].shape[1] if len(xs) == 1 else sum(x.shape[1] for x in xs) - 2
    outs = [jax.ShapeDtypeStruct((frames, cols, rows, ch), F32)]
    outs += [jax.ShapeDtypeStruct((frames, n, rows, ch), BF16) for n in out_cols]
    return pl.pallas_call(
        functools.partial(bwd_kernel, form, len(xs), len(gs)),
        out_shape=outs,
        in_specs=[SM] + [VM] * (len(xs) + len(gs) + 1) + [HB],
        out_specs=[VM] * len(outs),
        scratch_shapes=[
            pltpu.VMEM((6 * cols * rows, 9 * ch), BF16),
            pltpu.VMEM(weight_back.shape, BF16),
            pltpu.VMEM((frames, cols * rows, ch), F32),
            pltpu.VMEM((frames * cols * rows, ch), F32),
            pltpu.SemaphoreType.DMA((PIECES,)),
        ],
        name=f"bwd_{form}",
        compiler_params=GRANT,
    )(tile_info, *xs, *gs, gain, weight_back)


def turn_kernel(in_ref, out_ref):
    size = in_ref.shape[1]
    row = lax.broadcasted_iota(jnp.int32, (size, size), 0)
    lane = lax.broadcasted_iota(jnp.int32, (size, size), 1)
    same = (row == lane).astype(F32).astype(BF16)

    @pl.loop(0, in_ref.shape[0])
    def _(i):
        out_ref[i] = lax.dot_general(
            same, in_ref[i], (((1,), (1,)), ((), ())), preferred_element_type=F32
        ).astype(BF16)


def run_turn(weight):
    taps, ch, _ = weight.shape
    spec = pl.BlockSpec((3, ch, ch), lambda i: (i, 0, 0))
    return pl.pallas_call(
        turn_kernel,
        out_shape=jax.ShapeDtypeStruct(weight.shape, BF16),
        grid=(taps // 3,),
        in_specs=[spec],
        out_specs=spec,
        name="turn",
        compiler_params=GRANT,
    )(weight).reshape(taps * ch, ch)


def first_kernel(order_ref, latent_ref, x_ref, l_ref, r_ref):
    for t in range(x_ref.shape[0]):
        x = latent_ref[order_ref[t]]
        x_ref[t] = x
        l_ref[t] = x[:1]
        r_ref[t] = x[x.shape[0] - 1 :]


def run_first(order, latent):
    frames, cols, rows, ch = latent.shape
    return pl.pallas_call(
        first_kernel,
        out_shape=[jax.ShapeDtypeStruct((frames, n, rows, ch), BF16) for n in (cols, 1, 1)],
        in_specs=[SM, VM],
        out_specs=[VM] * 3,
        name="first",
        compiler_params=GRANT,
    )(order, latent)


def unwritten(*shapes, dtype=BF16):
    return tuple(
        pl.pallas_call(
            lambda out_ref: None,
            out_shape=jax.ShapeDtypeStruct(shape, dtype),
            out_specs=HB,
            name="unwritten",
        )()
        for shape in shapes
    )


def up_kernel(x_ref, wa_ref, wb_ref, spread_ref, *rest):
    pre_ref, *feat_refs, held, cells, phases, feats = rest
    frames, outer, rows, ch = x_ref.shape
    cols = outer - 2
    cu = wa_ref.shape[3]
    half = wa_ref.shape[0] * wa_ref.shape[2]
    block = outer * rows
    held[0 : 2 * block, :] = jnp.zeros((2 * block, 2 * half), BF16)
    for t in range(frames):
        held[(2 + t) * block : (3 + t) * block, :] = jnp.dot(
            x_ref[t].reshape(block, ch), spread_ref[...], preferred_element_type=F32
        ).astype(BF16)

    @pl.loop(0, 9)
    def _(tap):
        total = jnp.zeros((frames * block, cu), F32)
        for a in range(3):
            for part, w_ref in enumerate((wa_ref, wb_ref)):
                total = total + jnp.dot(
                    held[a * block : (a + frames) * block, part * half : (part + 1) * half],
                    w_ref[:, 9 * a + tap].reshape(half, cu),
                    preferred_element_type=F32,
                )
        cells[tap] = total

    shape = (frames, outer, rows, cu)
    by_phase = [[], []]
    for c in range(3):
        before, _ = row_shifts(cells[c])
        _, after = row_shifts(cells[6 + c])
        middle = cells[3 + c]
        by_phase[0].append((before + middle + cells[6 + c]).reshape(shape))
        by_phase[1].append((cells[c] + middle + after).reshape(shape))
    for p in range(2):
        left, mid, right = by_phase[p]
        phases[p, 0] = left[:, 0:cols] + mid[:, 1 : cols + 1] + right[:, 1 : cols + 1]
        phases[p, 1] = left[:, 1 : cols + 1] + mid[:, 1 : cols + 1] + right[:, 2 : cols + 2]

    @pl.loop(0, frames)
    def _(t):
        for w in range(cols):
            pair = [jnp.concatenate([phases[p, 0, t, w], phases[p, 1, t, w]], axis=1) for p in range(2)]
            lanes = slice(w * 2 * cu, (w + 1) * 2 * cu)
            for h in range(2):
                mine = slice(h * rows // 2, (h + 1) * rows // 2)
                piece = jnp.concatenate([pair[0][mine], pair[1][mine]], axis=0)
                pre_ref[2 * t + h, :, lanes] = piece
                feats[2 * t + h, :, lanes] = jax.nn.silu(piece).astype(BF16)

    for i, feat_ref in enumerate(feat_refs):
        feat_ref[...] = feats[i]


def run_up(x, wa, wb, spread):
    frames, outer, rows, ch = x.shape
    chunk = (rows, 2 * (outer - 2) * wa.shape[3])
    return pl.pallas_call(
        up_kernel,
        out_shape=[
            jax.ShapeDtypeStruct((2 * frames, *chunk), F32),
            *(jax.ShapeDtypeStruct(chunk, BF16) for _ in range(2 * frames)),
        ],
        in_specs=[VM] * 4,
        out_specs=[VM] * (1 + 2 * frames),
        scratch_shapes=[
            pltpu.VMEM((6 * outer * rows, spread.shape[1]), BF16),
            pltpu.VMEM((9, frames * outer * rows, wa.shape[3]), F32),
            pltpu.VMEM((2, 2, frames, outer - 2, rows, wa.shape[3]), F32),
            pltpu.VMEM((2 * frames, *chunk), BF16),
        ],
        name="up",
        compiler_params=GRANT,
    )(x, wa, wb, spread)


def exact_dot(value, ones, dims):
    total = None
    for _ in range(3):
        piece = value.astype(BF16)
        value = value - piece.astype(F32)
        part = lax.dot_general(piece, ones, dims, preferred_element_type=F32)
        total = part if total is None else total + part
    return total


GROUP = 48


def group_masks(rows, groups):
    row = lax.broadcasted_iota(jnp.int32, (rows, groups * GROUP), 0)
    lane = lax.broadcasted_iota(jnp.int32, (rows, groups * GROUP), 1)
    wanted = (row % 8) * 2 + (row // 8) % 2
    return lane // GROUP == wanted


def fold_matrix(groups):
    lane = lax.broadcasted_iota(jnp.int32, (groups * GROUP, GROUP), 0)
    column = lax.broadcasted_iota(jnp.int32, (groups * GROUP, GROUP), 1)
    return (lane % GROUP == column).astype(F32).astype(BF16)


def logit_kernel(half_ref, z_ref, w_hbm, out_ref, table, w_buf, sem):
    outs, keep = w_buf.shape
    span = z_ref.shape[1]
    groups = keep // span
    copy = pltpu.make_async_copy(
        w_hbm.at[:, pl.ds(pl.multiple_of(half_ref[0] * keep, 128), keep)], w_buf, sem
    )
    copy.start()
    mask = group_masks(z_ref.shape[0], groups)
    fold = fold_matrix(groups)
    copy.wait()

    @pl.loop(0, groups)
    def _(group):
        r, e = group // 2, group % 2
        true_row = 2 * (r % 4) + r // 4
        start = pl.multiple_of((2 * true_row + e) * span, 128)
        table[pl.ds(pl.multiple_of(group * GROUP, 16), GROUP), :] = jnp.concatenate(
            [w_buf[:, pl.ds(start, span)], jnp.zeros((GROUP - outs, span), BF16)], axis=0
        )

    pairs = lax.dot_general(
        z_ref[...], table[...], (((1,), (1,)), ((), ())), preferred_element_type=F32
    )
    pairs = jnp.where(mask, pairs, 0.0)
    patches = z_ref.shape[0] // groups
    summed = jnp.sum(pairs.reshape(patches, groups, groups * GROUP), axis=1)
    out_ref[...] = exact_dot(summed, fold, (((1,), (0,)), ((), ())))


def run_logit(half, z, weight, keep):
    outs = weight.shape[0]
    span = z.shape[1]
    groups = keep // span
    return pl.pallas_call(
        logit_kernel,
        out_shape=[
            jax.ShapeDtypeStruct((z.shape[0] // groups, GROUP), F32),
            jax.ShapeDtypeStruct((groups * GROUP, span), BF16),
        ],
        in_specs=[SM, VM, pl.BlockSpec(memory_space=pltpu.HBM)],
        out_specs=[VM, VM],
        scratch_shapes=[pltpu.VMEM((outs, keep), BF16), pltpu.SemaphoreType.DMA],
        name="logit",
        compiler_params=GRANT,
    )(half, z, weight)


def back_kernel(mine_ref, other_ref, coef_ref, table_ref, out_ref, wide_ref):
    groups = table_ref.shape[0] // GROUP
    patches = mine_ref.shape[0]
    squashed = jnp.tanh(mine_ref[...] + other_ref[...])
    grad = (coef_ref[...] * (1.0 - squashed * squashed)).astype(BF16)
    wide = lax.dot_general(
        grad, fold_matrix(groups), (((1,), (1,)), ((), ())), preferred_element_type=F32
    )
    wide = jnp.broadcast_to(wide[:, None, :], (patches, groups, groups * GROUP))
    wide = wide.reshape(patches * groups, groups * GROUP)
    wide_ref[...] = jnp.where(group_masks(patches * groups, groups), wide, 0.0).astype(BF16)

    @pl.loop(0, out_ref.shape[1] // 512)
    def _(i):
        lanes = pl.ds(pl.multiple_of(i * 512, 128), 512)
        out_ref[:, lanes] = jnp.dot(
            wide_ref[...], table_ref[:, lanes], preferred_element_type=F32
        ).astype(BF16)


def run_back(mine, other, coef, table):
    rows = mine.shape[0] * table.shape[0] // GROUP
    return pl.pallas_call(
        back_kernel,
        out_shape=jax.ShapeDtypeStruct((rows, table.shape[1]), BF16),
        in_specs=[VM] * 4,
        out_specs=VM,
        scratch_shapes=[pltpu.VMEM((rows, table.shape[0]), BF16)],
        name="back",
        compiler_params=GRANT,
    )(mine, other, coef, table)


def sum_kernel(in_ref, out_ref):
    total = in_ref[0].astype(F32)
    for i in range(1, in_ref.shape[0]):
        total = total + in_ref[i].astype(F32)
    out_ref[...] = total.astype(BF16)


def run_sum(values):
    return pl.pallas_call(
        sum_kernel,
        out_shape=jax.ShapeDtypeStruct(values.shape[1:], BF16),
        in_specs=[VM],
        out_specs=VM,
        name="sum",
        compiler_params=GRANT,
    )(values)


def order_kernel(wa_ref, wb_ref, spread_ref, out_ref):
    half = wa_ref.shape[0] * wa_ref.shape[2]
    cu = wa_ref.shape[3]

    @pl.loop(0, wa_ref.shape[1] // 3)
    def _(three):
        for within in range(3):
            tap = 3 * three + within
            total = None
            for part, w_ref in enumerate((wa_ref, wb_ref)):
                turned = lax.dot_general(
                    w_ref[:, tap].reshape(half, cu),
                    spread_ref[:, part * half : (part + 1) * half],
                    (((0,), (1,)), ((), ())),
                    preferred_element_type=F32,
                )
                total = turned if total is None else total + turned
            out_ref[tap] = total.astype(BF16)


def run_order(wa, wb, spread):
    return pl.pallas_call(
        order_kernel,
        out_shape=jax.ShapeDtypeStruct((wa.shape[1], wa.shape[3], spread.shape[0]), BF16),
        in_specs=[VM] * 3,
        out_specs=VM,
        name="order",
        compiler_params=GRANT,
    )(wa, wb, spread)


def adj_kernel(pre_ref, w_ref, *rest):
    grads, gf_ref, l_ref, r_ref, held, acc_ref = rest
    frames, cols, rows, ch = gf_ref.shape
    outer = cols + 2
    cu = w_ref.shape[1]
    block = outer * rows
    held[:, frames * block :, :] = jnp.zeros((9, 2 * block, cu), BF16)
    zero = jnp.zeros((1, rows, cu), F32)

    @pl.loop(0, frames)
    def _(t):
        chunks = []
        for h in range(2):
            pre = pre_ref[2 * t + h]
            sig = jax.nn.sigmoid(pre)
            grad = grads[2 * t + h].astype(F32) * sig * (1.0 + pre * (1.0 - sig))
            chunks.append(grad.astype(BF16).astype(F32))
        fine = []
        for p in range(2):
            low = slice(p * rows // 2, (p + 1) * rows // 2)
            whole = jnp.concatenate([chunks[0][low], chunks[1][low]], axis=0)
            even, odd = (
                jnp.concatenate(
                    [whole[:, (2 * w + q) * cu : (2 * w + q + 1) * cu][None] for w in range(cols)], axis=0
                )
                for q in range(2)
            )
            own = jnp.concatenate([zero, even + odd, zero], axis=0)
            later = jnp.concatenate([even[:1], odd[:-1] + even[1:], odd[-1:], zero], axis=0)
            sooner = jnp.concatenate([zero, even[:1], odd[:-1] + even[1:], odd[-1:]], axis=0)
            fine.append([v.reshape(block, cu) for v in (later, own, sooner)])
        for c in range(3):
            top, low = fine[0][c], fine[1][c]
            _, top_after = row_shifts(top)
            low_before, _ = row_shifts(low)
            for b, v in enumerate((low + top_after, top + low, low_before + top)):
                held[3 * b + c, pl.ds(pl.multiple_of(t * block, 16), block), :] = v.astype(BF16)
    acc_ref[...] = jnp.zeros_like(acc_ref)

    @pl.loop(0, 3)
    def _(a):
        total = acc_ref[...]
        for bc in range(9):
            total = total + jnp.dot(
                held[bc, pl.ds(pl.multiple_of((2 - a) * block, 16), frames * block), :],
                w_ref[9 * a + bc],
                preferred_element_type=F32,
            )
        acc_ref[...] = total

    out = acc_ref[...]
    out = out.reshape(frames, outer, rows, ch)
    gf_ref[...] = out[:, 1:-1]
    l_ref[...] = out[:, :2].astype(BF16)
    r_ref[...] = out[:, -2:].astype(BF16)


def run_adj(grads, pre, weight, frames, cols):
    rows = pre.shape[1]
    cu, ch = weight.shape[1:]
    return pl.pallas_call(
        adj_kernel,
        out_shape=[
            jax.ShapeDtypeStruct((frames, cols, rows, ch), F32),
            jax.ShapeDtypeStruct((frames, 2, rows, ch), BF16),
            jax.ShapeDtypeStruct((frames, 2, rows, ch), BF16),
        ],
        in_specs=[VM] * 3,
        out_specs=[VM] * 3,
        scratch_shapes=[
            pltpu.VMEM((9, 6 * (cols + 2) * rows, cu), BF16),
            pltpu.VMEM((frames * (cols + 2) * rows, ch), F32),
        ],
        name="adj",
        compiler_params=GRANT,
    )(pre, weight, grads)


def on_device(latent, frame_order, section_weight, section_gain, up_weight, reward_weight, reward_coef):
    segs = lax.axis_size("segment")
    chips = lax.axis_size("chip")
    tiles = 2 * chips
    seg = lax.axis_index("segment")
    core = lax.axis_index("core")
    tile = 2 * lax.axis_index("chip") + core
    frames, rows, cols, ch = latent.shape
    cu = up_weight.shape[2]
    outs_dev = reward_coef.shape[0]
    last = segs - 1
    halves = segs // frames
    span = 2 * cols * cu
    keep = 2 * rows // halves * 2 * span
    barrier = lax.optimization_barrier
    tile_info = jnp.stack([tile, jnp.full_like(tile, tiles)])
    block = (frames, cols, rows, ch)
    side = (frames, 1, rows, ch)
    side2 = (frames, 2, rows, ch)

    def route(pairs_of_segments, shift):
        return [
            (source * tiles + t, target * tiles + t + shift)
            for source, target in pairs_of_segments
            for t in range(tiles)
            if 0 <= t + shift < tiles
        ]

    def send(value, source, target):
        return lax.ppermute(value, AXES, route([(source, target)], 0))

    def beside(value, shift):
        return lax.ppermute(value, AXES, route([(s, s) for s in range(segs)], shift))

    def hop_route(source, target, shift):
        step = target - source
        pairs = [(s, s + step) for s in range(source % 2, segs, 2) if 0 <= s + step < segs]
        return pairs, shift

    def hop(center, left, right, source, target):
        center, left, right = (
            lax.ppermute(value, AXES, route(*hop_route(source, target, shift)))
            for value, shift in ((center, 0), (right, 1), (left, -1))
        )
        return left, center, right

    def turn_round(pairs_of_segments, shift):
        return [
            (source * tiles + t, target * tiles + (t + shift) % tiles)
            for source, target in pairs_of_segments
            for t in range(tiles)
        ]

    def half_hop(first_three, last_three, source, target):
        to_left, to_right = (-1, 0) if source % 2 == 0 else (0, 1)
        left = lax.ppermute(last_three, AXES, turn_round(*hop_route(source, target, to_right)))
        right = lax.ppermute(first_three, AXES, turn_round(*hop_route(source, target, to_left)))
        return left, right

    def gather_up():
        own = up_weight.shape[1]
        source = jnp.pad(up_weight, ((0, 0), (0, PAD - own), (0, 0)))
        wa = lax.all_to_all(
            jnp.broadcast_to(source[None], (chips, *source.shape)), "chip", 0, 0, tiled=True
        )
        wb = lax.ppermute(wa, "core", [(0, 1), (1, 0)])
        channel = lax.broadcasted_iota(jnp.int32, (ch, tiles * PAD), 0)
        place = lax.broadcasted_iota(jnp.int32, (ch, tiles * PAD), 1)
        other, chip_of, within = place // (chips * PAD), place // PAD % chips, place % PAD
        origin = 2 * chip_of + jnp.where(other == 0, core, 1 - core)
        spread = ((within < own) & (channel == origin * own + within)).astype(BF16)
        return wa, wb, spread, run_order(wa, wb, spread)

    up_shape = (chips, 27, PAD, cu)

    def turn(weight):
        return run_turn(weight[0])

    def start():
        x, left, right = run_first(frame_order, latent.transpose(0, 2, 1, 3))
        return beside(right, 1), x, beside(left, -1)

    weight_fwd = section_weight[0].reshape(27 * ch, ch)
    gathered = lax.cond(
        seg == last,
        gather_up,
        lambda: unwritten(up_shape, up_shape, (ch, tiles * PAD), (27, cu, ch)),
    )
    turned = lax.cond(seg > 1, lambda: turn(section_weight), lambda: unwritten((27 * ch, ch))[0])
    state = lax.cond(seg == 0, start, lambda: unwritten(side, block, side))
    gathered, turned, state = barrier((gathered, turned, state))

    three = (frames, 3, rows, ch)
    taken = [state]
    for k in range(last):
        wide = k == last - 1
        made_shapes = (block, side2, side2) if wide else (three, three)

        def go(state=state, k=k, wide=wide, made_shapes=made_shapes):
            form = "odd" if k % 2 else "even"
            made = lax.cond(
                seg == k,
                lambda: tuple(
                    run_fwd(form, [m[1] for m in made_shapes], tile_info, state, section_gain, weight_fwd)
                ),
                lambda: unwritten(*made_shapes),
            )
            return hop(*made, k, k + 1) if wide else half_hop(*made, k, k + 1)

        given = (side2, block, side2) if wide else (three, three)
        state = lax.cond(
            (seg == k) | (seg == k + 1), go, lambda given=given: unwritten(*given)
        )
        taken.append(state)
        if k == 1:
            late, state = barrier((section_weight, state))
            turned_late = lax.cond(
                seg <= 1, lambda late=late: turn(late), lambda: unwritten((27 * ch, ch))[0]
            )
            turned_late, state = barrier((turned_late, state))
            taken[-1] = state

    chunk = (rows, span)

    def upsampled():
        (deep,) = run_fwd("wide", [cols + 2], tile_info, state, section_gain, weight_fwd)
        return tuple(run_up(deep, *gathered[:3]))

    pre, *feats = lax.cond(
        seg == last,
        upsampled,
        lambda: (
            unwritten((segs, *chunk), dtype=F32)[0],
            *unwritten(*([chunk] * last)),
            jnp.zeros(chunk, BF16),
        ),
    )
    mine = functools.reduce(jnp.add, [send(feats[k], last, k) for k in range(last)], feats[last])
    coef = jnp.pad(reward_coef, (0, GROUP - outs_dev))[None]
    mine, coef = barrier((mine, coef))
    everyone = lax.cond(
        seg >= 0,
        lambda: lax.all_to_all(
            jnp.broadcast_to(mine[None], (tiles, *chunk)), TILE, 0, 0, tiled=True
        ),
        lambda: unwritten((tiles, *chunk))[0],
    )
    half = (seg % halves).reshape(1)
    partial, table = run_logit(half, everyone.reshape(tiles * rows, span), reward_weight.T, keep)
    group = [(s, s // halves * halves + (s + 1) % halves) for s in range(segs)]
    other = lax.ppermute(partial, "segment", group)
    shares = run_back(partial, other, coef, table)
    shares = lax.cond(
        seg >= 0,
        lambda: lax.all_to_all(shares.reshape(tiles, *chunk), TILE, 0, 0, tiled=True),
        lambda: unwritten((tiles, *chunk))[0],
    )
    share = run_sum(shares)
    grads = lax.cond(
        seg >= 0,
        lambda: lax.all_to_all(
            jnp.broadcast_to(share[None], (segs, *chunk)), "segment", 0, 0, tiled=True
        ),
        lambda: unwritten((segs, *chunk))[0],
    )

    results = {}
    for k in range(last, 0, -1):

        def go_back(state=state, k=k):
            def live():
                if k == last:
                    deep, lp, rp = run_adj(grads, pre, gathered[3], frames, cols)
                    from_r, from_l = beside(lp, -1), beside(rp, 1)
                    gs = (deep, lp, rp, from_l, from_r)
                    made = run_bwd(
                        "first", (cols, 1, 1), tile_info, taken[k][1:2], gs, section_gain, turned
                    )
                else:
                    form = "odd" if k % 2 else "even"
                    weight = turned if k > 1 else turned_late
                    made = run_bwd(form, (3, 3), tile_info, taken[k], state, section_gain, weight)
                return (*made[1:], made[0])

            shapes = (block, side, side) if k == last else (three, three)
            *made, result = lax.cond(
                seg == k,
                live,
                lambda: (*unwritten(*shapes), *unwritten(block, dtype=F32)),
            )
            passed = hop(*made, k, k - 1) if k == last else half_hop(*made, k, k - 1)
            return passed, result

        given = (side, block, side) if k == last else (three, three)
        state, results[k] = lax.cond(
            (seg == k) | (seg == k - 1),
            go_back,
            lambda given=given: (unwritten(*given), unwritten(block, dtype=F32)[0]),
        )

    def finish(k):
        if k == 0:
            result = run_bwd(
                "even", (), tile_info, taken[0][1:2], state, section_gain, turned_late
            )[0]
        else:
            result = results[k]
            if k != last and k % 2:
                moved = turn_round([(s, s) for s in range(segs)], 1)
                left = lax.ppermute(result[:, cols - 2 :], AXES, moved)
                result = jnp.concatenate([left, result[:, : cols - 2]], axis=1)
        return result.transpose(0, 2, 1, 3)

    return lax.switch(seg, [functools.partial(finish, k) for k in range(segs)])[None]


def solution(mesh):
    shape = mesh.devices.shape
    fine = jax.sharding.Mesh(mesh.devices.reshape(shape[0], shape[1] // 2, 2), AXES)
    in_specs = (
        P(None, None, TILE, None),
        P(),
        P("segment", None, None, None),
        P("segment", None),
        P(None, TILE, None),
        P(None, TILE),
        P(TILE),
    )
    out_specs = P("segment", None, None, TILE, None)
    return jax.shard_map(
        on_device, mesh=fine, in_specs=in_specs, out_specs=out_specs, check_vma=False
    )
```

```python
import functools

import jax
import jax.numpy as jnp
from jax import lax
from jax.experimental import pallas as pl
from jax.experimental.pallas import tpu as pltpu
from jax.sharding import PartitionSpec as P

EPS = 1e-06
F32 = jnp.float32
BF16 = jnp.bfloat16
AXES = ("segment", "chip", "core")
TILE = ("chip", "core")
PAD = 16
VM = pl.BlockSpec(memory_space=pltpu.VMEM)
HB = pl.BlockSpec(memory_space=pl.ANY)
SM = pl.BlockSpec(memory_space=pltpu.SMEM)
GRANT = pltpu.CompilerParams(vmem_limit_bytes=24 * 2**20)


def row_shifts(v):
    count = v.shape[0]
    row = lax.broadcasted_iota(jnp.int32, v.shape, 0) & 7
    before = jnp.where(row == 0, 0.0, pltpu.roll(v, 1, 0))
    after = jnp.where(row == 7, 0.0, pltpu.roll(v, count - 1, 0))
    return before, after


PIECES = 6


def weight_copy(w_hbm, w_buf, sem, piece):
    rows = w_hbm.shape[0] // PIECES
    part = pl.ds(pl.multiple_of(piece * rows, 64), rows)
    return pltpu.make_async_copy(w_hbm.at[part], w_buf.at[part], sem.at[piece])


def start_weights(w_hbm, w_buf, sem, backward):
    per = PIECES // 3
    for step in range(PIECES):
        a = 2 - step // per if backward else step // per
        weight_copy(w_hbm, w_buf, sem, a * per + step % per).start()


def convolve_turned(taps, w_hbm, w_buf, sem, acc_ref):
    count = acc_ref.shape[0]
    block = count // 4
    per = PIECES // 3
    ch = w_hbm.shape[1]
    acc_ref[...] = jnp.zeros_like(acc_ref)

    @pl.loop(0, 3)
    def _(step):
        a = 2 - step
        for part in range(per):
            weight_copy(w_hbm, w_buf, sem, a * per + part).wait()
        total = acc_ref[...]
        for tap in range(9):
            total = total + lax.dot_general(
                taps[pl.ds(pl.multiple_of(step * block, 16), count), tap * ch : (tap + 1) * ch],
                w_buf[pl.ds(pl.multiple_of((9 * a + tap) * ch, 128), ch), :],
                (((1,), (1,)), ((), ())),
                preferred_element_type=F32,
            )
        acc_ref[...] = total


def convolve(taps, w_hbm, w_buf, sem, acc_ref, backward):
    count = acc_ref.shape[0]
    block = count // 4
    per = PIECES // 3
    rows = w_hbm.shape[0] // PIECES
    acc_ref[...] = jnp.zeros_like(acc_ref)

    @pl.loop(0, 3)
    def _(step):
        a = 2 - step if backward else step
        for part in range(per):
            piece = a * per + part
            weight_copy(w_hbm, w_buf, sem, piece).wait()
            acc_ref[...] += jnp.dot(
                taps[pl.ds(pl.multiple_of(step * block, 16), count), part * rows : (part + 1) * rows],
                w_buf[pl.ds(pl.multiple_of(piece * rows, 64), rows), :],
                preferred_element_type=F32,
            )


def column_block(pieces, t):
    parts = [piece[t] for piece in pieces]
    return parts[0] if len(parts) == 1 else jnp.concatenate(parts, axis=0)


def write_block(out, refs, t):
    cols = out.shape[0]
    if len(refs) == 2:
        refs[0][t] = out[:3]
        refs[1][t] = out[cols - 3 :]
    else:
        edge = refs[1].shape[1]
        refs[0][t] = out
        refs[1][t] = out[:edge]
        refs[2][t] = out[cols - edge :]


def edge_scales(form, tile_ref, dtype):
    one, none = jnp.ones((), dtype), jnp.zeros((), dtype)
    low = jnp.where(tile_ref[0] == 0, none, one) if form == "even" else one
    high = jnp.where(tile_ref[0] == tile_ref[1] - 1, none, one)
    return low, high


def put_taps(taps, t_at, v, b, columns, ch, cut, backward):
    rows = 8
    block = columns * rows
    for c in range(3):
        start = (2 - c if backward else c) * rows
        piece = v[start : start + block]
        if cut is not None and c != 1:
            bad = (2 if start == 0 else 1) * rows
            piece = jnp.concatenate([piece[:bad], piece[bad : bad + rows] * cut, piece[bad + rows :]], axis=0)
        at = (3 * b + c) * ch
        taps[pl.ds(pl.multiple_of(t_at * block, 16), block), at : at + ch] = piece.astype(BF16)


def fwd_kernel(form, count, *refs):
    tile_ref, *pieces = refs[: count + 1]
    gain_ref, w_hbm = refs[count + 1 : count + 3]
    *outs, taps, w_buf, acc, sem = refs[count + 3 :]
    start_weights(w_hbm, w_buf, sem, False)
    frames, _, rows, ch = pieces[0].shape
    outer = sum(piece.shape[1] for piece in pieces)
    inner = outer - 2
    block = inner * rows
    gain = gain_ref[...].astype(F32)
    low, high = edge_scales(form, tile_ref, F32)
    taps[0 : 2 * block, :] = jnp.zeros((2 * block, 9 * ch), BF16)
    @pl.loop(0, frames)
    def _(t):
        x = column_block(pieces, t).astype(F32)
        if form == "even":
            x = jnp.concatenate([x[:1] * low, x[1:-1], x[-1:] * high], axis=0)
        x = x.reshape(outer * rows, ch)
        inv = lax.rsqrt(jnp.mean(x * x, axis=-1, keepdims=True) + EPS)
        act = jax.nn.silu(x * inv * gain)
        before, after = row_shifts(act)
        for b, v in enumerate((before, act, after)):
            put_taps(taps, 2 + t, v, b, inner, ch, high if form == "odd" else None, False)
    convolve(taps, w_hbm, w_buf, sem, acc, False)
    @pl.loop(0, frames)
    def _(t):
        x = column_block(pieces, t)[1:-1].astype(F32)
        out = x + acc[pl.ds(pl.multiple_of(t * block, 8), block)].reshape(inner, rows, ch)
        if form == "wide":
            tile = tile_ref[0]
            col = lax.broadcasted_iota(jnp.int32, out.shape, 0)
            first = jnp.where(tile == 0, 1, 0)
            stop = jnp.where(tile == tile_ref[1] - 1, inner - 1, inner)
            outs[0][t] = jnp.where((col >= first) & (col < stop), out, 0.0).astype(BF16)
        else:
            write_block(out.astype(BF16), outs, t)


def run_fwd(form, out_cols, tile_info, pieces, gain, weight):
    frames, _, rows, ch = pieces[0].shape
    inner = sum(piece.shape[1] for piece in pieces) - 2
    return pl.pallas_call(
        functools.partial(fwd_kernel, form, len(pieces)),
        out_shape=[jax.ShapeDtypeStruct((frames, n, rows, ch), BF16) for n in out_cols],
        in_specs=[SM] + [VM] * (len(pieces) + 1) + [HB],
        out_specs=[VM] * len(out_cols),
        scratch_shapes=[
            pltpu.VMEM((6 * inner * rows, 9 * ch), BF16),
            pltpu.VMEM(weight.shape, BF16),
            pltpu.VMEM((frames * inner * rows, ch), F32),
            pltpu.SemaphoreType.DMA((PIECES,)),
        ],
        name=f"fwd_{form}",
        compiler_params=GRANT,
    )(tile_info, *pieces, gain, weight)


def bwd_kernel(form, n_x, n_g, *refs):
    tile_ref, *refs = refs
    xs, gs, (gain_ref, w_hbm, *rest) = refs[:n_x], refs[n_x : n_x + n_g], refs[n_x + n_g :]
    gf_ref, *outs, taps, w_buf, fac_ref, acc, sem = rest
    start_weights(w_hbm, w_buf, sem, True)
    frames, cols, rows, ch = gf_ref.shape
    block = cols * rows
    outer = cols + 2
    gain = gain_ref[...].astype(F32)
    low, high = edge_scales("odd" if form == "odd" else "even", tile_ref, F32)
    taps[4 * block : 6 * block, :] = jnp.zeros((2 * block, 9 * ch), BF16)

    def gradient(t):
        if form == "first":
            gc, lp, rp, from_l, from_r = gs
            mid = gc[t].astype(F32)
            left = from_l[t, :1].astype(F32) + lp[t, :1].astype(F32)
            right = from_r[t, 1:].astype(F32) + rp[t, 1:].astype(F32)
            return jnp.concatenate(
                [
                    left,
                    mid[:1] + from_l[t, 1:].astype(F32),
                    mid[1:-1],
                    mid[-1:] + from_r[t, :1].astype(F32),
                    right,
                ],
                axis=0,
            )
        return column_block(gs, t).astype(F32)

    def inputs(t):
        x = column_block(xs, t)
        return (x if n_x == 1 else x[1:-1]).astype(F32).reshape(block, ch)

    @pl.loop(0, frames)
    def _(t):
        g = gradient(t)
        if form != "odd":
            g = jnp.concatenate([g[:1] * low, g[1:-1], g[-1:] * high], axis=0)
        g = g.reshape(outer * rows, ch)
        before, after = row_shifts(g)
        for b, v in enumerate((after, g, before)):
            put_taps(taps, t, v, b, cols, ch, high if form == "odd" else None, True)
    for t in range(frames):
        x = inputs(t)
        inv = lax.rsqrt(jnp.mean(x * x, axis=-1, keepdims=True) + EPS)
        u = x * inv * gain
        sig = jax.nn.sigmoid(u)
        fac_ref[t] = sig * (1.0 + u * (1.0 - sig)) * gain * inv
    if form == "first":
        convolve_turned(taps, w_hbm, w_buf, sem, acc)
    else:
        convolve(taps, w_hbm, w_buf, sem, acc, True)
    for t in range(frames):
        x = inputs(t)
        inv2 = 1.0 / (jnp.mean(x * x, axis=-1, keepdims=True) + EPS)
        y = acc[t * block : (t + 1) * block] * fac_ref[t]
        dx = y - x * (inv2 * jnp.mean(y * x, axis=-1, keepdims=True))
        out = gradient(t)[1:-1] + dx.reshape(cols, rows, ch)
        gf_ref[t] = out
        if outs:
            write_block(out.astype(BF16), outs, t)


def run_bwd(form, out_cols, tile_info, xs, gs, gain, weight_back):
    frames, _, rows, ch = xs[0].shape
    cols = xs[0].shape[1] if len(xs) == 1 else sum(x.shape[1] for x in xs) - 2
    outs = [jax.ShapeDtypeStruct((frames, cols, rows, ch), F32)]
    outs += [jax.ShapeDtypeStruct((frames, n, rows, ch), BF16) for n in out_cols]
    return pl.pallas_call(
        functools.partial(bwd_kernel, form, len(xs), len(gs)),
        out_shape=outs,
        in_specs=[SM] + [VM] * (len(xs) + len(gs) + 1) + [HB],
        out_specs=[VM] * len(outs),
        scratch_shapes=[
            pltpu.VMEM((6 * cols * rows, 9 * ch), BF16),
            pltpu.VMEM(weight_back.shape, BF16),
            pltpu.VMEM((frames, cols * rows, ch), F32),
            pltpu.VMEM((frames * cols * rows, ch), F32),
            pltpu.SemaphoreType.DMA((PIECES,)),
        ],
        name=f"bwd_{form}",
        compiler_params=GRANT,
    )(tile_info, *xs, *gs, gain, weight_back)


def first_kernel(order_ref, latent_ref, x_ref, l_ref, r_ref):
    for t in range(x_ref.shape[0]):
        x = latent_ref[order_ref[t]]
        x_ref[t] = x
        l_ref[t] = x[:1]
        r_ref[t] = x[x.shape[0] - 1 :]


def run_first(order, latent):
    frames, cols, rows, ch = latent.shape
    return pl.pallas_call(
        first_kernel,
        out_shape=[jax.ShapeDtypeStruct((frames, n, rows, ch), BF16) for n in (cols, 1, 1)],
        in_specs=[SM, VM],
        out_specs=[VM] * 3,
        name="first",
        compiler_params=GRANT,
    )(order, latent)


def unwritten(*shapes, dtype=BF16):
    return tuple(
        pl.pallas_call(
            lambda out_ref: None,
            out_shape=jax.ShapeDtypeStruct(shape, dtype),
            out_specs=HB,
            name="unwritten",
        )()
        for shape in shapes
    )


def up_kernel(x_ref, wa_ref, wb_ref, spread_ref, *rest):
    pre_ref, *feat_refs, held, cells, phases, feats = rest
    frames, outer, rows, ch = x_ref.shape
    cols = outer - 2
    cu = wa_ref.shape[3]
    half = wa_ref.shape[0] * wa_ref.shape[2]
    block = outer * rows
    held[0 : 2 * block, :] = jnp.zeros((2 * block, 2 * half), BF16)
    for t in range(frames):
        held[(2 + t) * block : (3 + t) * block, :] = jnp.dot(
            x_ref[t].reshape(block, ch), spread_ref[...], preferred_element_type=F32
        ).astype(BF16)

    @pl.loop(0, 3)
    def _(three):
        for within in range(3):
            tap = 3 * three + within
            total = jnp.zeros((frames * block, cu), F32)
            for a in range(3):
                for part, w_ref in enumerate((wa_ref, wb_ref)):
                    total = total + jnp.dot(
                        held[a * block : (a + frames) * block, part * half : (part + 1) * half],
                        w_ref[:, 9 * a + tap].reshape(half, cu),
                        preferred_element_type=F32,
                    )
            cells[tap] = total

    shape = (frames, outer, rows, cu)
    by_phase = [[], []]
    for c in range(3):
        before, _ = row_shifts(cells[c])
        _, after = row_shifts(cells[6 + c])
        middle = cells[3 + c]
        by_phase[0].append((before + middle + cells[6 + c]).reshape(shape))
        by_phase[1].append((cells[c] + middle + after).reshape(shape))
    for p in range(2):
        left, mid, right = by_phase[p]
        phases[p, 0] = left[:, 0:cols] + mid[:, 1 : cols + 1] + right[:, 1 : cols + 1]
        phases[p, 1] = left[:, 1 : cols + 1] + mid[:, 1 : cols + 1] + right[:, 2 : cols + 2]

    @pl.loop(0, frames)
    def _(t):
        for w in range(cols):
            pair = [jnp.concatenate([phases[p, 0, t, w], phases[p, 1, t, w]], axis=1) for p in range(2)]
            lanes = slice(w * 2 * cu, (w + 1) * 2 * cu)
            for h in range(2):
                mine = slice(h * rows // 2, (h + 1) * rows // 2)
                piece = jnp.concatenate([pair[0][mine], pair[1][mine]], axis=0)
                pre_ref[2 * t + h, :, lanes] = piece
                feats[2 * t + h, :, lanes] = jax.nn.silu(piece).astype(BF16)

    for i, feat_ref in enumerate(feat_refs):
        feat_ref[...] = feats[i]


def run_up(x, wa, wb, spread):
    frames, outer, rows, ch = x.shape
    chunk = (rows, 2 * (outer - 2) * wa.shape[3])
    return pl.pallas_call(
        up_kernel,
        out_shape=[
            jax.ShapeDtypeStruct((2 * frames, *chunk), F32),
            *(jax.ShapeDtypeStruct(chunk, BF16) for _ in range(2 * frames)),
        ],
        in_specs=[VM] * 4,
        out_specs=[VM] * (1 + 2 * frames),
        scratch_shapes=[
            pltpu.VMEM((6 * outer * rows, spread.shape[1]), BF16),
            pltpu.VMEM((9, frames * outer * rows, wa.shape[3]), F32),
            pltpu.VMEM((2, 2, frames, outer - 2, rows, wa.shape[3]), F32),
            pltpu.VMEM((2 * frames, *chunk), BF16),
        ],
        name="up",
        compiler_params=GRANT,
    )(x, wa, wb, spread)


def exact_dot(value, ones, dims):
    total = None
    for _ in range(3):
        piece = value.astype(BF16)
        value = value - piece.astype(F32)
        part = lax.dot_general(piece, ones, dims, preferred_element_type=F32)
        total = part if total is None else total + part
    return total


GROUP = 48


def group_masks(rows, groups):
    row = lax.broadcasted_iota(jnp.int32, (rows, groups * GROUP), 0)
    lane = lax.broadcasted_iota(jnp.int32, (rows, groups * GROUP), 1)
    wanted = (row % 8) * 2 + (row // 8) % 2
    return lane // GROUP == wanted


def fold_matrix(groups):
    lane = lax.broadcasted_iota(jnp.int32, (groups * GROUP, GROUP), 0)
    column = lax.broadcasted_iota(jnp.int32, (groups * GROUP, GROUP), 1)
    return (lane % GROUP == column).astype(F32).astype(BF16)


def logit_kernel(half_ref, z_ref, w_hbm, out_ref, table, w_buf, sem):
    outs, keep = w_buf.shape
    span = z_ref.shape[1]
    groups = keep // span
    copy = pltpu.make_async_copy(
        w_hbm.at[:, pl.ds(pl.multiple_of(half_ref[0] * keep, 128), keep)], w_buf, sem
    )
    copy.start()
    mask = group_masks(z_ref.shape[0], groups)
    fold = fold_matrix(groups)
    copy.wait()

    @pl.loop(0, groups)
    def _(group):
        r, e = group // 2, group % 2
        true_row = 2 * (r % 4) + r // 4
        start = pl.multiple_of((2 * true_row + e) * span, 128)
        table[pl.ds(pl.multiple_of(group * GROUP, 16), GROUP), :] = jnp.concatenate(
            [w_buf[:, pl.ds(start, span)], jnp.zeros((GROUP - outs, span), BF16)], axis=0
        )

    pairs = lax.dot_general(
        z_ref[...], table[...], (((1,), (1,)), ((), ())), preferred_element_type=F32
    )
    pairs = jnp.where(mask, pairs, 0.0)
    patches = z_ref.shape[0] // groups
    summed = jnp.sum(pairs.reshape(patches, groups, groups * GROUP), axis=1)
    out_ref[...] = exact_dot(summed, fold, (((1,), (0,)), ((), ())))


def run_logit(half, z, weight, keep):
    outs = weight.shape[0]
    span = z.shape[1]
    groups = keep // span
    return pl.pallas_call(
        logit_kernel,
        out_shape=[
            jax.ShapeDtypeStruct((z.shape[0] // groups, GROUP), F32),
            jax.ShapeDtypeStruct((groups * GROUP, span), BF16),
        ],
        in_specs=[SM, VM, pl.BlockSpec(memory_space=pltpu.HBM)],
        out_specs=[VM, VM],
        scratch_shapes=[pltpu.VMEM((outs, keep), BF16), pltpu.SemaphoreType.DMA],
        name="logit",
        compiler_params=GRANT,
    )(half, z, weight)


def back_kernel(mine_ref, other_ref, coef_ref, table_ref, out_ref, wide_ref):
    groups = table_ref.shape[0] // GROUP
    patches = mine_ref.shape[0]
    squashed = jnp.tanh(mine_ref[...] + other_ref[...])
    grad = (coef_ref[...] * (1.0 - squashed * squashed)).astype(BF16)
    wide = lax.dot_general(
        grad, fold_matrix(groups), (((1,), (1,)), ((), ())), preferred_element_type=F32
    )
    wide = jnp.broadcast_to(wide[:, None, :], (patches, groups, groups * GROUP))
    wide = wide.reshape(patches * groups, groups * GROUP)
    wide_ref[...] = jnp.where(group_masks(patches * groups, groups), wide, 0.0).astype(BF16)

    @pl.loop(0, out_ref.shape[1] // 512)
    def _(i):
        lanes = pl.ds(pl.multiple_of(i * 512, 128), 512)
        out_ref[:, lanes] = jnp.dot(
            wide_ref[...], table_ref[:, lanes], preferred_element_type=F32
        ).astype(BF16)


def run_back(mine, other, coef, table):
    rows = mine.shape[0] * table.shape[0] // GROUP
    return pl.pallas_call(
        back_kernel,
        out_shape=jax.ShapeDtypeStruct((rows, table.shape[1]), BF16),
        in_specs=[VM] * 4,
        out_specs=VM,
        scratch_shapes=[pltpu.VMEM((rows, table.shape[0]), BF16)],
        name="back",
        compiler_params=GRANT,
    )(mine, other, coef, table)


def sum_kernel(in_ref, out_ref):
    total = in_ref[0].astype(F32)
    for i in range(1, in_ref.shape[0]):
        total = total + in_ref[i].astype(F32)
    out_ref[...] = total.astype(BF16)


def run_sum(values):
    return pl.pallas_call(
        sum_kernel,
        out_shape=jax.ShapeDtypeStruct(values.shape[1:], BF16),
        in_specs=[VM],
        out_specs=VM,
        name="sum",
        compiler_params=GRANT,
    )(values)


def order_kernel(wa_ref, wb_ref, spread_ref, out_ref):
    half = wa_ref.shape[0] * wa_ref.shape[2]
    cu = wa_ref.shape[3]

    @pl.loop(0, wa_ref.shape[1] // 3)
    def _(three):
        for within in range(3):
            tap = 3 * three + within
            total = None
            for part, w_ref in enumerate((wa_ref, wb_ref)):
                turned = lax.dot_general(
                    w_ref[:, tap].reshape(half, cu),
                    spread_ref[:, part * half : (part + 1) * half],
                    (((0,), (1,)), ((), ())),
                    preferred_element_type=F32,
                )
                total = turned if total is None else total + turned
            out_ref[tap] = total.astype(BF16)


def run_order(wa, wb, spread):
    return pl.pallas_call(
        order_kernel,
        out_shape=jax.ShapeDtypeStruct((wa.shape[1], wa.shape[3], spread.shape[0]), BF16),
        in_specs=[VM] * 3,
        out_specs=VM,
        name="order",
        compiler_params=GRANT,
    )(wa, wb, spread)


def adj_kernel(pre_ref, w_ref, *rest):
    grads, gf_ref, l_ref, r_ref, held, acc_ref = rest
    frames, cols, rows, ch = gf_ref.shape
    outer = cols + 2
    cu = w_ref.shape[1]
    block = outer * rows
    held[:, frames * block :, :] = jnp.zeros((9, 2 * block, cu), BF16)
    zero = jnp.zeros((1, rows, cu), F32)

    @pl.loop(0, frames)
    def _(t):
        chunks = []
        for h in range(2):
            pre = pre_ref[2 * t + h]
            sig = jax.nn.sigmoid(pre)
            grad = grads[2 * t + h].astype(F32) * sig * (1.0 + pre * (1.0 - sig))
            chunks.append(grad.astype(BF16).astype(F32))
        fine = []
        for p in range(2):
            low = slice(p * rows // 2, (p + 1) * rows // 2)
            whole = jnp.concatenate([chunks[0][low], chunks[1][low]], axis=0)
            even, odd = (
                jnp.concatenate(
                    [whole[:, (2 * w + q) * cu : (2 * w + q + 1) * cu][None] for w in range(cols)], axis=0
                )
                for q in range(2)
            )
            own = jnp.concatenate([zero, even + odd, zero], axis=0)
            later = jnp.concatenate([even[:1], odd[:-1] + even[1:], odd[-1:], zero], axis=0)
            sooner = jnp.concatenate([zero, even[:1], odd[:-1] + even[1:], odd[-1:]], axis=0)
            fine.append([v.reshape(block, cu) for v in (later, own, sooner)])
        for c in range(3):
            top, low = fine[0][c], fine[1][c]
            _, top_after = row_shifts(top)
            low_before, _ = row_shifts(low)
            for b, v in enumerate((low + top_after, top + low, low_before + top)):
                held[3 * b + c, pl.ds(pl.multiple_of(t * block, 16), block), :] = v.astype(BF16)
    acc_ref[...] = jnp.zeros_like(acc_ref)

    @pl.loop(0, 3)
    def _(a):
        total = acc_ref[...]
        for bc in range(9):
            total = total + jnp.dot(
                held[bc, pl.ds(pl.multiple_of((2 - a) * block, 16), frames * block), :],
                w_ref[9 * a + bc],
                preferred_element_type=F32,
            )
        acc_ref[...] = total

    out = acc_ref[...]
    out = out.reshape(frames, outer, rows, ch)
    gf_ref[...] = out[:, 1:-1]
    l_ref[...] = out[:, :2].astype(BF16)
    r_ref[...] = out[:, -2:].astype(BF16)


def run_adj(grads, pre, weight, frames, cols):
    rows = pre.shape[1]
    cu, ch = weight.shape[1:]
    return pl.pallas_call(
        adj_kernel,
        out_shape=[
            jax.ShapeDtypeStruct((frames, cols, rows, ch), F32),
            jax.ShapeDtypeStruct((frames, 2, rows, ch), BF16),
            jax.ShapeDtypeStruct((frames, 2, rows, ch), BF16),
        ],
        in_specs=[VM] * 3,
        out_specs=[VM] * 3,
        scratch_shapes=[
            pltpu.VMEM((9, 6 * (cols + 2) * rows, cu), BF16),
            pltpu.VMEM((frames * (cols + 2) * rows, ch), F32),
        ],
        name="adj",
        compiler_params=GRANT,
    )(pre, weight, grads)


def on_device(latent, frame_order, section_weight, section_gain, up_weight, reward_weight, reward_coef):
    segs = lax.axis_size("segment")
    chips = lax.axis_size("chip")
    tiles = 2 * chips
    seg = lax.axis_index("segment")
    core = lax.axis_index("core")
    tile = 2 * lax.axis_index("chip") + core
    frames, rows, cols, ch = latent.shape
    cu = up_weight.shape[2]
    outs_dev = reward_coef.shape[0]
    last = segs - 1
    halves = segs // frames
    span = 2 * cols * cu
    keep = 2 * rows // halves * 2 * span
    barrier = lax.optimization_barrier
    tile_info = jnp.stack([tile, jnp.full_like(tile, tiles)])
    block = (frames, cols, rows, ch)
    side = (frames, 1, rows, ch)
    side2 = (frames, 2, rows, ch)

    def route(pairs_of_segments, shift):
        return [
            (source * tiles + t, target * tiles + t + shift)
            for source, target in pairs_of_segments
            for t in range(tiles)
            if 0 <= t + shift < tiles
        ]

    def send(value, source, target):
        return lax.ppermute(value, AXES, route([(source, target)], 0))

    def beside(value, shift):
        return lax.ppermute(value, AXES, route([(s, s) for s in range(segs)], shift))

    def hop_route(source, target, shift):
        step = target - source
        pairs = [(s, s + step) for s in range(source % 2, segs, 2) if 0 <= s + step < segs]
        return pairs, shift

    def hop(center, left, right, source, target):
        center, left, right = (
            lax.ppermute(value, AXES, route(*hop_route(source, target, shift)))
            for value, shift in ((center, 0), (right, 1), (left, -1))
        )
        return left, center, right

    def turn_round(pairs_of_segments, shift):
        return [
            (source * tiles + t, target * tiles + (t + shift) % tiles)
            for source, target in pairs_of_segments
            for t in range(tiles)
        ]

    def half_hop(first_three, last_three, source, target):
        to_left, to_right = (-1, 0) if source % 2 == 0 else (0, 1)
        left = lax.ppermute(last_three, AXES, turn_round(*hop_route(source, target, to_right)))
        right = lax.ppermute(first_three, AXES, turn_round(*hop_route(source, target, to_left)))
        return left, right

    def gather_up():
        own = up_weight.shape[1]
        source = jnp.pad(up_weight, ((0, 0), (0, PAD - own), (0, 0)))
        wa = lax.all_to_all(
            jnp.broadcast_to(source[None], (chips, *source.shape)), "chip", 0, 0, tiled=True
        )
        wb = lax.ppermute(wa, "core", [(0, 1), (1, 0)])
        channel = lax.broadcasted_iota(jnp.int32, (ch, tiles * PAD), 0)
        place = lax.broadcasted_iota(jnp.int32, (ch, tiles * PAD), 1)
        other, chip_of, within = place // (chips * PAD), place // PAD % chips, place % PAD
        origin = 2 * chip_of + jnp.where(other == 0, core, 1 - core)
        spread = ((within < own) & (channel == origin * own + within)).astype(BF16)
        return wa, wb, spread, run_order(wa, wb, spread)

    up_shape = (chips, 27, PAD, cu)

    def turn(weight):
        return weight[0].transpose(0, 2, 1).reshape(27 * ch, ch)

    def start():
        x, left, right = run_first(frame_order, latent.transpose(0, 2, 1, 3))
        return beside(right, 1), x, beside(left, -1)

    weight_fwd = section_weight[0].reshape(27 * ch, ch)
    gathered = lax.cond(
        seg == last,
        gather_up,
        lambda: unwritten(up_shape, up_shape, (ch, tiles * PAD), (27, cu, ch)),
    )
    turned = lax.cond((seg > 1) & (seg < last), lambda: turn(section_weight), lambda: unwritten((27 * ch, ch))[0])
    state = lax.cond(seg == 0, start, lambda: unwritten(side, block, side))
    gathered, turned, state = barrier((gathered, turned, state))

    three = (frames, 3, rows, ch)
    taken = [state]
    for k in range(last):
        wide = k == last - 1
        made_shapes = (block, side2, side2) if wide else (three, three)

        def go(state=state, k=k, wide=wide, made_shapes=made_shapes):
            form = "odd" if k % 2 else "even"
            made = lax.cond(
                seg == k,
                lambda: tuple(
                    run_fwd(form, [m[1] for m in made_shapes], tile_info, state, section_gain, weight_fwd)
                ),
                lambda: unwritten(*made_shapes),
            )
            return hop(*made, k, k + 1) if wide else half_hop(*made, k, k + 1)

        given = (side2, block, side2) if wide else (three, three)
        state = lax.cond(
            (seg == k) | (seg == k + 1), go, lambda given=given: unwritten(*given)
        )
        taken.append(state)
        if k == 1:
            late, state = barrier((section_weight, state))
            turned_late = lax.cond(
                seg <= 1, lambda late=late: turn(late), lambda: unwritten((27 * ch, ch))[0]
            )
            turned_late, state = barrier((turned_late, state))
            taken[-1] = state

    chunk = (rows, span)

    def upsampled():
        (deep,) = run_fwd("wide", [cols + 2], tile_info, state, section_gain, weight_fwd)
        return tuple(run_up(deep, *gathered[:3]))

    pre, *feats = lax.cond(
        seg == last,
        upsampled,
        lambda: (
            unwritten((segs, *chunk), dtype=F32)[0],
            *unwritten(*([chunk] * last)),
            jnp.zeros(chunk, BF16),
        ),
    )
    mine = functools.reduce(jnp.add, [send(feats[k], last, k) for k in range(last)], feats[last])
    coef = jnp.pad(reward_coef, (0, GROUP - outs_dev))[None]
    mine, coef = barrier((mine, coef))
    everyone = lax.cond(
        seg >= 0,
        lambda: lax.all_to_all(
            jnp.broadcast_to(mine[None], (tiles, *chunk)), TILE, 0, 0, tiled=True
        ),
        lambda: unwritten((tiles, *chunk))[0],
    )
    half = (seg % halves).reshape(1)
    partial, table = run_logit(half, everyone.reshape(tiles * rows, span), reward_weight.T, keep)
    group = [(s, s // halves * halves + (s + 1) % halves) for s in range(segs)]
    other = lax.ppermute(partial, "segment", group)
    shares = run_back(partial, other, coef, table)
    shares = lax.cond(
        seg >= 0,
        lambda: lax.all_to_all(shares.reshape(tiles, *chunk), TILE, 0, 0, tiled=True),
        lambda: unwritten((tiles, *chunk))[0],
    )
    share = run_sum(shares)
    grads = lax.cond(
        seg >= 0,
        lambda: lax.all_to_all(
            jnp.broadcast_to(share[None], (segs, *chunk)), "segment", 0, 0, tiled=True
        ),
        lambda: unwritten((segs, *chunk))[0],
    )

    results = {}
    for k in range(last, 0, -1):

        def go_back(state=state, k=k):
            def live():
                if k == last:
                    deep, lp, rp = run_adj(grads, pre, gathered[3], frames, cols)
                    from_r, from_l = beside(lp, -1), beside(rp, 1)
                    gs = (deep, lp, rp, from_l, from_r)
                    made = run_bwd(
                        "first", (cols, 1, 1), tile_info, taken[k][1:2], gs, section_gain, weight_fwd
                    )
                else:
                    form = "odd" if k % 2 else "even"
                    weight = turned if k > 1 else turned_late
                    made = run_bwd(form, (3, 3), tile_info, taken[k], state, section_gain, weight)
                return (*made[1:], made[0])

            shapes = (block, side, side) if k == last else (three, three)
            *made, result = lax.cond(
                seg == k,
                live,
                lambda: (*unwritten(*shapes), *unwritten(block, dtype=F32)),
            )
            passed = hop(*made, k, k - 1) if k == last else half_hop(*made, k, k - 1)
            return passed, result

        given = (side, block, side) if k == last else (three, three)
        state, results[k] = lax.cond(
            (seg == k) | (seg == k - 1),
            go_back,
            lambda given=given: (unwritten(*given), unwritten(block, dtype=F32)[0]),
        )

    def finish(k):
        if k == 0:
            result = run_bwd(
                "even", (), tile_info, taken[0][1:2], state, section_gain, turned_late
            )[0]
        else:
            result = results[k]
            if k != last and k % 2:
                moved = turn_round([(s, s) for s in range(segs)], 1)
                left = lax.ppermute(result[:, cols - 2 :], AXES, moved)
                result = jnp.concatenate([left, result[:, : cols - 2]], axis=1)
        return result.transpose(0, 2, 1, 3)

    return lax.switch(seg, [functools.partial(finish, k) for k in range(segs)])[None]


def solution(mesh):
    shape = mesh.devices.shape
    fine = jax.sharding.Mesh(mesh.devices.reshape(shape[0], shape[1] // 2, 2), AXES)
    in_specs = (
        P(None, None, TILE, None),
        P(),
        P("segment", None, None, None),
        P("segment", None),
        P(None, TILE, None),
        P(None, TILE),
        P(TILE),
    )
    out_specs = P("segment", None, None, TILE, None)
    return jax.shard_map(
        on_device, mesh=fine, in_specs=in_specs, out_specs=out_specs, check_vma=False
    )
```
